512 devices in a mesh: dp: 64 (over y, x, core), mp: 8 (over z).
Axes of the slice: x: 4, y: 8, z: 8, core: 2. Of those that a mesh axis runs over, the one named last changes fastest.
Arguments:
- tokens: bfloat16 [32768, 2048], P('dp'), may hold values from -6 to 6
- q_weight: bfloat16 [2048, 256], P('dp', 'mp'), may hold values from -0.125 to 0.125
- k_weight: bfloat16 [2048, 256], P('dp', 'mp'), may hold values from -0.125 to 0.125
- v_weight: bfloat16 [2048, 2048], P('dp', 'mp'), may hold values from -0.125 to 0.125
- adapter_down: bfloat16 [2048, 256], P(None, 'mp'), may hold values from -0.125 to 0.125
- adapter_up: bfloat16 [256, 2048], P(None, 'mp'), may hold values from -1.5 to 1.5
- lengths: int32 [4], replicated, may hold values from 1 to 16384, 32768 in all
- adapter_ids: int32 [4], replicated, may hold values from 0 to 15
- head_gain: float32 [2048], P('mp'), may hold values from 0.1 to 1.9
- out_weight: bfloat16 [2048, 2048], P('mp', 'dp'), may hold values from -0.125 to 0.125
Outputs:
- layer_out: bfloat16 [32768, 2048], P('dp', 'mp')
The draws below stay inside these ranges and needn't reach their ends.
Inputs may be any that keep to these rules, and one draw needn't show every extreme that they name: The lengths sum to 32768 and the longest request has exactly 32768 // 2 tokens.
All inputs are finite; a program needn't handle non-finite values.
Results may differ from the reference program's by a relative error of at most 0.022.
Values may be sent and summed in bfloat16 or wider, within the bound.
A program may use at most 128 MiB of HBM per device.

```python
import math
import jax
import jax.numpy as jnp
import numpy as np
from jax import lax

D = 2048
H = 16
F = 16
R = 16
ADAPTERS = 16
REQS = 4
TOK_DEV = 512
DV = 128
FEATS = 273
TOKENS = 32768


def place_ends(drawn, rng, smallest, high):
    shape = drawn.shape
    index_at = [jax.random.randint(jax.random.fold_in(rng, axis), (), 0, shape[axis]) for axis in range(len(shape))]
    drawn = drawn.at[tuple(index_at)].set(smallest)
    longest = shape.index(max(shape))
    index_at[longest] = (index_at[longest] + 1) % shape[longest]
    return drawn.at[tuple(index_at)].set(high)


def levels(key, dims, shards, low, high):
    factor_of, own = 1.0, jax.random.fold_in(key, 6)
    for axis_at, parts in shards:
        steps = jnp.exp(jax.random.uniform(jax.random.fold_in(own, axis_at), (parts,), jnp.float32, low / len(shards), high / len(shards)))
        factor_of = factor_of * jnp.repeat(steps, dims[axis_at] // parts).reshape([-1 if axis == axis_at else 1 for axis in range(len(dims))])
    return factor_of


def split_up(count, total, most, slope):
    loads = [(1 << 20) // math.isqrt(grade ** slope) + 1 for grade in range(2, count + 1)]
    spare, holding = total - most - (count - 1), [1] * (count - 1)
    while spare > 0:
        movable = [i for i in range(count - 1) if holding[i] < most]
        mass, remaining = sum([loads[i] for i in movable]), spare
        for i in movable:
            addition = min(most - holding[i], max(1, remaining * loads[i] // mass), spare)
            holding[i] = holding[i] + addition
            spare = spare - addition
    return np.array([most] + holding)


def ragged(key, number_of, total, reach, skew):
    if number_of == 2:
        one = jax.random.randint(key, (), max(1, total - reach), min(reach, total - 1) + 1)
        return jnp.stack([one, total - one])
    sizes = jnp.asarray(split_up(number_of, total, reach, skew), jnp.int32)
    couples = (number_of - 1) // 2
    giver, receiver = sizes[1:1 + 2 * couples:2], sizes[2:2 + 2 * couples:2]
    margin = jnp.minimum(giver - 1, reach - receiver)
    moved = jax.random.randint(jax.random.fold_in(key, 1), (couples,), 0, 1 << 20) % (margin + 1)
    sizes = sizes.at[1:1 + 2 * couples:2].set(giver - moved).at[2:2 + 2 * couples:2].set(receiver + moved)
    return sizes[jax.random.permutation(jax.random.fold_in(key, 2), number_of)]


def noise(own_key, dims, scale, limit, split=(), held_as=jnp.bfloat16):
    level = levels(own_key, dims, split, -0.22, 0.18) if split else 1.0
    values = jax.random.normal(own_key, dims, jnp.float32) * scale * level
    return jnp.minimum(jnp.maximum(values, -limit), limit).astype(held_as)


def setup_inputs(seed: int = 0) -> dict:
    key_list = jax.random.split(jax.random.key(seed), 11)
    tokens = noise(key_list[0], (TOKENS, D), 1.0, 6.0, ((0, 64),))
    q_weight = noise(key_list[1], (D, H * F), D ** -0.5, 0.125, ((0, 64), (1, 8)))
    k_weight = noise(key_list[2], (D, H * F), D ** -0.5, 0.125, ((0, 64), (1, 8)))
    v_weight = noise(key_list[3], (D, D), D ** -0.5, 0.125, ((0, 64), (1, 8)))
    adapter_down = noise(key_list[4], (D, ADAPTERS * R), D ** -0.5, 0.125, ((1, 8),))
    adapter_up = noise(key_list[5], (ADAPTERS * R, D), R ** -0.5, 1.5, ((1, 8),))
    lengths = ragged(key_list[6], REQS, TOKENS, TOKENS // 2, 2).astype(jnp.int32)
    adapter_ids = place_ends(jax.random.randint(key_list[7], (REQS,), 0, ADAPTERS), jax.random.fold_in(key_list[7], 1), 0, ADAPTERS - 1).astype(jnp.int32)
    head_gain = jnp.clip(1.0 + 0.18 * jax.random.normal(key_list[8], (D,), jnp.float32), 0.1, 1.9)
    out_weight = noise(key_list[9], (D, D), D ** -0.5, 0.125, ((0, 8), (1, 64)))
    return {"tokens": tokens, "q_weight": q_weight, "k_weight": k_weight, "v_weight": v_weight, "adapter_down": adapter_down, "adapter_up": adapter_up, "lengths": lengths, "adapter_ids": adapter_ids, "head_gain": head_gain, "out_weight": out_weight}


EPSILON = 1e-05

def taylor(inputs):
    squares = (inputs[..., :, None] * inputs[..., None, :]).reshape(inputs.shape[:-1] + (inputs.shape[-1] * inputs.shape[-1],))
    constant = jnp.ones(inputs.shape[:-1] + (1,), jnp.float32)
    return jnp.concatenate([constant, 0.5 * inputs, squares * (0.25 / math.sqrt(2.0))], axis=-1)

def token_tables(lengths, adapter_ids, positions):
    bounds = jnp.cumsum(lengths).astype(jnp.int32)
    request = lax.optimization_barrier(jnp.sum((positions[:, None] >= bounds[None, :]).astype(jnp.int32), axis=1)).astype(jnp.int32)
    openings = (bounds - lengths).astype(jnp.int32)
    starts = jnp.any(positions[:, None] == openings[None, :], axis=1)
    picked = request[:, None] == jnp.arange(lengths.shape[0], dtype=jnp.int32)[None, :]
    adapter = lax.optimization_barrier(jnp.sum(jnp.where(picked, adapter_ids[None, :], 0), axis=1)).astype(jnp.int32)
    return (request, starts, adapter)

def block_local(query, key_rows, values, request, starts):
    scores = jnp.einsum('ihd,jhd->hij', query.astype(jnp.float32), key_rows.astype(jnp.float32)) * 0.25
    weights = 1.0 + scores + 0.5 * scores * scores
    indexes = jnp.arange(request.shape[0], dtype=jnp.int32)
    allowed = (indexes[None, :] <= indexes[:, None]) & (request[None, :] == request[:, None])
    weights = jnp.where(allowed[None], weights, 0.0).astype(jnp.bfloat16)
    within = jnp.einsum('hij,jhe->ihe', weights.astype(jnp.float32), values.astype(jnp.float32))
    query_map = taylor(query.astype(jnp.float32)).astype(jnp.bfloat16)
    key_map = taylor(key_rows.astype(jnp.float32)).astype(jnp.bfloat16)
    tail_mask = (request == request[-1]).astype(jnp.bfloat16)
    masked_keys = key_map * tail_mask[:, None, None]
    summary = jnp.einsum('ihf,ihe->hfe', masked_keys.astype(jnp.float32), values.astype(jnp.float32))
    restart = jnp.max(starts.astype(jnp.float32))
    return (within, query_map, summary, restart)

def finish(within, query_map, carried, request, starts, gains):
    follows = ((request == request[0]) & jnp.logical_not(starts[0])).astype(jnp.float32)
    cross = jnp.einsum('ihf,hfe->ihe', query_map.astype(jnp.float32), carried.astype(jnp.bfloat16).astype(jnp.float32))
    combined = within + follows[:, None, None] * cross
    factor = lax.rsqrt(lax.optimization_barrier(jnp.mean(combined * combined, axis=-1, keepdims=True)) + EPSILON)
    return (combined * factor * gains[None]).astype(jnp.bfloat16)

def reference(tokens, q_weight, k_weight, v_weight, adapter_down, adapter_up, lengths, adapter_ids, head_gain, out_weight):
    total_rows = tokens.shape[0]
    positions = jnp.arange(total_rows, dtype=jnp.int32)
    request, starts, adapter = token_tables(lengths, adapter_ids, positions)
    query = jnp.dot(tokens, q_weight, preferred_element_type=jnp.float32).astype(jnp.bfloat16).reshape(total_rows, H, F)
    key_rows = jnp.dot(tokens, k_weight, preferred_element_type=jnp.float32).astype(jnp.bfloat16).reshape(total_rows, H, F)
    low_rank = jnp.dot(tokens, adapter_down, preferred_element_type=jnp.float32)
    owners = jnp.arange(ADAPTERS * R, dtype=jnp.int32) // R
    low_rank = jnp.where(adapter[:, None] == owners[None, :], low_rank, 0.0).astype(jnp.bfloat16)
    values = jnp.dot(tokens, v_weight, preferred_element_type=jnp.float32) + jnp.dot(low_rank, adapter_up, preferred_element_type=jnp.float32)
    values = values.astype(jnp.bfloat16).reshape(total_rows, H, DV)
    gains = head_gain.reshape(H, DV)
    block_count = total_rows // TOK_DEV

    def by_block(array):
        return array.reshape((block_count, TOK_DEV) + array.shape[1:])

    def advance(carried, pieces):
        block_query, block_keys, block_values, block_request, block_starts = pieces
        within, query_map, summary, restart = block_local(block_query, block_keys, block_values, block_request, block_starts)
        normed = finish(within, query_map, carried, block_request, block_starts, gains)
        following = jnp.where(restart > 0, summary, carried + summary)
        return (following, normed)
    initial = jnp.zeros((H, FEATS, DV), jnp.float32)
    _, normed = lax.scan(advance, initial, (by_block(query), by_block(key_rows), by_block(values), by_block(request), by_block(starts)))
    normed = normed.reshape(total_rows, D)
    return jnp.dot(normed, out_weight, preferred_element_type=jnp.float32).astype(jnp.bfloat16)
```

```python
import math

import jax
import jax.numpy as jnp
from jax import lax
from jax.sharding import PartitionSpec as P

F = 16
R = 16


EPSILON = 1e-05


def taylor(inputs):
    squares = (inputs[..., :, None] * inputs[..., None, :]).reshape(
        inputs.shape[:-1] + (inputs.shape[-1] * inputs.shape[-1],)
    )
    constant = jnp.ones(inputs.shape[:-1] + (1,), jnp.float32)
    return jnp.concatenate([constant, 0.5 * inputs, squares * (0.25 / math.sqrt(2.0))], axis=-1)


def request_of(bounds, positions):
    return jnp.sum((positions[:, None] >= bounds[None, :]).astype(jnp.int32), axis=1)


def token_tables(lengths, adapter_ids, positions):
    bounds = jnp.cumsum(lengths)
    request = request_of(bounds, positions)
    openings = bounds - lengths
    starts = jnp.any(positions[:, None] == openings[None, :], axis=1)
    picked = request[:, None] == jnp.arange(lengths.shape[0], dtype=jnp.int32)[None, :]
    adapter = jnp.sum(jnp.where(picked, adapter_ids[None, :], 0), axis=1)
    return (request, starts, adapter)


def block_local(query, key_rows, values, request, starts):
    scores = jnp.einsum("ihd,jhd->hij", query, key_rows, preferred_element_type=jnp.float32) * 0.25
    weights = 1.0 + scores + 0.5 * scores * scores
    indexes = jnp.arange(request.shape[0], dtype=jnp.int32)
    allowed = (indexes[None, :] <= indexes[:, None]) & (request[None, :] == request[:, None])
    weights = jnp.where(allowed[None], weights, 0.0).astype(jnp.bfloat16)
    within = jnp.einsum("hij,jhe->ihe", weights, values, preferred_element_type=jnp.float32)
    query_map = taylor(query.astype(jnp.float32)).astype(jnp.bfloat16)
    key_map = taylor(key_rows.astype(jnp.float32)).astype(jnp.bfloat16)
    tail_mask = (request == request[-1]).astype(jnp.bfloat16)
    masked_keys = key_map * tail_mask[:, None, None]
    summary = jnp.einsum("ihf,ihe->hfe", masked_keys, values, preferred_element_type=jnp.float32)
    return (within, query_map, summary)


def finish(within, query_map, carried, request, starts, gains):
    follows = ((request == request[0]) & jnp.logical_not(starts[0])).astype(jnp.float32)
    cross = jnp.einsum(
        "ihf,hfe->ihe", query_map, carried.astype(jnp.bfloat16), preferred_element_type=jnp.float32
    )
    combined = within + follows[:, None, None] * cross
    factor = lax.rsqrt(jnp.mean(combined * combined, axis=-1, keepdims=True) + EPSILON)
    return (combined * factor * gains[None]).astype(jnp.bfloat16)


def carry_weights(lengths, row_count, place, blocks):
    bounds = jnp.cumsum(lengths)
    firsts = jnp.arange(blocks, dtype=jnp.int32) * row_count
    tails = request_of(bounds, firsts + (row_count - 1))
    head = request_of(bounds, place[None] * row_count)[0]
    chosen = (jnp.arange(blocks, dtype=jnp.int32) < place) & (tails == head)
    return chosen.astype(jnp.bfloat16)


def per_device(
    tokens,
    q_weight,
    k_weight,
    v_weight,
    adapter_down,
    adapter_up,
    lengths,
    adapter_ids,
    head_gain,
    out_weight,
):
    row_count = tokens.shape[0]
    qf = q_weight.shape[1]
    heads_here = qf // F
    vw = v_weight.shape[1]
    value_width = vw // heads_here
    blocks = lax.axis_size("dp")
    place = lax.axis_index("dp")
    positions = place * row_count + jnp.arange(row_count, dtype=jnp.int32)
    request, starts, adapter = token_tables(lengths, adapter_ids, positions)

    local = jnp.concatenate([q_weight, k_weight, v_weight, out_weight.T], axis=1)
    gathered = lax.all_gather(local, "dp", axis=0, tiled=True)
    q_full = gathered[:, :qf]
    k_full = gathered[:, qf : 2 * qf]
    v_full = gathered[:, 2 * qf : 2 * qf + vw]
    out_t = gathered[:, 2 * qf + vw :]

    part_low = jnp.dot(tokens, adapter_down, preferred_element_type=jnp.float32)
    owners = lax.axis_index("mp") * (adapter_down.shape[1] // R) + (
        jnp.arange(adapter_down.shape[1], dtype=jnp.int32) // R
    )
    part_low = jnp.where(adapter[:, None] == owners[None, :], part_low, 0.0).astype(jnp.bfloat16)
    low_rank = lax.all_gather(part_low, "mp", axis=1, tiled=True)

    query_sum = jnp.dot(tokens, q_full, preferred_element_type=jnp.float32)
    key_sum = jnp.dot(tokens, k_full, preferred_element_type=jnp.float32)
    value_sum = jnp.dot(tokens, v_full, preferred_element_type=jnp.float32)
    query = query_sum.astype(jnp.bfloat16).reshape(row_count, heads_here, F)
    key_rows = key_sum.astype(jnp.bfloat16).reshape(row_count, heads_here, F)
    values = value_sum + jnp.dot(low_rank, adapter_up, preferred_element_type=jnp.float32)
    values = values.astype(jnp.bfloat16).reshape(row_count, heads_here, value_width)
    within, query_map, summary = block_local(query, key_rows, values, request, starts)

    every = lax.all_gather(summary.astype(jnp.bfloat16), "dp")
    chosen = carry_weights(lengths, row_count, place, blocks)
    carried = jnp.dot(
        chosen[None, :], every.reshape(blocks, -1), preferred_element_type=jnp.float32
    ).reshape(summary.shape)

    gains = head_gain.reshape(heads_here, value_width)
    normed = finish(within, query_map, carried, request, starts, gains).reshape(
        row_count, heads_here * value_width
    )
    partial_terms = lax.dot_general(
        normed, out_t, (((1,), (1,)), ((), ())), preferred_element_type=jnp.float32
    )
    return lax.psum_scatter(
        partial_terms.astype(jnp.bfloat16), "mp", scatter_dimension=1, tiled=True
    )


def solution(mesh):
    placed = (
        P("dp", None),
        P("dp", "mp"),
        P("dp", "mp"),
        P("dp", "mp"),
        P(None, "mp"),
        P(None, "mp"),
        P(),
        P(),
        P("mp"),
        P("mp", "dp"),
    )
    return jax.shard_map(
        per_device, mesh=mesh, in_specs=placed, out_specs=P("dp", "mp"), check_vma=False
    )
```

```python
import math

import functools

import jax
import jax.numpy as jnp
from jax import lax
from jax.experimental import pallas as pl
from jax.experimental.pallas import tpu as pltpu
from jax.sharding import PartitionSpec as P

MESH = pl.DeviceIdType.MESH

F = 16
R = 16


EPSILON = 1e-05


def taylor(inputs):
    squares = (inputs[..., :, None] * inputs[..., None, :]).reshape(
        inputs.shape[:-1] + (inputs.shape[-1] * inputs.shape[-1],)
    )
    constant = jnp.ones(inputs.shape[:-1] + (1,), jnp.float32)
    return jnp.concatenate([constant, 0.5 * inputs, squares * (0.25 / math.sqrt(2.0))], axis=-1)


def request_of(bounds, positions):
    return jnp.sum((positions[:, None] >= bounds[None, :]).astype(jnp.int32), axis=1)


def token_tables(lengths, adapter_ids, positions):
    bounds = jnp.cumsum(lengths)
    request = request_of(bounds, positions)
    openings = bounds - lengths
    starts = jnp.any(positions[:, None] == openings[None, :], axis=1)
    picked = request[:, None] == jnp.arange(lengths.shape[0], dtype=jnp.int32)[None, :]
    adapter = jnp.sum(jnp.where(picked, adapter_ids[None, :], 0), axis=1)
    return (request, starts, adapter)


def block_local(query, key_rows, values, request, starts):
    scores = jnp.einsum("ihd,jhd->hij", query, key_rows, preferred_element_type=jnp.float32) * 0.25
    weights = 1.0 + scores + 0.5 * scores * scores
    indexes = jnp.arange(request.shape[0], dtype=jnp.int32)
    allowed = (indexes[None, :] <= indexes[:, None]) & (request[None, :] == request[:, None])
    weights = jnp.where(allowed[None], weights, 0.0).astype(jnp.bfloat16)
    within = jnp.einsum("hij,jhe->ihe", weights, values, preferred_element_type=jnp.float32)
    query_map = taylor(query.astype(jnp.float32)).astype(jnp.bfloat16)
    key_map = taylor(key_rows.astype(jnp.float32)).astype(jnp.bfloat16)
    tail_mask = (request == request[-1]).astype(jnp.bfloat16)
    masked_keys = key_map * tail_mask[:, None, None]
    summary = jnp.einsum("ihf,ihe->hfe", masked_keys, values, preferred_element_type=jnp.float32)
    return (within, query_map, summary)


def finish(within, query_map, carried, request, starts, gains):
    follows = ((request == request[0]) & jnp.logical_not(starts[0])).astype(jnp.float32)
    cross = jnp.einsum(
        "ihf,hfe->ihe", query_map, carried.astype(jnp.bfloat16), preferred_element_type=jnp.float32
    )
    combined = within + follows[:, None, None] * cross
    factor = lax.rsqrt(jnp.mean(combined * combined, axis=-1, keepdims=True) + EPSILON)
    return (combined * factor * gains[None]).astype(jnp.bfloat16)


def scan_masks(lengths, row_count, place, blocks, rounds):
    openings = jnp.cumsum(lengths) - lengths
    firsts = jnp.arange(blocks, dtype=jnp.int32) * row_count
    inside = (openings[None, :] >= firsts[:, None]) & (openings[None, :] < firsts[:, None] + row_count)
    restarts = jnp.concatenate(
        [jnp.zeros((1,), jnp.int32), jnp.cumsum(jnp.any(inside, axis=1).astype(jnp.int32))]
    )

    def clean(lo, hi):
        lo = jnp.maximum(lo, 0)
        return (restarts[hi + 1] - restarts[lo] == 0).astype(jnp.float32)

    rows = []
    for k in range(rounds):
        d = 1 << k
        rows.append(clean(place - d + 1, place))
        rows.append(jnp.where(place >= 1, clean(place - d + 1, place - 1), 1.0))
    return jnp.stack(rows)


def scan_kernel(n, rounds, s_ref, m_ref, e_ref, parts, recv, send_sem, recv_sem):
    me = lax.axis_index("dp")
    col = lax.axis_index("mp")
    barrier = pltpu.get_barrier_semaphore()
    for k in range(rounds):
        d = 1 << k

        @pl.when(me + d < n)
        def _():
            pl.semaphore_signal(barrier, 1, device_id=(me + d, col), device_id_type=MESH)

        @pl.when(me >= d)
        def _():
            pl.semaphore_signal(barrier, 1, device_id=(me - d, col), device_id_type=MESH)

    peers = 0
    for k in range(rounds):
        d = 1 << k
        peers = peers + (me // d + n - 1) // n + ((n - 1 - me) // d + n - 1) // n
    pl.semaphore_wait(barrier, peers)

    e_ref[...] = jnp.zeros_like(e_ref)
    copies = []
    for k in range(rounds):
        d = 1 << k
        src = s_ref if k == 0 else parts.at[k - 1]
        copy = pltpu.make_async_remote_copy(
            src_ref=src,
            dst_ref=recv.at[k],
            send_sem=send_sem.at[k],
            recv_sem=recv_sem.at[k],
            device_id=(me + d, col),
            device_id_type=MESH,
        )
        copies.append(copy)

        @pl.when(me + d < n)
        def _():
            copy.start()

        @pl.when(me >= d)
        def _():
            copy.wait_recv()
            got = recv[k]
            if k < rounds - 1:
                parts[k] = src[...] + m_ref[2 * k] * got
            e_ref[...] += m_ref[2 * k + 1] * got

        if k < rounds - 1:

            @pl.when(me < d)
            def _():
                parts[k] = src[...]

    for k in range(rounds):
        d = 1 << k

        @pl.when(me + d < n)
        def _():
            copies[k].wait_send()


def carried_scan(summary, masks, n, rounds):
    shape = summary.shape
    flat = summary.reshape(-1, shape[-1])
    size = flat.shape[0] * flat.shape[1]
    out = pl.pallas_call(
        functools.partial(scan_kernel, n, rounds),
        out_shape=jax.ShapeDtypeStruct(flat.shape, jnp.float32),
        in_specs=[
            pl.BlockSpec(memory_space=pltpu.VMEM),
            pl.BlockSpec(memory_space=pltpu.SMEM),
        ],
        out_specs=pl.BlockSpec(memory_space=pltpu.VMEM),
        scratch_shapes=[
            pltpu.VMEM((max(rounds - 1, 1),) + flat.shape, jnp.float32),
            pltpu.VMEM((rounds,) + flat.shape, jnp.float32),
            pltpu.SemaphoreType.DMA((rounds,)),
            pltpu.SemaphoreType.DMA((rounds,)),
        ],
        compiler_params=pltpu.CompilerParams(collective_id=0, has_side_effects=True),
        cost_estimate=pl.CostEstimate(
            flops=3 * rounds * size, bytes_accessed=8 * rounds * size, transcendentals=0
        ),
    )(flat, masks.reshape(-1))
    return out.reshape(shape)


def per_device(
    tokens,
    q_weight,
    k_weight,
    v_weight,
    adapter_down,
    adapter_up,
    lengths,
    adapter_ids,
    head_gain,
    out_weight,
):
    row_count = tokens.shape[0]
    qf = q_weight.shape[1]
    heads_here = qf // F
    vw = v_weight.shape[1]
    value_width = vw // heads_here
    blocks = lax.axis_size("dp")
    place = lax.axis_index("dp")
    positions = place * row_count + jnp.arange(row_count, dtype=jnp.int32)
    request, starts, adapter = token_tables(lengths, adapter_ids, positions)

    local = jnp.concatenate([q_weight, k_weight, v_weight, out_weight.T], axis=1)
    gathered = lax.all_gather(local, "dp", axis=0, tiled=True)
    q_full = gathered[:, :qf]
    k_full = gathered[:, qf : 2 * qf]
    v_full = gathered[:, 2 * qf : 2 * qf + vw]
    out_t = gathered[:, 2 * qf + vw :]

    part_low = jnp.dot(tokens, adapter_down, preferred_element_type=jnp.float32)
    owners = lax.axis_index("mp") * (adapter_down.shape[1] // R) + (
        jnp.arange(adapter_down.shape[1], dtype=jnp.int32) // R
    )
    part_low = jnp.where(adapter[:, None] == owners[None, :], part_low, 0.0).astype(jnp.bfloat16)
    low_rank = lax.all_gather(part_low, "mp", axis=1, tiled=True)

    query_sum = jnp.dot(tokens, q_full, preferred_element_type=jnp.float32)
    key_sum = jnp.dot(tokens, k_full, preferred_element_type=jnp.float32)
    value_sum = jnp.dot(tokens, v_full, preferred_element_type=jnp.float32)
    query = query_sum.astype(jnp.bfloat16).reshape(row_count, heads_here, F)
    key_rows = key_sum.astype(jnp.bfloat16).reshape(row_count, heads_here, F)
    values = value_sum + jnp.dot(low_rank, adapter_up, preferred_element_type=jnp.float32)
    values = values.astype(jnp.bfloat16).reshape(row_count, heads_here, value_width)
    within, query_map, summary = block_local(query, key_rows, values, request, starts)

    rounds = max(1, (blocks - 1).bit_length())
    masks = scan_masks(lengths, row_count, place, blocks, rounds)
    carried = carried_scan(summary, masks, blocks, rounds)

    gains = head_gain.reshape(heads_here, value_width)
    normed = finish(within, query_map, carried, request, starts, gains).reshape(
        row_count, heads_here * value_width
    )
    partial_terms = lax.dot_general(
        normed, out_t, (((1,), (1,)), ((), ())), preferred_element_type=jnp.float32
    )
    return lax.psum_scatter(
        partial_terms.astype(jnp.bfloat16), "mp", scatter_dimension=1, tiled=True
    )


def solution(mesh):
    placed = (
        P("dp", None),
        P("dp", "mp"),
        P("dp", "mp"),
        P("dp", "mp"),
        P(None, "mp"),
        P(None, "mp"),
        P(),
        P(),
        P("mp"),
        P("mp", "dp"),
    )
    return jax.shard_map(
        per_device, mesh=mesh, in_specs=placed, out_specs=P("dp", "mp"), check_vma=False
    )
```

```python
import math

import functools

import jax
import jax.numpy as jnp
from jax import lax
from jax.experimental import pallas as pl
from jax.experimental.pallas import tpu as pltpu
from jax.sharding import PartitionSpec as P

MESH = pl.DeviceIdType.MESH

F = 16
R = 16


EPSILON = 1e-05


def taylor(inputs):
    squares = (inputs[..., :, None] * inputs[..., None, :]).reshape(
        inputs.shape[:-1] + (inputs.shape[-1] * inputs.shape[-1],)
    )
    constant = jnp.ones(inputs.shape[:-1] + (1,), jnp.float32)
    return jnp.concatenate([constant, 0.5 * inputs, squares * (0.25 / math.sqrt(2.0))], axis=-1)


def request_of(bounds, positions):
    return jnp.sum((positions[:, None] >= bounds[None, :]).astype(jnp.int32), axis=1)


def token_tables(lengths, adapter_ids, positions):
    bounds = jnp.cumsum(lengths)
    request = request_of(bounds, positions)
    openings = bounds - lengths
    starts = jnp.any(positions[:, None] == openings[None, :], axis=1)
    picked = request[:, None] == jnp.arange(lengths.shape[0], dtype=jnp.int32)[None, :]
    adapter = jnp.sum(jnp.where(picked, adapter_ids[None, :], 0), axis=1)
    return (request, starts, adapter)


def block_local(query, key_rows, values, request, starts):
    scores = jnp.einsum("ihd,jhd->hij", query, key_rows, preferred_element_type=jnp.float32) * 0.25
    weights = 1.0 + scores + 0.5 * scores * scores
    indexes = jnp.arange(request.shape[0], dtype=jnp.int32)
    allowed = (indexes[None, :] <= indexes[:, None]) & (request[None, :] == request[:, None])
    weights = jnp.where(allowed[None], weights, 0.0).astype(jnp.bfloat16)
    within = jnp.einsum("hij,jhe->ihe", weights, values, preferred_element_type=jnp.float32)
    query_map = taylor(query.astype(jnp.float32)).astype(jnp.bfloat16)
    key_map = taylor(key_rows.astype(jnp.float32)).astype(jnp.bfloat16)
    tail_mask = (request == request[-1]).astype(jnp.bfloat16)
    masked_keys = key_map * tail_mask[:, None, None]
    summary = jnp.einsum("ihf,ihe->hfe", masked_keys, values, preferred_element_type=jnp.float32)
    return (within, query_map, summary)


def finish(within, query_map, carried, request, starts, gains):
    follows = ((request == request[0]) & jnp.logical_not(starts[0])).astype(jnp.float32)
    cross = jnp.einsum(
        "ihf,hfe->ihe", query_map, carried.astype(jnp.bfloat16), preferred_element_type=jnp.float32
    )
    combined = within + follows[:, None, None] * cross
    factor = lax.rsqrt(jnp.mean(combined * combined, axis=-1, keepdims=True) + EPSILON)
    return (combined * factor * gains[None]).astype(jnp.bfloat16)


def scan_masks(lengths, row_count, place, blocks, rounds):
    openings = jnp.cumsum(lengths) - lengths
    firsts = jnp.arange(blocks, dtype=jnp.int32) * row_count
    inside = (openings[None, :] >= firsts[:, None]) & (openings[None, :] < firsts[:, None] + row_count)
    restarts = jnp.concatenate(
        [jnp.zeros((1,), jnp.int32), jnp.cumsum(jnp.any(inside, axis=1).astype(jnp.int32))]
    )

    def clean(lo, hi):
        lo = jnp.maximum(lo, 0)
        return (restarts[hi + 1] - restarts[lo] == 0).astype(jnp.float32)

    rows = []
    for k in range(rounds):
        d = 1 << k
        rows.append(clean(place - d + 1, place))
        rows.append(jnp.where(place >= 1, clean(place - d + 1, place - 1), 1.0))
    return jnp.stack(rows)


def scan_kernel(n, rounds, s_ref, m_ref, e_ref, parts, recv, send_sem, recv_sem):
    me = lax.axis_index("dp")
    col = lax.axis_index("mp")
    barrier = pltpu.get_barrier_semaphore()
    for k in range(rounds):
        d = 1 << k

        @pl.when(me + d < n)
        def _():
            pl.semaphore_signal(barrier, 1, device_id=(me + d, col), device_id_type=MESH)

        @pl.when(me >= d)
        def _():
            pl.semaphore_signal(barrier, 1, device_id=(me - d, col), device_id_type=MESH)

    peers = 0
    for k in range(rounds):
        d = 1 << k
        peers = peers + (me // d + n - 1) // n + ((n - 1 - me) // d + n - 1) // n
    pl.semaphore_wait(barrier, peers)

    e_ref[...] = jnp.zeros_like(e_ref)
    copies = []
    for k in range(rounds):
        d = 1 << k
        src = s_ref if k == 0 else parts.at[k - 1]
        copy = pltpu.make_async_remote_copy(
            src_ref=src,
            dst_ref=recv.at[k],
            send_sem=send_sem.at[k],
            recv_sem=recv_sem.at[k],
            device_id=(me + d, col),
            device_id_type=MESH,
        )
        copies.append(copy)

        @pl.when(me + d < n)
        def _():
            copy.start()

        @pl.when(me >= d)
        def _():
            copy.wait_recv()
            got = recv[k]
            if k < rounds - 1:
                parts[k] = src[...] + m_ref[2 * k] * got
            e_ref[...] += m_ref[2 * k + 1] * got

        if k < rounds - 1:

            @pl.when(me < d)
            def _():
                parts[k] = src[...]

    for k in range(rounds):
        d = 1 << k

        @pl.when(me + d < n)
        def _():
            copies[k].wait_send()


def carried_scan(summary, masks, n, rounds):
    shape = summary.shape
    flat = summary.reshape(-1, shape[-1])
    size = flat.shape[0] * flat.shape[1]
    out = pl.pallas_call(
        functools.partial(scan_kernel, n, rounds),
        out_shape=jax.ShapeDtypeStruct(flat.shape, jnp.float32),
        in_specs=[
            pl.BlockSpec(memory_space=pltpu.VMEM),
            pl.BlockSpec(memory_space=pltpu.SMEM),
        ],
        out_specs=pl.BlockSpec(memory_space=pltpu.VMEM),
        scratch_shapes=[
            pltpu.VMEM((max(rounds - 1, 1),) + flat.shape, jnp.float32),
            pltpu.VMEM((rounds,) + flat.shape, jnp.float32),
            pltpu.SemaphoreType.DMA((rounds,)),
            pltpu.SemaphoreType.DMA((rounds,)),
        ],
        compiler_params=pltpu.CompilerParams(collective_id=0, has_side_effects=True),
        cost_estimate=pl.CostEstimate(
            flops=3 * rounds * size, bytes_accessed=8 * rounds * size, transcendentals=0
        ),
    )(flat, masks.reshape(-1))
    return out.reshape(shape)


def gather_kernel(n, m, xd_ref, xm_ref, gd_ref, gm_ref, send_d, recv_d, send_m, recv_m):
    me = lax.axis_index("dp")
    col = lax.axis_index("mp")
    barrier = pltpu.get_barrier_semaphore()

    def greet_dp(k, carry):
        pl.semaphore_signal(barrier, 1, device_id=((me + k) % n, col), device_id_type=MESH)
        return carry

    def greet_mp(k, carry):
        pl.semaphore_signal(barrier, 1, device_id=(me, (col + k) % m), device_id_type=MESH)
        return carry

    lax.fori_loop(1, n, greet_dp, 0)
    lax.fori_loop(1, m, greet_mp, 0)
    pl.semaphore_wait(barrier, n + m - 2)

    def to_dp(k):
        return pltpu.make_async_remote_copy(
            src_ref=xd_ref,
            dst_ref=gd_ref.at[me],
            send_sem=send_d.at[k],
            recv_sem=recv_d.at[me],
            device_id=((me + k) % n, col),
            device_id_type=MESH,
        )

    def to_mp(k):
        return pltpu.make_async_remote_copy(
            src_ref=xm_ref,
            dst_ref=gm_ref.at[col],
            send_sem=send_m.at[k],
            recv_sem=recv_m.at[col],
            device_id=(me, (col + k) % m),
            device_id_type=MESH,
        )

    def start_mp(k, carry):
        to_mp(k).start()
        return carry

    def start_dp(k, carry):
        to_dp(k).start()
        return carry

    lax.fori_loop(1, m, start_mp, 0)
    lax.fori_loop(1, n, start_dp, 0)
    gd_ref[me] = xd_ref[...]
    gm_ref[col] = xm_ref[...]

    def land_dp(k, carry):
        pltpu.make_async_remote_copy(
            src_ref=xd_ref,
            dst_ref=gd_ref.at[(me + n - k) % n],
            send_sem=send_d.at[k],
            recv_sem=recv_d.at[(me + n - k) % n],
            device_id=((me + n - k) % n, col),
            device_id_type=MESH,
        ).wait_recv()
        to_dp(k).wait_send()
        return carry

    def land_mp(k, carry):
        pltpu.make_async_remote_copy(
            src_ref=xm_ref,
            dst_ref=gm_ref.at[(col + m - k) % m],
            send_sem=send_m.at[k],
            recv_sem=recv_m.at[(col + m - k) % m],
            device_id=(me, (col + m - k) % m),
            device_id_type=MESH,
        ).wait_recv()
        to_mp(k).wait_send()
        return carry

    lax.fori_loop(1, m, land_mp, 0)
    lax.fori_loop(1, n, land_dp, 0)


def direct_gather(xd, xm, n, m):
    moved = n * xd.size * 2 + m * xm.size * 2
    return pl.pallas_call(
        functools.partial(gather_kernel, n, m),
        out_shape=(
            jax.ShapeDtypeStruct((n,) + xd.shape, xd.dtype),
            jax.ShapeDtypeStruct((m,) + xm.shape, xm.dtype),
        ),
        in_specs=[pl.BlockSpec(memory_space=pltpu.VMEM)] * 2,
        out_specs=(pl.BlockSpec(memory_space=pltpu.VMEM), pl.BlockSpec(memory_space=pltpu.VMEM)),
        scratch_shapes=[
            pltpu.SemaphoreType.DMA((n,)),
            pltpu.SemaphoreType.DMA((n,)),
            pltpu.SemaphoreType.DMA((m,)),
            pltpu.SemaphoreType.DMA((m,)),
        ],
        compiler_params=pltpu.CompilerParams(collective_id=1, has_side_effects=True),
        cost_estimate=pl.CostEstimate(flops=0, bytes_accessed=moved, transcendentals=0),
    )(xd, xm)


def per_device(
    tokens,
    q_weight,
    k_weight,
    v_weight,
    adapter_down,
    adapter_up,
    lengths,
    adapter_ids,
    head_gain,
    out_weight,
):
    row_count = tokens.shape[0]
    qf = q_weight.shape[1]
    heads_here = qf // F
    vw = v_weight.shape[1]
    value_width = vw // heads_here
    blocks = lax.axis_size("dp")
    place = lax.axis_index("dp")
    positions = place * row_count + jnp.arange(row_count, dtype=jnp.int32)
    request, starts, adapter = token_tables(lengths, adapter_ids, positions)

    local = jnp.concatenate([q_weight, k_weight, v_weight, out_weight.T], axis=1)
    part_low = jnp.dot(tokens, adapter_down, preferred_element_type=jnp.float32)
    owners = lax.axis_index("mp") * (adapter_down.shape[1] // R) + (
        jnp.arange(adapter_down.shape[1], dtype=jnp.int32) // R
    )
    part_low = jnp.where(adapter[:, None] == owners[None, :], part_low, 0.0).astype(jnp.bfloat16)
    cols = lax.axis_size("mp")
    gathered, low_parts = direct_gather(local, part_low, blocks, cols)
    gathered = gathered.reshape(blocks * local.shape[0], local.shape[1])
    q_full = gathered[:, :qf]
    k_full = gathered[:, qf : 2 * qf]
    v_full = gathered[:, 2 * qf : 2 * qf + vw]
    out_t = gathered[:, 2 * qf + vw :]
    low_rank = jnp.transpose(low_parts, (1, 0, 2)).reshape(row_count, cols * part_low.shape[1])

    query_sum = jnp.dot(tokens, q_full, preferred_element_type=jnp.float32)
    key_sum = jnp.dot(tokens, k_full, preferred_element_type=jnp.float32)
    value_sum = jnp.dot(tokens, v_full, preferred_element_type=jnp.float32)
    query = query_sum.astype(jnp.bfloat16).reshape(row_count, heads_here, F)
    key_rows = key_sum.astype(jnp.bfloat16).reshape(row_count, heads_here, F)
    values = value_sum + jnp.dot(low_rank, adapter_up, preferred_element_type=jnp.float32)
    values = values.astype(jnp.bfloat16).reshape(row_count, heads_here, value_width)
    within, query_map, summary = block_local(query, key_rows, values, request, starts)

    rounds = max(1, (blocks - 1).bit_length())
    masks = scan_masks(lengths, row_count, place, blocks, rounds)
    carried = carried_scan(summary, masks, blocks, rounds)

    gains = head_gain.reshape(heads_here, value_width)
    normed = finish(within, query_map, carried, request, starts, gains).reshape(
        row_count, heads_here * value_width
    )
    partial_terms = lax.dot_general(
        normed, out_t, (((1,), (1,)), ((), ())), preferred_element_type=jnp.float32
    )
    return lax.psum_scatter(
        partial_terms.astype(jnp.bfloat16), "mp", scatter_dimension=1, tiled=True
    )


def solution(mesh):
    placed = (
        P("dp", None),
        P("dp", "mp"),
        P("dp", "mp"),
        P("dp", "mp"),
        P(None, "mp"),
        P(None, "mp"),
        P(),
        P(),
        P("mp"),
        P("mp", "dp"),
    )
    return jax.shard_map(
        per_device, mesh=mesh, in_specs=placed, out_specs=P("dp", "mp"), check_vma=False
    )
```

```python
import math

import functools

import jax
import jax.numpy as jnp
from jax import lax
from jax.experimental import pallas as pl
from jax.experimental.pallas import tpu as pltpu
from jax.sharding import PartitionSpec as P

MESH = pl.DeviceIdType.MESH

F = 16
R = 16


EPSILON = 1e-05


def taylor(inputs):
    squares = (inputs[..., :, None] * inputs[..., None, :]).reshape(
        inputs.shape[:-1] + (inputs.shape[-1] * inputs.shape[-1],)
    )
    constant = jnp.ones(inputs.shape[:-1] + (1,), jnp.float32)
    return jnp.concatenate([constant, 0.5 * inputs, squares * (0.25 / math.sqrt(2.0))], axis=-1)


def request_of(bounds, positions):
    return jnp.sum((positions[:, None] >= bounds[None, :]).astype(jnp.int32), axis=1)


def token_tables(lengths, adapter_ids, positions):
    bounds = jnp.cumsum(lengths)
    request = request_of(bounds, positions)
    openings = bounds - lengths
    starts = jnp.any(positions[:, None] == openings[None, :], axis=1)
    picked = request[:, None] == jnp.arange(lengths.shape[0], dtype=jnp.int32)[None, :]
    adapter = jnp.sum(jnp.where(picked, adapter_ids[None, :], 0), axis=1)
    return (request, starts, adapter)


def block_local(query, key_rows, values, request, starts):
    scores = jnp.einsum("ihd,jhd->hij", query, key_rows, preferred_element_type=jnp.float32) * 0.25
    weights = 1.0 + scores + 0.5 * scores * scores
    indexes = jnp.arange(request.shape[0], dtype=jnp.int32)
    allowed = (indexes[None, :] <= indexes[:, None]) & (request[None, :] == request[:, None])
    weights = jnp.where(allowed[None], weights, 0.0).astype(jnp.bfloat16)
    within = jnp.einsum("hij,jhe->ihe", weights, values, preferred_element_type=jnp.float32)
    query_map = taylor(query.astype(jnp.float32)).astype(jnp.bfloat16)
    key_map = taylor(key_rows.astype(jnp.float32)).astype(jnp.bfloat16)
    tail_mask = (request == request[-1]).astype(jnp.bfloat16)
    masked_keys = key_map * tail_mask[:, None, None]
    summary = jnp.einsum("ihf,ihe->hfe", masked_keys, values, preferred_element_type=jnp.float32)
    return (within, query_map, summary)


def finish(within, query_map, carried, request, starts, gains):
    follows = ((request == request[0]) & jnp.logical_not(starts[0])).astype(jnp.float32)
    cross = jnp.einsum(
        "ihf,hfe->ihe", query_map, carried.astype(jnp.bfloat16), preferred_element_type=jnp.float32
    )
    combined = within + follows[:, None, None] * cross
    factor = lax.rsqrt(jnp.mean(combined * combined, axis=-1, keepdims=True) + EPSILON)
    return (combined * factor * gains[None]).astype(jnp.bfloat16)


def scan_masks(lengths, row_count, place, blocks, rounds):
    openings = jnp.cumsum(lengths) - lengths
    ids = jnp.arange(blocks, dtype=jnp.int32)
    firsts = ids * row_count
    inside = (openings[None, :] >= firsts[:, None]) & (openings[None, :] < firsts[:, None] + row_count)
    flags = jnp.any(inside, axis=1).astype(jnp.int32)
    spans = jnp.asarray([1 << (k // 2) for k in range(2 * rounds)], jnp.int32)
    tops = place - jnp.asarray([k % 2 for k in range(2 * rounds)], jnp.int32)
    lows = place - spans + 1
    covered = (ids[None, :] >= lows[:, None]) & (ids[None, :] <= tops[:, None])
    hits = jnp.sum(jnp.where(covered, flags[None, :], 0), axis=1)
    return (hits == 0).astype(jnp.float32)


def scan_kernel(n, rounds, s_ref, m_ref, e_ref, parts, recv, send_sem, recv_sem):
    me = lax.axis_index("dp")
    col = lax.axis_index("mp")
    barrier = pltpu.get_barrier_semaphore()
    for k in range(rounds):
        d = 1 << k

        @pl.when(me + d < n)
        def _():
            pl.semaphore_signal(barrier, 1, device_id=(me + d, col), device_id_type=MESH)

        @pl.when(me >= d)
        def _():
            pl.semaphore_signal(barrier, 1, device_id=(me - d, col), device_id_type=MESH)

    peers = 0
    for k in range(rounds):
        d = 1 << k
        peers = peers + (me // d + n - 1) // n + ((n - 1 - me) // d + n - 1) // n
    pl.semaphore_wait(barrier, peers)

    e_ref[...] = jnp.zeros_like(e_ref)
    copies = []
    for k in range(rounds):
        d = 1 << k
        src = s_ref if k == 0 else parts.at[k - 1]
        copy = pltpu.make_async_remote_copy(
            src_ref=src,
            dst_ref=recv.at[k],
            send_sem=send_sem.at[k],
            recv_sem=recv_sem.at[k],
            device_id=(me + d, col),
            device_id_type=MESH,
        )
        copies.append(copy)

        @pl.when(me + d < n)
        def _():
            copy.start()

        @pl.when(me >= d)
        def _():
            copy.wait_recv()
            got = recv[k]
            if k < rounds - 1:
                parts[k] = src[...] + m_ref[2 * k] * got
            e_ref[...] += m_ref[2 * k + 1] * got

        if k < rounds - 1:

            @pl.when(me < d)
            def _():
                parts[k] = src[...]

    for k in range(rounds):
        d = 1 << k

        @pl.when(me + d < n)
        def _():
            copies[k].wait_send()


def carried_scan(summary, masks, n, rounds):
    shape = summary.shape
    flat = summary.reshape(-1, shape[-1])
    size = flat.shape[0] * flat.shape[1]
    out = pl.pallas_call(
        functools.partial(scan_kernel, n, rounds),
        out_shape=jax.ShapeDtypeStruct(flat.shape, jnp.float32),
        in_specs=[
            pl.BlockSpec(memory_space=pltpu.VMEM),
            pl.BlockSpec(memory_space=pltpu.SMEM),
        ],
        out_specs=pl.BlockSpec(memory_space=pltpu.VMEM),
        scratch_shapes=[
            pltpu.VMEM((max(rounds - 1, 1),) + flat.shape, jnp.float32),
            pltpu.VMEM((rounds,) + flat.shape, jnp.float32),
            pltpu.SemaphoreType.DMA((rounds,)),
            pltpu.SemaphoreType.DMA((rounds,)),
        ],
        compiler_params=pltpu.CompilerParams(collective_id=0, has_side_effects=True),
        cost_estimate=pl.CostEstimate(
            flops=3 * rounds * size, bytes_accessed=8 * rounds * size, transcendentals=0
        ),
    )(flat, masks)
    return out.reshape(shape)


def gather_kernel(n, m, xd_ref, xm_ref, gd_ref, gm_ref, send_d, recv_d, send_m, recv_m):
    me = lax.axis_index("dp")
    col = lax.axis_index("mp")
    barrier = pltpu.get_barrier_semaphore()

    def greet_dp(k, carry):
        pl.semaphore_signal(barrier, 1, device_id=((me + k) % n, col), device_id_type=MESH)
        return carry

    def greet_mp(k, carry):
        pl.semaphore_signal(barrier, 1, device_id=(me, (col + k) % m), device_id_type=MESH)
        return carry

    lax.fori_loop(1, n, greet_dp, 0)
    lax.fori_loop(1, m, greet_mp, 0)
    pl.semaphore_wait(barrier, n + m - 2)

    def to_dp(k):
        return pltpu.make_async_remote_copy(
            src_ref=xd_ref,
            dst_ref=gd_ref.at[me],
            send_sem=send_d.at[k],
            recv_sem=recv_d.at[me],
            device_id=((me + k) % n, col),
            device_id_type=MESH,
        )

    def to_mp(k):
        return pltpu.make_async_remote_copy(
            src_ref=xm_ref,
            dst_ref=gm_ref.at[col],
            send_sem=send_m.at[k],
            recv_sem=recv_m.at[col],
            device_id=(me, (col + k) % m),
            device_id_type=MESH,
        )

    def start_mp(k, carry):
        to_mp(k).start()
        return carry

    def start_dp(k, carry):
        to_dp(k).start()
        return carry

    lax.fori_loop(1, m, start_mp, 0)
    lax.fori_loop(1, n, start_dp, 0)
    gd_ref[me] = xd_ref[...]
    gm_ref[col] = xm_ref[...]

    def land_dp(k, carry):
        pltpu.make_async_remote_copy(
            src_ref=xd_ref,
            dst_ref=gd_ref.at[(me + n - k) % n],
            send_sem=send_d.at[k],
            recv_sem=recv_d.at[(me + n - k) % n],
            device_id=((me + n - k) % n, col),
            device_id_type=MESH,
        ).wait_recv()
        to_dp(k).wait_send()
        return carry

    def land_mp(k, carry):
        pltpu.make_async_remote_copy(
            src_ref=xm_ref,
            dst_ref=gm_ref.at[(col + m - k) % m],
            send_sem=send_m.at[k],
            recv_sem=recv_m.at[(col + m - k) % m],
            device_id=(me, (col + m - k) % m),
            device_id_type=MESH,
        ).wait_recv()
        to_mp(k).wait_send()
        return carry

    lax.fori_loop(1, m, land_mp, 0)
    lax.fori_loop(1, n, land_dp, 0)


def direct_gather(xd, xm, n, m):
    moved = n * xd.size * 2 + m * xm.size * 2
    return pl.pallas_call(
        functools.partial(gather_kernel, n, m),
        out_shape=(
            jax.ShapeDtypeStruct((n,) + xd.shape, xd.dtype),
            jax.ShapeDtypeStruct((m,) + xm.shape, xm.dtype),
        ),
        in_specs=[pl.BlockSpec(memory_space=pltpu.VMEM)] * 2,
        out_specs=(pl.BlockSpec(memory_space=pltpu.VMEM), pl.BlockSpec(memory_space=pltpu.VMEM)),
        scratch_shapes=[
            pltpu.SemaphoreType.DMA((n,)),
            pltpu.SemaphoreType.DMA((n,)),
            pltpu.SemaphoreType.DMA((m,)),
            pltpu.SemaphoreType.DMA((m,)),
        ],
        compiler_params=pltpu.CompilerParams(collective_id=1, has_side_effects=True),
        cost_estimate=pl.CostEstimate(flops=0, bytes_accessed=moved, transcendentals=0),
    )(xd, xm)


def per_device(
    tokens,
    q_weight,
    k_weight,
    v_weight,
    adapter_down,
    adapter_up,
    lengths,
    adapter_ids,
    head_gain,
    out_weight,
):
    row_count = tokens.shape[0]
    qf = q_weight.shape[1]
    heads_here = qf // F
    vw = v_weight.shape[1]
    value_width = vw // heads_here
    blocks = lax.axis_size("dp")
    place = lax.axis_index("dp")
    positions = place * row_count + jnp.arange(row_count, dtype=jnp.int32)
    request, starts, adapter = token_tables(lengths, adapter_ids, positions)

    local = jnp.concatenate([q_weight, k_weight, v_weight], axis=1)
    out_t = lax.all_gather(out_weight.T, "dp", axis=0, tiled=True)
    part_low = jnp.dot(tokens, adapter_down, preferred_element_type=jnp.float32)
    owners = lax.axis_index("mp") * (adapter_down.shape[1] // R) + (
        jnp.arange(adapter_down.shape[1], dtype=jnp.int32) // R
    )
    part_low = jnp.where(adapter[:, None] == owners[None, :], part_low, 0.0).astype(jnp.bfloat16)
    cols = lax.axis_size("mp")
    gathered, low_parts = direct_gather(local, part_low, blocks, cols)
    gathered = gathered.reshape(blocks * local.shape[0], local.shape[1])
    q_full = gathered[:, :qf]
    k_full = gathered[:, qf : 2 * qf]
    v_full = gathered[:, 2 * qf :]
    low_rank = jnp.transpose(low_parts, (1, 0, 2)).reshape(row_count, cols * part_low.shape[1])

    query_sum = jnp.dot(tokens, q_full, preferred_element_type=jnp.float32)
    key_sum = jnp.dot(tokens, k_full, preferred_element_type=jnp.float32)
    value_sum = jnp.dot(tokens, v_full, preferred_element_type=jnp.float32)
    query = query_sum.astype(jnp.bfloat16).reshape(row_count, heads_here, F)
    key_rows = key_sum.astype(jnp.bfloat16).reshape(row_count, heads_here, F)
    values = value_sum + jnp.dot(low_rank, adapter_up, preferred_element_type=jnp.float32)
    values = values.astype(jnp.bfloat16).reshape(row_count, heads_here, value_width)
    within, query_map, summary = block_local(query, key_rows, values, request, starts)

    rounds = max(1, (blocks - 1).bit_length())
    masks = scan_masks(lengths, row_count, place, blocks, rounds)
    carried = carried_scan(summary, masks, blocks, rounds)

    gains = head_gain.reshape(heads_here, value_width)
    normed = finish(within, query_map, carried, request, starts, gains).reshape(
        row_count, heads_here * value_width
    )
    partial_terms = lax.dot_general(
        normed, out_t, (((1,), (1,)), ((), ())), preferred_element_type=jnp.float32
    )
    return lax.psum_scatter(
        partial_terms.astype(jnp.bfloat16), "mp", scatter_dimension=1, tiled=True
    )


def solution(mesh):
    placed = (
        P("dp", None),
        P("dp", "mp"),
        P("dp", "mp"),
        P("dp", "mp"),
        P(None, "mp"),
        P(None, "mp"),
        P(),
        P(),
        P("mp"),
        P("mp", "dp"),
    )
    return jax.shard_map(
        per_device, mesh=mesh, in_specs=placed, out_specs=P("dp", "mp"), check_vma=False
    )
```

```python
import math

import functools

import jax
import jax.numpy as jnp
from jax import lax
from jax.experimental import pallas as pl
from jax.experimental.pallas import tpu as pltpu
from jax.sharding import PartitionSpec as P

MESH = pl.DeviceIdType.MESH

F = 16
R = 16


EPSILON = 1e-05


def taylor(inputs):
    squares = (inputs[..., :, None] * inputs[..., None, :]).reshape(
        inputs.shape[:-1] + (inputs.shape[-1] * inputs.shape[-1],)
    )
    constant = jnp.ones(inputs.shape[:-1] + (1,), jnp.float32)
    return jnp.concatenate([constant, 0.5 * inputs, squares * (0.25 / math.sqrt(2.0))], axis=-1)


def request_of(bounds, positions):
    return jnp.sum((positions[:, None] >= bounds[None, :]).astype(jnp.int32), axis=1)


def token_tables(lengths, adapter_ids, positions):
    bounds = jnp.cumsum(lengths)
    request = request_of(bounds, positions)
    openings = bounds - lengths
    starts = jnp.any(positions[:, None] == openings[None, :], axis=1)
    picked = request[:, None] == jnp.arange(lengths.shape[0], dtype=jnp.int32)[None, :]
    adapter = jnp.sum(jnp.where(picked, adapter_ids[None, :], 0), axis=1)
    return (request, starts, adapter)


def block_local(query, key_rows, values, request, starts):
    scores = jnp.einsum("ihd,jhd->hij", query, key_rows, preferred_element_type=jnp.float32) * 0.25
    weights = 1.0 + scores + 0.5 * scores * scores
    indexes = jnp.arange(request.shape[0], dtype=jnp.int32)
    allowed = (indexes[None, :] <= indexes[:, None]) & (request[None, :] == request[:, None])
    weights = jnp.where(allowed[None], weights, 0.0).astype(jnp.bfloat16)
    within = jnp.einsum("hij,jhe->ihe", weights, values, preferred_element_type=jnp.float32)
    query_map = taylor(query.astype(jnp.float32)).astype(jnp.bfloat16)
    key_map = taylor(key_rows.astype(jnp.float32)).astype(jnp.bfloat16)
    tail_mask = (request == request[-1]).astype(jnp.bfloat16)
    masked_keys = key_map * tail_mask[:, None, None]
    summary = jnp.einsum("ihf,ihe->hfe", masked_keys, values, preferred_element_type=jnp.float32)
    return (within, query_map, summary)


def finish(within, query_map, carried, request, starts, gains):
    follows = ((request == request[0]) & jnp.logical_not(starts[0])).astype(jnp.float32)
    cross = jnp.einsum(
        "ihf,hfe->ihe", query_map, carried.astype(jnp.bfloat16), preferred_element_type=jnp.float32
    )
    combined = within + follows[:, None, None] * cross
    factor = lax.rsqrt(jnp.mean(combined * combined, axis=-1, keepdims=True) + EPSILON)
    return (combined * factor * gains[None]).astype(jnp.bfloat16)


def scan_masks(lengths, row_count, place, blocks, rounds):
    openings = jnp.cumsum(lengths) - lengths
    ids = jnp.arange(blocks, dtype=jnp.int32)
    firsts = ids * row_count
    inside = (openings[None, :] >= firsts[:, None]) & (openings[None, :] < firsts[:, None] + row_count)
    flags = jnp.any(inside, axis=1).astype(jnp.int32)
    spans = jnp.asarray([1 << (k // 2) for k in range(2 * rounds)], jnp.int32)
    tops = place - jnp.asarray([k % 2 for k in range(2 * rounds)], jnp.int32)
    lows = place - spans + 1
    covered = (ids[None, :] >= lows[:, None]) & (ids[None, :] <= tops[:, None])
    hits = jnp.sum(jnp.where(covered, flags[None, :], 0), axis=1)
    return (hits == 0).astype(jnp.float32)


def scan_kernel(n, rounds, s_ref, m_ref, e_ref, parts, recv, send_sem, recv_sem):
    me = lax.axis_index("dp")
    col = lax.axis_index("mp")
    barrier = pltpu.get_barrier_semaphore()
    for k in range(rounds):
        d = 1 << k

        @pl.when(me + d < n)
        def _():
            pl.semaphore_signal(barrier, 1, device_id=(me + d, col), device_id_type=MESH)

        @pl.when(me >= d)
        def _():
            pl.semaphore_signal(barrier, 1, device_id=(me - d, col), device_id_type=MESH)

    peers = 0
    for k in range(rounds):
        d = 1 << k
        peers = peers + (me // d + n - 1) // n + ((n - 1 - me) // d + n - 1) // n
    pl.semaphore_wait(barrier, peers)

    e_ref[...] = jnp.zeros_like(e_ref)
    copies = []
    for k in range(rounds):
        d = 1 << k
        src = s_ref if k == 0 else parts.at[k - 1]
        copy = pltpu.make_async_remote_copy(
            src_ref=src,
            dst_ref=recv.at[k],
            send_sem=send_sem.at[k],
            recv_sem=recv_sem.at[k],
            device_id=(me + d, col),
            device_id_type=MESH,
        )
        copies.append(copy)

        @pl.when(me + d < n)
        def _():
            copy.start()

        @pl.when(me >= d)
        def _():
            copy.wait_recv()
            got = recv[k].astype(jnp.float32)
            if k < rounds - 1:
                parts[k] = (src[...].astype(jnp.float32) + m_ref[2 * k] * got).astype(parts.dtype)
            e_ref[...] += m_ref[2 * k + 1] * got

        if k < rounds - 1:

            @pl.when(me < d)
            def _():
                parts[k] = src[...]

    for k in range(rounds):
        d = 1 << k

        @pl.when(me + d < n)
        def _():
            copies[k].wait_send()


def carried_scan(summary, masks, n, rounds):
    shape = summary.shape
    flat = summary.reshape(-1, shape[-1]).astype(jnp.bfloat16)
    size = flat.shape[0] * flat.shape[1]
    out = pl.pallas_call(
        functools.partial(scan_kernel, n, rounds),
        out_shape=jax.ShapeDtypeStruct(flat.shape, jnp.float32),
        in_specs=[
            pl.BlockSpec(memory_space=pltpu.VMEM),
            pl.BlockSpec(memory_space=pltpu.SMEM),
        ],
        out_specs=pl.BlockSpec(memory_space=pltpu.VMEM),
        scratch_shapes=[
            pltpu.VMEM((max(rounds - 1, 1),) + flat.shape, jnp.bfloat16),
            pltpu.VMEM((rounds,) + flat.shape, jnp.bfloat16),
            pltpu.SemaphoreType.DMA((rounds,)),
            pltpu.SemaphoreType.DMA((rounds,)),
        ],
        compiler_params=pltpu.CompilerParams(collective_id=0, has_side_effects=True),
        cost_estimate=pl.CostEstimate(
            flops=3 * rounds * size, bytes_accessed=6 * rounds * size, transcendentals=0
        ),
    )(flat, masks)
    return out.reshape(shape)


def gather_kernel(n, m, xd_ref, xm_ref, gd_ref, gm_ref, send_d, recv_d, send_m, recv_m):
    me = lax.axis_index("dp")
    col = lax.axis_index("mp")
    barrier = pltpu.get_barrier_semaphore()

    def greet_dp(k, carry):
        pl.semaphore_signal(barrier, 1, device_id=((me + k) % n, col), device_id_type=MESH)
        return carry

    def greet_mp(k, carry):
        pl.semaphore_signal(barrier, 1, device_id=(me, (col + k) % m), device_id_type=MESH)
        return carry

    lax.fori_loop(1, n, greet_dp, 0)
    lax.fori_loop(1, m, greet_mp, 0)
    pl.semaphore_wait(barrier, n + m - 2)

    def to_dp(k):
        return pltpu.make_async_remote_copy(
            src_ref=xd_ref,
            dst_ref=gd_ref.at[me],
            send_sem=send_d.at[k],
            recv_sem=recv_d.at[me],
            device_id=((me + k) % n, col),
            device_id_type=MESH,
        )

    def to_mp(k):
        return pltpu.make_async_remote_copy(
            src_ref=xm_ref,
            dst_ref=gm_ref.at[col],
            send_sem=send_m.at[k],
            recv_sem=recv_m.at[col],
            device_id=(me, (col + k) % m),
            device_id_type=MESH,
        )

    def start_mp(k, carry):
        to_mp(k).start()
        return carry

    def start_dp(k, carry):
        to_dp(k).start()
        return carry

    lax.fori_loop(1, m, start_mp, 0)
    lax.fori_loop(1, n, start_dp, 0)
    gd_ref[me] = xd_ref[...]
    gm_ref[col] = xm_ref[...]

    def land_dp(k, carry):
        pltpu.make_async_remote_copy(
            src_ref=xd_ref,
            dst_ref=gd_ref.at[(me + n - k) % n],
            send_sem=send_d.at[k],
            recv_sem=recv_d.at[(me + n - k) % n],
            device_id=((me + n - k) % n, col),
            device_id_type=MESH,
        ).wait_recv()
        to_dp(k).wait_send()
        return carry

    def land_mp(k, carry):
        pltpu.make_async_remote_copy(
            src_ref=xm_ref,
            dst_ref=gm_ref.at[(col + m - k) % m],
            send_sem=send_m.at[k],
            recv_sem=recv_m.at[(col + m - k) % m],
            device_id=(me, (col + m - k) % m),
            device_id_type=MESH,
        ).wait_recv()
        to_mp(k).wait_send()
        return carry

    lax.fori_loop(1, m, land_mp, 0)
    lax.fori_loop(1, n, land_dp, 0)


def direct_gather(xd, xm, n, m):
    moved = n * xd.size * 2 + m * xm.size * 2
    return pl.pallas_call(
        functools.partial(gather_kernel, n, m),
        out_shape=(
            jax.ShapeDtypeStruct((n,) + xd.shape, xd.dtype),
            jax.ShapeDtypeStruct((m,) + xm.shape, xm.dtype),
        ),
        in_specs=[pl.BlockSpec(memory_space=pltpu.VMEM)] * 2,
        out_specs=(pl.BlockSpec(memory_space=pltpu.VMEM), pl.BlockSpec(memory_space=pltpu.VMEM)),
        scratch_shapes=[
            pltpu.SemaphoreType.DMA((n,)),
            pltpu.SemaphoreType.DMA((n,)),
            pltpu.SemaphoreType.DMA((m,)),
            pltpu.SemaphoreType.DMA((m,)),
        ],
        compiler_params=pltpu.CompilerParams(collective_id=1, has_side_effects=True),
        cost_estimate=pl.CostEstimate(flops=0, bytes_accessed=moved, transcendentals=0),
    )(xd, xm)


def per_device(
    tokens,
    q_weight,
    k_weight,
    v_weight,
    adapter_down,
    adapter_up,
    lengths,
    adapter_ids,
    head_gain,
    out_weight,
):
    row_count = tokens.shape[0]
    qf = q_weight.shape[1]
    heads_here = qf // F
    vw = v_weight.shape[1]
    value_width = vw // heads_here
    blocks = lax.axis_size("dp")
    place = lax.axis_index("dp")
    positions = place * row_count + jnp.arange(row_count, dtype=jnp.int32)
    request, starts, adapter = token_tables(lengths, adapter_ids, positions)

    local = jnp.concatenate([q_weight, k_weight, v_weight], axis=1)
    out_t = lax.all_gather(out_weight.T, "dp", axis=0, tiled=True)
    part_low = jnp.dot(tokens, adapter_down, preferred_element_type=jnp.float32)
    owners = lax.axis_index("mp") * (adapter_down.shape[1] // R) + (
        jnp.arange(adapter_down.shape[1], dtype=jnp.int32) // R
    )
    part_low = jnp.where(adapter[:, None] == owners[None, :], part_low, 0.0).astype(jnp.bfloat16)
    cols = lax.axis_size("mp")
    gathered, low_parts = direct_gather(local, part_low, blocks, cols)
    gathered = gathered.reshape(blocks * local.shape[0], local.shape[1])
    q_full = gathered[:, :qf]
    k_full = gathered[:, qf : 2 * qf]
    v_full = gathered[:, 2 * qf :]
    low_rank = jnp.transpose(low_parts, (1, 0, 2)).reshape(row_count, cols * part_low.shape[1])

    query_sum = jnp.dot(tokens, q_full, preferred_element_type=jnp.float32)
    key_sum = jnp.dot(tokens, k_full, preferred_element_type=jnp.float32)
    value_sum = jnp.dot(tokens, v_full, preferred_element_type=jnp.float32)
    query = query_sum.astype(jnp.bfloat16).reshape(row_count, heads_here, F)
    key_rows = key_sum.astype(jnp.bfloat16).reshape(row_count, heads_here, F)
    values = value_sum + jnp.dot(low_rank, adapter_up, preferred_element_type=jnp.float32)
    values = values.astype(jnp.bfloat16).reshape(row_count, heads_here, value_width)
    within, query_map, summary = block_local(query, key_rows, values, request, starts)

    rounds = max(1, (blocks - 1).bit_length())
    masks = scan_masks(lengths, row_count, place, blocks, rounds)
    carried = carried_scan(summary, masks, blocks, rounds)

    gains = head_gain.reshape(heads_here, value_width)
    normed = finish(within, query_map, carried, request, starts, gains).reshape(
        row_count, heads_here * value_width
    )
    partial_terms = lax.dot_general(
        normed, out_t, (((1,), (1,)), ((), ())), preferred_element_type=jnp.float32
    )
    return lax.psum_scatter(
        partial_terms.astype(jnp.bfloat16), "mp", scatter_dimension=1, tiled=True
    )


def solution(mesh):
    placed = (
        P("dp", None),
        P("dp", "mp"),
        P("dp", "mp"),
        P("dp", "mp"),
        P(None, "mp"),
        P(None, "mp"),
        P(),
        P(),
        P("mp"),
        P("mp", "dp"),
    )
    return jax.shard_map(
        per_device, mesh=mesh, in_specs=placed, out_specs=P("dp", "mp"), check_vma=False
    )
```

```python
import math

import functools

import jax
import jax.numpy as jnp
from jax import lax
from jax.experimental import pallas as pl
from jax.experimental.pallas import tpu as pltpu
from jax.sharding import PartitionSpec as P

MESH = pl.DeviceIdType.MESH

F = 16
R = 16


EPSILON = 1e-05


def taylor(inputs):
    squares = (inputs[..., :, None] * inputs[..., None, :]).reshape(
        inputs.shape[:-1] + (inputs.shape[-1] * inputs.shape[-1],)
    )
    constant = jnp.ones(inputs.shape[:-1] + (1,), jnp.float32)
    return jnp.concatenate([constant, 0.5 * inputs, squares * (0.25 / math.sqrt(2.0))], axis=-1)


def request_of(bounds, positions):
    return jnp.sum((positions[:, None] >= bounds[None, :]).astype(jnp.int32), axis=1)


def token_tables(lengths, adapter_ids, positions):
    bounds = jnp.cumsum(lengths)
    request = request_of(bounds, positions)
    openings = bounds - lengths
    starts = jnp.any(positions[:, None] == openings[None, :], axis=1)
    picked = request[:, None] == jnp.arange(lengths.shape[0], dtype=jnp.int32)[None, :]
    adapter = jnp.sum(jnp.where(picked, adapter_ids[None, :], 0), axis=1)
    return (request, starts, adapter)


def block_local(query, key_rows, values, request, starts):
    scores = jnp.einsum("ihd,jhd->hij", query, key_rows, preferred_element_type=jnp.float32) * 0.25
    weights = 1.0 + scores + 0.5 * scores * scores
    indexes = jnp.arange(request.shape[0], dtype=jnp.int32)
    allowed = (indexes[None, :] <= indexes[:, None]) & (request[None, :] == request[:, None])
    weights = jnp.where(allowed[None], weights, 0.0).astype(jnp.bfloat16)
    within = jnp.einsum("hij,jhe->ihe", weights, values, preferred_element_type=jnp.float32)
    query_map = taylor(query.astype(jnp.float32)).astype(jnp.bfloat16)
    key_map = taylor(key_rows.astype(jnp.float32)).astype(jnp.bfloat16)
    tail_mask = (request == request[-1]).astype(jnp.bfloat16)
    masked_keys = key_map * tail_mask[:, None, None]
    summary = jnp.einsum("ihf,ihe->hfe", masked_keys, values, preferred_element_type=jnp.float32)
    return (within, query_map, summary)


def finish(within, query_map, carried, request, starts, gains):
    follows = ((request == request[0]) & jnp.logical_not(starts[0])).astype(jnp.float32)
    cross = jnp.einsum(
        "ihf,hfe->ihe", query_map, carried.astype(jnp.bfloat16), preferred_element_type=jnp.float32
    )
    combined = within + follows[:, None, None] * cross
    factor = lax.rsqrt(jnp.mean(combined * combined, axis=-1, keepdims=True) + EPSILON)
    return (combined * factor * gains[None]).astype(jnp.bfloat16)


def scan_masks(lengths, row_count, place, blocks, rounds):
    openings = jnp.cumsum(lengths) - lengths
    ids = jnp.arange(blocks, dtype=jnp.int32)
    firsts = ids * row_count
    inside = (openings[None, :] >= firsts[:, None]) & (openings[None, :] < firsts[:, None] + row_count)
    flags = jnp.any(inside, axis=1).astype(jnp.int32)
    spans = jnp.asarray([1 << (k // 2) for k in range(2 * rounds)], jnp.int32)
    tops = place - jnp.asarray([k % 2 for k in range(2 * rounds)], jnp.int32)
    lows = place - spans + 1
    covered = (ids[None, :] >= lows[:, None]) & (ids[None, :] <= tops[:, None])
    hits = jnp.sum(jnp.where(covered, flags[None, :], 0), axis=1)
    return (hits == 0).astype(jnp.float32)


def scan_kernel(n, rounds, s_ref, m_ref, e_ref, parts, recv, send_sem, recv_sem):
    me = lax.axis_index("dp")
    col = lax.axis_index("mp")
    barrier = pltpu.get_barrier_semaphore()
    for k in range(rounds):
        d = 1 << k

        @pl.when(me + d < n)
        def _():
            pl.semaphore_signal(barrier, 1, device_id=(me + d, col), device_id_type=MESH)

        @pl.when(me >= d)
        def _():
            pl.semaphore_signal(barrier, 1, device_id=(me - d, col), device_id_type=MESH)

    peers = 0
    for k in range(rounds):
        d = 1 << k
        peers = peers + (me // d + n - 1) // n + ((n - 1 - me) // d + n - 1) // n
    pl.semaphore_wait(barrier, peers)

    e_ref[...] = jnp.zeros_like(e_ref)
    copies = []
    for k in range(rounds):
        d = 1 << k
        src = s_ref if k == 0 else parts.at[k - 1]
        copy = pltpu.make_async_remote_copy(
            src_ref=src,
            dst_ref=recv.at[k],
            send_sem=send_sem.at[k],
            recv_sem=recv_sem.at[k],
            device_id=(me + d, col),
            device_id_type=MESH,
        )
        copies.append(copy)

        @pl.when(me + d < n)
        def _():
            copy.start()

        @pl.when(me >= d)
        def _():
            copy.wait_recv()
            got = recv[k].astype(jnp.float32)
            if k < rounds - 1:
                parts[k] = (src[...].astype(jnp.float32) + m_ref[2 * k] * got).astype(parts.dtype)
            e_ref[...] += m_ref[2 * k + 1] * got

        if k < rounds - 1:

            @pl.when(me < d)
            def _():
                parts[k] = src[...]

    for k in range(rounds):
        d = 1 << k

        @pl.when(me + d < n)
        def _():
            copies[k].wait_send()


def carried_scan(summary, masks, n, rounds):
    shape = summary.shape
    flat = summary.reshape(-1, shape[-1]).astype(jnp.bfloat16)
    size = flat.shape[0] * flat.shape[1]
    out = pl.pallas_call(
        functools.partial(scan_kernel, n, rounds),
        out_shape=jax.ShapeDtypeStruct(flat.shape, jnp.float32),
        in_specs=[
            pl.BlockSpec(memory_space=pltpu.VMEM),
            pl.BlockSpec(memory_space=pltpu.SMEM),
        ],
        out_specs=pl.BlockSpec(memory_space=pltpu.VMEM),
        scratch_shapes=[
            pltpu.VMEM((max(rounds - 1, 1),) + flat.shape, jnp.bfloat16),
            pltpu.VMEM((rounds,) + flat.shape, jnp.bfloat16),
            pltpu.SemaphoreType.DMA((rounds,)),
            pltpu.SemaphoreType.DMA((rounds,)),
        ],
        compiler_params=pltpu.CompilerParams(collective_id=0, has_side_effects=True),
        cost_estimate=pl.CostEstimate(
            flops=3 * rounds * size, bytes_accessed=6 * rounds * size, transcendentals=0
        ),
    )(flat, masks)
    return out.reshape(shape)


def gather_kernel(n, m, row, xd_ref, xm_ref, gd_ref, gm_ref, send_r, recv_r, send_c, recv_c, send_m, recv_m, own):
    me = lax.axis_index("dp")
    col = lax.axis_index("mp")
    rows = n // row
    pos = me % row
    rid = me // row
    base = rid * row
    barrier = pltpu.get_barrier_semaphore()

    def greet_row(k, carry):
        pl.semaphore_signal(barrier, 1, device_id=(base + (pos + k) % row, col), device_id_type=MESH)
        return carry

    def greet_col(j, carry):
        pl.semaphore_signal(barrier, 1, device_id=((me + row * j) % n, col), device_id_type=MESH)
        return carry

    def greet_mp(k, carry):
        pl.semaphore_signal(barrier, 1, device_id=(me, (col + k) % m), device_id_type=MESH)
        return carry

    lax.fori_loop(1, row, greet_row, 0)
    lax.fori_loop(1, rows, greet_col, 0)
    lax.fori_loop(1, m, greet_mp, 0)
    pl.semaphore_wait(barrier, row + rows + m - 3)

    mine = pltpu.make_async_copy(xd_ref, gd_ref.at[me], own)
    mine.start()

    def to_row(k):
        return pltpu.make_async_remote_copy(
            src_ref=xd_ref,
            dst_ref=gd_ref.at[me],
            send_sem=send_r.at[k],
            recv_sem=recv_r.at[pos],
            device_id=(base + (pos + k) % row, col),
            device_id_type=MESH,
        )

    def from_row(k):
        other = (pos + row - k) % row
        return pltpu.make_async_remote_copy(
            src_ref=xd_ref,
            dst_ref=gd_ref.at[base + other],
            send_sem=send_r.at[k],
            recv_sem=recv_r.at[other],
            device_id=(base + other, col),
            device_id_type=MESH,
        )

    def to_col(j):
        return pltpu.make_async_remote_copy(
            src_ref=gd_ref.at[pl.ds(base, row)],
            dst_ref=gd_ref.at[pl.ds(base, row)],
            send_sem=send_c.at[j],
            recv_sem=recv_c.at[rid],
            device_id=((me + row * j) % n, col),
            device_id_type=MESH,
        )

    def from_col(j):
        other = (rid + rows - j) % rows
        return pltpu.make_async_remote_copy(
            src_ref=gd_ref.at[pl.ds(other * row, row)],
            dst_ref=gd_ref.at[pl.ds(other * row, row)],
            send_sem=send_c.at[j],
            recv_sem=recv_c.at[other],
            device_id=((me + n - row * j) % n, col),
            device_id_type=MESH,
        )

    def to_mp(k):
        return pltpu.make_async_remote_copy(
            src_ref=xm_ref,
            dst_ref=gm_ref.at[col],
            send_sem=send_m.at[k],
            recv_sem=recv_m.at[col],
            device_id=(me, (col + k) % m),
            device_id_type=MESH,
        )

    def from_mp(k):
        other = (col + m - k) % m
        return pltpu.make_async_remote_copy(
            src_ref=xm_ref,
            dst_ref=gm_ref.at[other],
            send_sem=send_m.at[k],
            recv_sem=recv_m.at[other],
            device_id=(me, other),
            device_id_type=MESH,
        )

    def each(lo, hi, body):
        def step(k, carry):
            body(k)
            return carry

        lax.fori_loop(lo, hi, step, 0)

    each(1, m, lambda k: to_mp(k).start())
    each(1, row, lambda k: to_row(k).start())
    gm_ref[col] = xm_ref[...]
    each(1, row, lambda k: from_row(k).wait_recv())
    mine.wait()
    each(1, rows, lambda j: to_col(j).start())
    each(1, m, lambda k: from_mp(k).wait_recv())
    each(1, rows, lambda j: from_col(j).wait_recv())
    each(1, row, lambda k: to_row(k).wait_send())
    each(1, rows, lambda j: to_col(j).wait_send())
    each(1, m, lambda k: to_mp(k).wait_send())


def direct_gather(xd, xm, n, m):
    row = 16 if n % 16 == 0 else n
    moved = n * xd.size * 2 + m * xm.size * 2
    return pl.pallas_call(
        functools.partial(gather_kernel, n, m, row),
        out_shape=(
            jax.ShapeDtypeStruct((n,) + xd.shape, xd.dtype),
            jax.ShapeDtypeStruct((m,) + xm.shape, xm.dtype),
        ),
        in_specs=[pl.BlockSpec(memory_space=pltpu.VMEM)] * 2,
        out_specs=(pl.BlockSpec(memory_space=pltpu.VMEM), pl.BlockSpec(memory_space=pltpu.VMEM)),
        scratch_shapes=[
            pltpu.SemaphoreType.DMA((row,)),
            pltpu.SemaphoreType.DMA((row,)),
            pltpu.SemaphoreType.DMA((n // row,)),
            pltpu.SemaphoreType.DMA((n // row,)),
            pltpu.SemaphoreType.DMA((m,)),
            pltpu.SemaphoreType.DMA((m,)),
            pltpu.SemaphoreType.DMA(()),
        ],
        compiler_params=pltpu.CompilerParams(collective_id=1, has_side_effects=True),
        cost_estimate=pl.CostEstimate(flops=0, bytes_accessed=moved, transcendentals=0),
    )(xd, xm)


def per_device(
    tokens,
    q_weight,
    k_weight,
    v_weight,
    adapter_down,
    adapter_up,
    lengths,
    adapter_ids,
    head_gain,
    out_weight,
):
    row_count = tokens.shape[0]
    qf = q_weight.shape[1]
    heads_here = qf // F
    vw = v_weight.shape[1]
    value_width = vw // heads_here
    blocks = lax.axis_size("dp")
    place = lax.axis_index("dp")
    positions = place * row_count + jnp.arange(row_count, dtype=jnp.int32)
    request, starts, adapter = token_tables(lengths, adapter_ids, positions)

    local = jnp.concatenate([q_weight, k_weight, v_weight], axis=1)
    out_t = lax.all_gather(out_weight.T, "dp", axis=0, tiled=True)
    part_low = jnp.dot(tokens, adapter_down, preferred_element_type=jnp.float32)
    owners = lax.axis_index("mp") * (adapter_down.shape[1] // R) + (
        jnp.arange(adapter_down.shape[1], dtype=jnp.int32) // R
    )
    part_low = jnp.where(adapter[:, None] == owners[None, :], part_low, 0.0).astype(jnp.bfloat16)
    cols = lax.axis_size("mp")
    gathered, low_parts = direct_gather(local, part_low, blocks, cols)
    gathered = gathered.reshape(blocks * local.shape[0], local.shape[1])
    q_full = gathered[:, :qf]
    k_full = gathered[:, qf : 2 * qf]
    v_full = gathered[:, 2 * qf :]
    low_rank = jnp.transpose(low_parts, (1, 0, 2)).reshape(row_count, cols * part_low.shape[1])

    query_sum = jnp.dot(tokens, q_full, preferred_element_type=jnp.float32)
    key_sum = jnp.dot(tokens, k_full, preferred_element_type=jnp.float32)
    value_sum = jnp.dot(tokens, v_full, preferred_element_type=jnp.float32)
    query = query_sum.astype(jnp.bfloat16).reshape(row_count, heads_here, F)
    key_rows = key_sum.astype(jnp.bfloat16).reshape(row_count, heads_here, F)
    values = value_sum + jnp.dot(low_rank, adapter_up, preferred_element_type=jnp.float32)
    values = values.astype(jnp.bfloat16).reshape(row_count, heads_here, value_width)
    within, query_map, summary = block_local(query, key_rows, values, request, starts)

    rounds = max(1, (blocks - 1).bit_length())
    masks = scan_masks(lengths, row_count, place, blocks, rounds)
    carried = carried_scan(summary, masks, blocks, rounds)

    gains = head_gain.reshape(heads_here, value_width)
    normed = finish(within, query_map, carried, request, starts, gains).reshape(
        row_count, heads_here * value_width
    )
    partial_terms = lax.dot_general(
        normed, out_t, (((1,), (1,)), ((), ())), preferred_element_type=jnp.float32
    )
    return lax.psum_scatter(
        partial_terms.astype(jnp.bfloat16), "mp", scatter_dimension=1, tiled=True
    )


def solution(mesh):
    placed = (
        P("dp", None),
        P("dp", "mp"),
        P("dp", "mp"),
        P("dp", "mp"),
        P(None, "mp"),
        P(None, "mp"),
        P(),
        P(),
        P("mp"),
        P("mp", "dp"),
    )
    return jax.shard_map(
        per_device, mesh=mesh, in_specs=placed, out_specs=P("dp", "mp"), check_vma=False
    )
```

```python
import math

import functools

import jax
import jax.numpy as jnp
from jax import lax
from jax.experimental import pallas as pl
from jax.experimental.pallas import tpu as pltpu
from jax.sharding import PartitionSpec as P

MESH = pl.DeviceIdType.MESH

F = 16
R = 16


EPSILON = 1e-05


def taylor(inputs):
    squares = (inputs[..., :, None] * inputs[..., None, :]).reshape(
        inputs.shape[:-1] + (inputs.shape[-1] * inputs.shape[-1],)
    )
    constant = jnp.ones(inputs.shape[:-1] + (1,), jnp.float32)
    return jnp.concatenate([constant, 0.5 * inputs, squares * (0.25 / math.sqrt(2.0))], axis=-1)


def request_of(bounds, positions):
    return jnp.sum((positions[:, None] >= bounds[None, :]).astype(jnp.int32), axis=1)


def token_tables(lengths, adapter_ids, positions):
    bounds = jnp.cumsum(lengths)
    request = request_of(bounds, positions)
    openings = bounds - lengths
    starts = jnp.any(positions[:, None] == openings[None, :], axis=1)
    picked = request[:, None] == jnp.arange(lengths.shape[0], dtype=jnp.int32)[None, :]
    adapter = jnp.sum(jnp.where(picked, adapter_ids[None, :], 0), axis=1)
    return (request, starts, adapter)


def block_local(query, key_rows, values, request, starts):
    scores = jnp.einsum("ihd,jhd->hij", query, key_rows, preferred_element_type=jnp.float32) * 0.25
    weights = 1.0 + scores + 0.5 * scores * scores
    indexes = jnp.arange(request.shape[0], dtype=jnp.int32)
    allowed = (indexes[None, :] <= indexes[:, None]) & (request[None, :] == request[:, None])
    weights = jnp.where(allowed[None], weights, 0.0).astype(jnp.bfloat16)
    within = jnp.einsum("hij,jhe->ihe", weights, values, preferred_element_type=jnp.float32)
    query_map = taylor(query.astype(jnp.float32)).astype(jnp.bfloat16)
    key_map = taylor(key_rows.astype(jnp.float32)).astype(jnp.bfloat16)
    tail_mask = (request == request[-1]).astype(jnp.bfloat16)
    masked_keys = key_map * tail_mask[:, None, None]
    summary = jnp.einsum("ihf,ihe->hfe", masked_keys, values, preferred_element_type=jnp.float32)
    return (within, query_map, summary)


def finish(within, query_map, carried, request, starts, gains):
    follows = ((request == request[0]) & jnp.logical_not(starts[0])).astype(jnp.float32)
    cross = jnp.einsum(
        "ihf,hfe->ihe", query_map, carried.astype(jnp.bfloat16), preferred_element_type=jnp.float32
    )
    combined = within + follows[:, None, None] * cross
    factor = lax.rsqrt(jnp.mean(combined * combined, axis=-1, keepdims=True) + EPSILON)
    return (combined * factor * gains[None]).astype(jnp.bfloat16)


def scan_masks(lengths, row_count, place, blocks, rounds):
    openings = jnp.cumsum(lengths) - lengths
    ids = jnp.arange(blocks, dtype=jnp.int32)
    firsts = ids * row_count
    inside = (openings[None, :] >= firsts[:, None]) & (openings[None, :] < firsts[:, None] + row_count)
    flags = jnp.any(inside, axis=1).astype(jnp.int32)
    spans = jnp.asarray([1 << (k // 2) for k in range(2 * rounds)], jnp.int32)
    tops = place - jnp.asarray([k % 2 for k in range(2 * rounds)], jnp.int32)
    lows = place - spans + 1
    covered = (ids[None, :] >= lows[:, None]) & (ids[None, :] <= tops[:, None])
    hits = jnp.sum(jnp.where(covered, flags[None, :], 0), axis=1)
    return (hits == 0).astype(jnp.float32)


def scan_kernel(n, rounds, s_ref, m_ref, e_ref, parts, recv, send_sem, recv_sem):
    me = lax.axis_index("dp")
    col = lax.axis_index("mp")
    barrier = pltpu.get_barrier_semaphore()
    for k in range(rounds):
        d = 1 << k

        @pl.when(me + d < n)
        def _():
            pl.semaphore_signal(barrier, 1, device_id=(me + d, col), device_id_type=MESH)

        @pl.when(me >= d)
        def _():
            pl.semaphore_signal(barrier, 1, device_id=(me - d, col), device_id_type=MESH)

    peers = 0
    for k in range(rounds):
        d = 1 << k
        peers = peers + (me // d + n - 1) // n + ((n - 1 - me) // d + n - 1) // n
    pl.semaphore_wait(barrier, peers)

    e_ref[...] = jnp.zeros_like(e_ref)
    copies = []
    for k in range(rounds):
        d = 1 << k
        src = s_ref if k == 0 else parts.at[k - 1]
        copy = pltpu.make_async_remote_copy(
            src_ref=src,
            dst_ref=recv.at[k],
            send_sem=send_sem.at[k],
            recv_sem=recv_sem.at[k],
            device_id=(me + d, col),
            device_id_type=MESH,
        )
        copies.append(copy)

        @pl.when(me + d < n)
        def _():
            copy.start()

        @pl.when(me >= d)
        def _():
            copy.wait_recv()
            got = recv[k].astype(jnp.float32)
            if k < rounds - 1:
                parts[k] = (src[...].astype(jnp.float32) + m_ref[2 * k] * got).astype(parts.dtype)
            e_ref[...] += m_ref[2 * k + 1] * got

        if k < rounds - 1:

            @pl.when(me < d)
            def _():
                parts[k] = src[...]

    for k in range(rounds):
        d = 1 << k

        @pl.when(me + d < n)
        def _():
            copies[k].wait_send()


def carried_scan(summary, masks, n, rounds):
    shape = summary.shape
    flat = summary.reshape(-1, shape[-1]).astype(jnp.bfloat16)
    size = flat.shape[0] * flat.shape[1]
    out = pl.pallas_call(
        functools.partial(scan_kernel, n, rounds),
        out_shape=jax.ShapeDtypeStruct(flat.shape, jnp.float32),
        in_specs=[
            pl.BlockSpec(memory_space=pltpu.VMEM),
            pl.BlockSpec(memory_space=pltpu.SMEM),
        ],
        out_specs=pl.BlockSpec(memory_space=pltpu.VMEM),
        scratch_shapes=[
            pltpu.VMEM((max(rounds - 1, 1),) + flat.shape, jnp.bfloat16),
            pltpu.VMEM((rounds,) + flat.shape, jnp.bfloat16),
            pltpu.SemaphoreType.DMA((rounds,)),
            pltpu.SemaphoreType.DMA((rounds,)),
        ],
        compiler_params=pltpu.CompilerParams(collective_id=0, has_side_effects=True),
        cost_estimate=pl.CostEstimate(
            flops=3 * rounds * size, bytes_accessed=6 * rounds * size, transcendentals=0
        ),
    )(flat, masks)
    return out.reshape(shape)


def gather_kernel(n, m, xd_ref, xm_ref, gd_ref, gm_ref, send_d, recv_d, send_m, recv_m):
    me = lax.axis_index("dp")
    col = lax.axis_index("mp")
    barrier = pltpu.get_barrier_semaphore()

    def greet_dp(k, carry):
        pl.semaphore_signal(barrier, 1, device_id=((me + k) % n, col), device_id_type=MESH)
        return carry

    def greet_mp(k, carry):
        pl.semaphore_signal(barrier, 1, device_id=(me, (col + k) % m), device_id_type=MESH)
        return carry

    lax.fori_loop(1, n, greet_dp, 0)
    lax.fori_loop(1, m, greet_mp, 0)
    pl.semaphore_wait(barrier, n + m - 2)

    def to_dp(k):
        return pltpu.make_async_remote_copy(
            src_ref=xd_ref,
            dst_ref=gd_ref.at[me],
            send_sem=send_d.at[k],
            recv_sem=recv_d.at[me],
            device_id=((me + k) % n, col),
            device_id_type=MESH,
        )

    def to_mp(k):
        return pltpu.make_async_remote_copy(
            src_ref=xm_ref,
            dst_ref=gm_ref.at[col],
            send_sem=send_m.at[k],
            recv_sem=recv_m.at[col],
            device_id=(me, (col + k) % m),
            device_id_type=MESH,
        )

    def start_mp(k, carry):
        to_mp(k).start()
        return carry

    def start_dp(k, carry):
        to_dp(k).start()
        return carry

    lax.fori_loop(1, m, start_mp, 0)
    lax.fori_loop(1, n, start_dp, 0)
    gd_ref[me] = xd_ref[...]
    gm_ref[col] = xm_ref[...]

    def land_dp(k, carry):
        pltpu.make_async_remote_copy(
            src_ref=xd_ref,
            dst_ref=gd_ref.at[(me + n - k) % n],
            send_sem=send_d.at[k],
            recv_sem=recv_d.at[(me + n - k) % n],
            device_id=((me + n - k) % n, col),
            device_id_type=MESH,
        ).wait_recv()
        to_dp(k).wait_send()
        return carry

    def land_mp(k, carry):
        pltpu.make_async_remote_copy(
            src_ref=xm_ref,
            dst_ref=gm_ref.at[(col + m - k) % m],
            send_sem=send_m.at[k],
            recv_sem=recv_m.at[(col + m - k) % m],
            device_id=(me, (col + m - k) % m),
            device_id_type=MESH,
        ).wait_recv()
        to_mp(k).wait_send()
        return carry

    lax.fori_loop(1, m, land_mp, 0)
    lax.fori_loop(1, n, land_dp, 0)


def direct_gather(xd, xm, n, m):
    moved = n * xd.size * 2 + m * xm.size * 2
    return pl.pallas_call(
        functools.partial(gather_kernel, n, m),
        out_shape=(
            jax.ShapeDtypeStruct((n,) + xd.shape, xd.dtype),
            jax.ShapeDtypeStruct((m,) + xm.shape, xm.dtype),
        ),
        in_specs=[pl.BlockSpec(memory_space=pltpu.VMEM)] * 2,
        out_specs=(pl.BlockSpec(memory_space=pltpu.VMEM), pl.BlockSpec(memory_space=pltpu.VMEM)),
        scratch_shapes=[
            pltpu.SemaphoreType.DMA((n,)),
            pltpu.SemaphoreType.DMA((n,)),
            pltpu.SemaphoreType.DMA((m,)),
            pltpu.SemaphoreType.DMA((m,)),
        ],
        compiler_params=pltpu.CompilerParams(collective_id=1, has_side_effects=True),
        cost_estimate=pl.CostEstimate(flops=0, bytes_accessed=moved, transcendentals=0),
    )(xd, xm)


def ring_kernel(m, x_ref, o_ref, acc_a, acc_b, got_a, got_b, send_a, recv_a, send_b, recv_b):
    me = lax.axis_index("dp")
    col = lax.axis_index("mp")
    right = (col + 1) % m
    left = (col + m - 1) % m
    width = o_ref.shape[1]
    half = width // 2
    barrier = pltpu.get_barrier_semaphore()
    pl.semaphore_signal(barrier, 1, device_id=(me, right), device_id_type=MESH)
    pl.semaphore_signal(barrier, 1, device_id=(me, left), device_id_type=MESH)
    pl.semaphore_wait(barrier, 2)

    def piece(t, side):
        return pl.ds(pl.multiple_of(t * width + side * half, half), half)

    copies = []
    for s in range(m - 1):
        ta = (col + 2 * m - 1 - s) % m
        tb = (col + 1 + s) % m
        if s == 0:
            src_a = x_ref.at[:, piece(ta, 0)]
            src_b = x_ref.at[:, piece(tb, 1)]
        else:
            copies[-1][0].wait_recv()
            copies[-1][1].wait_recv()
            acc_a[s - 1] = (
                got_a[s - 1].astype(jnp.float32) + x_ref[:, piece(ta, 0)].astype(jnp.float32)
            ).astype(acc_a.dtype)
            acc_b[s - 1] = (
                got_b[s - 1].astype(jnp.float32) + x_ref[:, piece(tb, 1)].astype(jnp.float32)
            ).astype(acc_b.dtype)
            src_a = acc_a.at[s - 1]
            src_b = acc_b.at[s - 1]
        ca = pltpu.make_async_remote_copy(
            src_ref=src_a,
            dst_ref=got_a.at[s],
            send_sem=send_a.at[s],
            recv_sem=recv_a.at[s],
            device_id=(me, right),
            device_id_type=MESH,
        )
        cb = pltpu.make_async_remote_copy(
            src_ref=src_b,
            dst_ref=got_b.at[s],
            send_sem=send_b.at[s],
            recv_sem=recv_b.at[s],
            device_id=(me, left),
            device_id_type=MESH,
        )
        ca.start()
        cb.start()
        copies.append((ca, cb))
    copies[-1][0].wait_recv()
    copies[-1][1].wait_recv()
    last = m - 2
    o_ref[:, :half] = (
        got_a[last].astype(jnp.float32) + x_ref[:, piece(col, 0)].astype(jnp.float32)
    ).astype(o_ref.dtype)
    o_ref[:, half:] = (
        got_b[last].astype(jnp.float32) + x_ref[:, piece(col, 1)].astype(jnp.float32)
    ).astype(o_ref.dtype)
    for ca, cb in copies:
        ca.wait_send()
        cb.wait_send()


def ring_scatter(x, m):
    rows, total = x.shape
    width = total // m
    half = width // 2
    slot = (m - 1, rows, half)
    return pl.pallas_call(
        functools.partial(ring_kernel, m),
        out_shape=jax.ShapeDtypeStruct((rows, width), x.dtype),
        in_specs=[pl.BlockSpec(memory_space=pltpu.VMEM)],
        out_specs=pl.BlockSpec(memory_space=pltpu.VMEM),
        scratch_shapes=[
            pltpu.VMEM(slot, x.dtype),
            pltpu.VMEM(slot, x.dtype),
            pltpu.VMEM(slot, x.dtype),
            pltpu.VMEM(slot, x.dtype),
            pltpu.SemaphoreType.DMA((m - 1,)),
            pltpu.SemaphoreType.DMA((m - 1,)),
            pltpu.SemaphoreType.DMA((m - 1,)),
            pltpu.SemaphoreType.DMA((m - 1,)),
        ],
        compiler_params=pltpu.CompilerParams(collective_id=2, has_side_effects=True),
        cost_estimate=pl.CostEstimate(
            flops=2 * rows * total, bytes_accessed=4 * rows * total, transcendentals=0
        ),
    )(x)


def per_device(
    tokens,
    q_weight,
    k_weight,
    v_weight,
    adapter_down,
    adapter_up,
    lengths,
    adapter_ids,
    head_gain,
    out_weight,
):
    row_count = tokens.shape[0]
    qf = q_weight.shape[1]
    heads_here = qf // F
    vw = v_weight.shape[1]
    value_width = vw // heads_here
    blocks = lax.axis_size("dp")
    place = lax.axis_index("dp")
    positions = place * row_count + jnp.arange(row_count, dtype=jnp.int32)
    request, starts, adapter = token_tables(lengths, adapter_ids, positions)

    local = jnp.concatenate([q_weight, k_weight, v_weight], axis=1)
    out_t = lax.all_gather(out_weight.T, "dp", axis=0, tiled=True)
    part_low = jnp.dot(tokens, adapter_down, preferred_element_type=jnp.float32)
    owners = lax.axis_index("mp") * (adapter_down.shape[1] // R) + (
        jnp.arange(adapter_down.shape[1], dtype=jnp.int32) // R
    )
    part_low = jnp.where(adapter[:, None] == owners[None, :], part_low, 0.0).astype(jnp.bfloat16)
    cols = lax.axis_size("mp")
    gathered, low_parts = direct_gather(local, part_low, blocks, cols)
    gathered = gathered.reshape(blocks * local.shape[0], local.shape[1])
    q_full = gathered[:, :qf]
    k_full = gathered[:, qf : 2 * qf]
    v_full = gathered[:, 2 * qf :]
    low_rank = jnp.transpose(low_parts, (1, 0, 2)).reshape(row_count, cols * part_low.shape[1])

    query_sum = jnp.dot(tokens, q_full, preferred_element_type=jnp.float32)
    key_sum = jnp.dot(tokens, k_full, preferred_element_type=jnp.float32)
    value_sum = jnp.dot(tokens, v_full, preferred_element_type=jnp.float32)
    query = query_sum.astype(jnp.bfloat16).reshape(row_count, heads_here, F)
    key_rows = key_sum.astype(jnp.bfloat16).reshape(row_count, heads_here, F)
    values = value_sum + jnp.dot(low_rank, adapter_up, preferred_element_type=jnp.float32)
    values = values.astype(jnp.bfloat16).reshape(row_count, heads_here, value_width)
    within, query_map, summary = block_local(query, key_rows, values, request, starts)

    rounds = max(1, (blocks - 1).bit_length())
    masks = scan_masks(lengths, row_count, place, blocks, rounds)
    carried = carried_scan(summary, masks, blocks, rounds)

    gains = head_gain.reshape(heads_here, value_width)
    normed = finish(within, query_map, carried, request, starts, gains).reshape(
        row_count, heads_here * value_width
    )
    partial_terms = lax.dot_general(
        normed, out_t, (((1,), (1,)), ((), ())), preferred_element_type=jnp.float32
    )
    return ring_scatter(partial_terms.astype(jnp.bfloat16), cols)


def solution(mesh):
    placed = (
        P("dp", None),
        P("dp", "mp"),
        P("dp", "mp"),
        P("dp", "mp"),
        P(None, "mp"),
        P(None, "mp"),
        P(),
        P(),
        P("mp"),
        P("mp", "dp"),
    )
    return jax.shard_map(
        per_device, mesh=mesh, in_specs=placed, out_specs=P("dp", "mp"), check_vma=False
    )
```

```python
import math

import functools

import jax
import jax.numpy as jnp
from jax import lax
from jax.experimental import pallas as pl
from jax.experimental.pallas import tpu as pltpu
from jax.sharding import PartitionSpec as P

MESH = pl.DeviceIdType.MESH

F = 16
R = 16


EPSILON = 1e-05


def taylor(inputs):
    squares = (inputs[..., :, None] * inputs[..., None, :]).reshape(
        inputs.shape[:-1] + (inputs.shape[-1] * inputs.shape[-1],)
    )
    constant = jnp.ones(inputs.shape[:-1] + (1,), jnp.float32)
    return jnp.concatenate([constant, 0.5 * inputs, squares * (0.25 / math.sqrt(2.0))], axis=-1)


def request_of(bounds, positions):
    return jnp.sum((positions[:, None] >= bounds[None, :]).astype(jnp.int32), axis=1)


def token_tables(lengths, adapter_ids, positions):
    bounds = jnp.cumsum(lengths)
    request = request_of(bounds, positions)
    openings = bounds - lengths
    starts = jnp.any(positions[:, None] == openings[None, :], axis=1)
    picked = request[:, None] == jnp.arange(lengths.shape[0], dtype=jnp.int32)[None, :]
    adapter = jnp.sum(jnp.where(picked, adapter_ids[None, :], 0), axis=1)
    return (request, starts, adapter)


def block_local(query, key_rows, values, request, starts):
    scores = jnp.einsum("ihd,jhd->hij", query, key_rows, preferred_element_type=jnp.float32) * 0.25
    weights = 1.0 + scores + 0.5 * scores * scores
    indexes = jnp.arange(request.shape[0], dtype=jnp.int32)
    allowed = (indexes[None, :] <= indexes[:, None]) & (request[None, :] == request[:, None])
    weights = jnp.where(allowed[None], weights, 0.0).astype(jnp.bfloat16)
    within = jnp.einsum("hij,jhe->ihe", weights, values, preferred_element_type=jnp.float32)
    query_map = taylor(query.astype(jnp.float32)).astype(jnp.bfloat16)
    key_map = taylor(key_rows.astype(jnp.float32)).astype(jnp.bfloat16)
    tail_mask = (request == request[-1]).astype(jnp.bfloat16)
    masked_keys = key_map * tail_mask[:, None, None]
    summary = jnp.einsum("ihf,ihe->hfe", masked_keys, values, preferred_element_type=jnp.float32)
    return (within, query_map, summary)


def finish(within, query_map, carried, request, starts, gains):
    follows = ((request == request[0]) & jnp.logical_not(starts[0])).astype(jnp.float32)
    cross = jnp.einsum(
        "ihf,hfe->ihe", query_map, carried.astype(jnp.bfloat16), preferred_element_type=jnp.float32
    )
    combined = within + follows[:, None, None] * cross
    factor = lax.rsqrt(jnp.mean(combined * combined, axis=-1, keepdims=True) + EPSILON)
    return (combined * factor * gains[None]).astype(jnp.bfloat16)


def scan_masks(lengths, row_count, place, blocks, rounds):
    openings = jnp.cumsum(lengths) - lengths
    ids = jnp.arange(blocks, dtype=jnp.int32)
    firsts = ids * row_count
    inside = (openings[None, :] >= firsts[:, None]) & (openings[None, :] < firsts[:, None] + row_count)
    flags = jnp.any(inside, axis=1).astype(jnp.int32)
    spans = jnp.asarray([1 << (k // 2) for k in range(2 * rounds)], jnp.int32)
    tops = place - jnp.asarray([k % 2 for k in range(2 * rounds)], jnp.int32)
    lows = place - spans + 1
    covered = (ids[None, :] >= lows[:, None]) & (ids[None, :] <= tops[:, None])
    hits = jnp.sum(jnp.where(covered, flags[None, :], 0), axis=1)
    return (hits == 0).astype(jnp.float32)


def scan_kernel(n, rounds, s_ref, m_ref, e_ref, parts, recv, send_sem, recv_sem):
    me = lax.axis_index("dp")
    col = lax.axis_index("mp")
    barrier = pltpu.get_barrier_semaphore()
    for k in range(rounds):
        d = 1 << k

        @pl.when(me + d < n)
        def _():
            pl.semaphore_signal(barrier, 1, device_id=(me + d, col), device_id_type=MESH)

        @pl.when(me >= d)
        def _():
            pl.semaphore_signal(barrier, 1, device_id=(me - d, col), device_id_type=MESH)

    peers = 0
    for k in range(rounds):
        d = 1 << k
        peers = peers + (me // d + n - 1) // n + ((n - 1 - me) // d + n - 1) // n
    pl.semaphore_wait(barrier, peers)

    e_ref[...] = jnp.zeros_like(e_ref)
    copies = []
    for k in range(rounds):
        d = 1 << k
        src = s_ref if k == 0 else parts.at[k - 1]
        copy = pltpu.make_async_remote_copy(
            src_ref=src,
            dst_ref=recv.at[k],
            send_sem=send_sem.at[k],
            recv_sem=recv_sem.at[k],
            device_id=(me + d, col),
            device_id_type=MESH,
        )
        copies.append(copy)

        @pl.when(me + d < n)
        def _():
            copy.start()

        @pl.when(me >= d)
        def _():
            copy.wait_recv()
            got = recv[k].astype(jnp.float32)
            if k < rounds - 1:
                parts[k] = (src[...].astype(jnp.float32) + m_ref[2 * k] * got).astype(parts.dtype)
            e_ref[...] += m_ref[2 * k + 1] * got

        if k < rounds - 1:

            @pl.when(me < d)
            def _():
                parts[k] = src[...]

    for k in range(rounds):
        d = 1 << k

        @pl.when(me + d < n)
        def _():
            copies[k].wait_send()


def carried_scan(summary, masks, n, rounds):
    shape = summary.shape
    flat = summary.reshape(-1, shape[-1]).astype(jnp.bfloat16)
    size = flat.shape[0] * flat.shape[1]
    out = pl.pallas_call(
        functools.partial(scan_kernel, n, rounds),
        out_shape=jax.ShapeDtypeStruct(flat.shape, jnp.float32),
        in_specs=[
            pl.BlockSpec(memory_space=pltpu.VMEM),
            pl.BlockSpec(memory_space=pltpu.SMEM),
        ],
        out_specs=pl.BlockSpec(memory_space=pltpu.VMEM),
        scratch_shapes=[
            pltpu.VMEM((max(rounds - 1, 1),) + flat.shape, jnp.bfloat16),
            pltpu.VMEM((rounds,) + flat.shape, jnp.bfloat16),
            pltpu.SemaphoreType.DMA((rounds,)),
            pltpu.SemaphoreType.DMA((rounds,)),
        ],
        compiler_params=pltpu.CompilerParams(collective_id=0, has_side_effects=True),
        cost_estimate=pl.CostEstimate(
            flops=3 * rounds * size, bytes_accessed=6 * rounds * size, transcendentals=0
        ),
    )(flat, masks)
    return out.reshape(shape)


def gather_kernel(n, m, xd_ref, xm_ref, gd_ref, gm_ref, send_d, recv_d, send_m, recv_m):
    me = lax.axis_index("dp")
    col = lax.axis_index("mp")
    barrier = pltpu.get_barrier_semaphore()

    def greet_dp(k, carry):
        pl.semaphore_signal(barrier, 1, device_id=((me + k) % n, col), device_id_type=MESH)
        return carry

    def greet_mp(k, carry):
        pl.semaphore_signal(barrier, 1, device_id=(me, (col + k) % m), device_id_type=MESH)
        return carry

    lax.fori_loop(1, n, greet_dp, 0)
    lax.fori_loop(1, m, greet_mp, 0)
    pl.semaphore_wait(barrier, n + m - 2)

    def to_dp(k):
        return pltpu.make_async_remote_copy(
            src_ref=xd_ref,
            dst_ref=gd_ref.at[me],
            send_sem=send_d.at[k],
            recv_sem=recv_d.at[me],
            device_id=((me + k) % n, col),
            device_id_type=MESH,
        )

    def to_mp(k):
        return pltpu.make_async_remote_copy(
            src_ref=xm_ref,
            dst_ref=gm_ref.at[col],
            send_sem=send_m.at[k],
            recv_sem=recv_m.at[col],
            device_id=(me, (col + k) % m),
            device_id_type=MESH,
        )

    def start_mp(k, carry):
        to_mp(k).start()
        return carry

    def start_dp(k, carry):
        to_dp(k).start()
        return carry

    lax.fori_loop(1, m, start_mp, 0)
    lax.fori_loop(1, n, start_dp, 0)
    gd_ref[me] = xd_ref[...]
    gm_ref[col] = xm_ref[...]

    def land_dp(k, carry):
        pltpu.make_async_remote_copy(
            src_ref=xd_ref,
            dst_ref=gd_ref.at[(me + n - k) % n],
            send_sem=send_d.at[k],
            recv_sem=recv_d.at[(me + n - k) % n],
            device_id=((me + n - k) % n, col),
            device_id_type=MESH,
        ).wait_recv()
        to_dp(k).wait_send()
        return carry

    def land_mp(k, carry):
        pltpu.make_async_remote_copy(
            src_ref=xm_ref,
            dst_ref=gm_ref.at[(col + m - k) % m],
            send_sem=send_m.at[k],
            recv_sem=recv_m.at[(col + m - k) % m],
            device_id=(me, (col + m - k) % m),
            device_id_type=MESH,
        ).wait_recv()
        to_mp(k).wait_send()
        return carry

    lax.fori_loop(1, m, land_mp, 0)
    lax.fori_loop(1, n, land_dp, 0)


def direct_gather(xd, xm, n, m):
    moved = n * xd.size * 2 + m * xm.size * 2
    return pl.pallas_call(
        functools.partial(gather_kernel, n, m),
        out_shape=(
            jax.ShapeDtypeStruct((n,) + xd.shape, xd.dtype),
            jax.ShapeDtypeStruct((m,) + xm.shape, xm.dtype),
        ),
        in_specs=[pl.BlockSpec(memory_space=pltpu.VMEM)] * 2,
        out_specs=(pl.BlockSpec(memory_space=pltpu.VMEM), pl.BlockSpec(memory_space=pltpu.VMEM)),
        scratch_shapes=[
            pltpu.SemaphoreType.DMA((n,)),
            pltpu.SemaphoreType.DMA((n,)),
            pltpu.SemaphoreType.DMA((m,)),
            pltpu.SemaphoreType.DMA((m,)),
        ],
        compiler_params=pltpu.CompilerParams(collective_id=1, has_side_effects=True),
        cost_estimate=pl.CostEstimate(flops=0, bytes_accessed=moved, transcendentals=0),
    )(xd, xm)


def ring_kernel(m, x_ref, o_ref, acc_a, acc_b, got_a, got_b, send_a, recv_a, send_b, recv_b):
    me = lax.axis_index("dp")
    col = lax.axis_index("mp")
    right = (col + 1) % m
    left = (col + m - 1) % m
    width = o_ref.shape[1]
    half = width // 2
    barrier = pltpu.get_barrier_semaphore()
    pl.semaphore_signal(barrier, 1, device_id=(me, right), device_id_type=MESH)
    pl.semaphore_signal(barrier, 1, device_id=(me, left), device_id_type=MESH)
    pl.semaphore_wait(barrier, 2)

    def piece(t, side):
        return pl.ds(pl.multiple_of(t * width + side * half, half), half)

    copies = []
    for s in range(m - 1):
        ta = (col + 2 * m - 1 - s) % m
        tb = (col + 1 + s) % m
        if s == 0:
            src_a = x_ref.at[:, piece(ta, 0)]
            src_b = x_ref.at[:, piece(tb, 1)]
        else:
            copies[-1][0].wait_recv()
            copies[-1][1].wait_recv()
            acc_a[s - 1] = (
                got_a[s - 1].astype(jnp.float32) + x_ref[:, piece(ta, 0)].astype(jnp.float32)
            ).astype(acc_a.dtype)
            acc_b[s - 1] = (
                got_b[s - 1].astype(jnp.float32) + x_ref[:, piece(tb, 1)].astype(jnp.float32)
            ).astype(acc_b.dtype)
            src_a = acc_a.at[s - 1]
            src_b = acc_b.at[s - 1]
        ca = pltpu.make_async_remote_copy(
            src_ref=src_a,
            dst_ref=got_a.at[s],
            send_sem=send_a.at[s],
            recv_sem=recv_a.at[s],
            device_id=(me, right),
            device_id_type=MESH,
        )
        cb = pltpu.make_async_remote_copy(
            src_ref=src_b,
            dst_ref=got_b.at[s],
            send_sem=send_b.at[s],
            recv_sem=recv_b.at[s],
            device_id=(me, left),
            device_id_type=MESH,
        )
        ca.start()
        cb.start()
        copies.append((ca, cb))
    copies[-1][0].wait_recv()
    copies[-1][1].wait_recv()
    last = m - 2
    o_ref[:, :half] = (
        got_a[last].astype(jnp.float32) + x_ref[:, piece(col, 0)].astype(jnp.float32)
    ).astype(o_ref.dtype)
    o_ref[:, half:] = (
        got_b[last].astype(jnp.float32) + x_ref[:, piece(col, 1)].astype(jnp.float32)
    ).astype(o_ref.dtype)
    for ca, cb in copies:
        ca.wait_send()
        cb.wait_send()


def ring_scatter(x, m):
    rows, total = x.shape
    width = total // m
    half = width // 2
    slot = (m - 1, rows, half)
    return pl.pallas_call(
        functools.partial(ring_kernel, m),
        out_shape=jax.ShapeDtypeStruct((rows, width), x.dtype),
        in_specs=[pl.BlockSpec(memory_space=pltpu.VMEM)],
        out_specs=pl.BlockSpec(memory_space=pltpu.VMEM),
        scratch_shapes=[
            pltpu.VMEM(slot, x.dtype),
            pltpu.VMEM(slot, x.dtype),
            pltpu.VMEM(slot, x.dtype),
            pltpu.VMEM(slot, x.dtype),
            pltpu.SemaphoreType.DMA((m - 1,)),
            pltpu.SemaphoreType.DMA((m - 1,)),
            pltpu.SemaphoreType.DMA((m - 1,)),
            pltpu.SemaphoreType.DMA((m - 1,)),
        ],
        compiler_params=pltpu.CompilerParams(collective_id=2, has_side_effects=True),
        cost_estimate=pl.CostEstimate(
            flops=2 * rows * total, bytes_accessed=4 * rows * total, transcendentals=0
        ),
    )(x)


def doubling_gather(piece, n, place):
    held = piece
    step = 1
    while step < n:
        other = lax.ppermute(held, "dp", perm=[(i, i ^ step) for i in range(n)])
        low = (place // step) % 2 == 0
        held = jnp.where(
            low, jnp.concatenate([held, other], axis=0), jnp.concatenate([other, held], axis=0)
        )
        step *= 2
    return held


def per_device(
    tokens,
    q_weight,
    k_weight,
    v_weight,
    adapter_down,
    adapter_up,
    lengths,
    adapter_ids,
    head_gain,
    out_weight,
):
    row_count = tokens.shape[0]
    qf = q_weight.shape[1]
    heads_here = qf // F
    vw = v_weight.shape[1]
    value_width = vw // heads_here
    blocks = lax.axis_size("dp")
    place = lax.axis_index("dp")
    positions = place * row_count + jnp.arange(row_count, dtype=jnp.int32)
    request, starts, adapter = token_tables(lengths, adapter_ids, positions)

    local = jnp.concatenate([q_weight, k_weight, v_weight], axis=1)
    out_t = doubling_gather(out_weight.T, blocks, place)
    part_low = jnp.dot(tokens, adapter_down, preferred_element_type=jnp.float32)
    owners = lax.axis_index("mp") * (adapter_down.shape[1] // R) + (
        jnp.arange(adapter_down.shape[1], dtype=jnp.int32) // R
    )
    part_low = jnp.where(adapter[:, None] == owners[None, :], part_low, 0.0).astype(jnp.bfloat16)
    cols = lax.axis_size("mp")
    gathered, low_parts = direct_gather(local, part_low, blocks, cols)
    gathered = gathered.reshape(blocks * local.shape[0], local.shape[1])
    q_full = gathered[:, :qf]
    k_full = gathered[:, qf : 2 * qf]
    v_full = gathered[:, 2 * qf :]
    low_rank = jnp.transpose(low_parts, (1, 0, 2)).reshape(row_count, cols * part_low.shape[1])

    query_sum = jnp.dot(tokens, q_full, preferred_element_type=jnp.float32)
    key_sum = jnp.dot(tokens, k_full, preferred_element_type=jnp.float32)
    value_sum = jnp.dot(tokens, v_full, preferred_element_type=jnp.float32)
    query = query_sum.astype(jnp.bfloat16).reshape(row_count, heads_here, F)
    key_rows = key_sum.astype(jnp.bfloat16).reshape(row_count, heads_here, F)
    values = value_sum + jnp.dot(low_rank, adapter_up, preferred_element_type=jnp.float32)
    values = values.astype(jnp.bfloat16).reshape(row_count, heads_here, value_width)
    within, query_map, summary = block_local(query, key_rows, values, request, starts)

    rounds = max(1, (blocks - 1).bit_length())
    masks = scan_masks(lengths, row_count, place, blocks, rounds)
    carried = carried_scan(summary, masks, blocks, rounds)

    gains = head_gain.reshape(heads_here, value_width)
    normed = finish(within, query_map, carried, request, starts, gains).reshape(
        row_count, heads_here * value_width
    )
    partial_terms = lax.dot_general(
        normed, out_t, (((1,), (1,)), ((), ())), preferred_element_type=jnp.float32
    )
    return ring_scatter(partial_terms.astype(jnp.bfloat16), cols)


def solution(mesh):
    placed = (
        P("dp", None),
        P("dp", "mp"),
        P("dp", "mp"),
        P("dp", "mp"),
        P(None, "mp"),
        P(None, "mp"),
        P(),
        P(),
        P("mp"),
        P("mp", "dp"),
    )
    return jax.shard_map(
        per_device, mesh=mesh, in_specs=placed, out_specs=P("dp", "mp"), check_vma=False
    )
```

```python
import math

import functools

import jax
import jax.numpy as jnp
from jax import lax
from jax.experimental import pallas as pl
from jax.experimental.pallas import tpu as pltpu
from jax.sharding import PartitionSpec as P

MESH = pl.DeviceIdType.MESH

F = 16
R = 16


EPSILON = 1e-05


def taylor(inputs):
    squares = (inputs[..., :, None] * inputs[..., None, :]).reshape(
        inputs.shape[:-1] + (inputs.shape[-1] * inputs.shape[-1],)
    )
    constant = jnp.ones(inputs.shape[:-1] + (1,), jnp.float32)
    return jnp.concatenate([constant, 0.5 * inputs, squares * (0.25 / math.sqrt(2.0))], axis=-1)


def request_of(bounds, positions):
    return jnp.sum((positions[:, None] >= bounds[None, :]).astype(jnp.int32), axis=1)


def token_tables(lengths, adapter_ids, positions):
    bounds = jnp.cumsum(lengths)
    request = request_of(bounds, positions)
    openings = bounds - lengths
    starts = jnp.any(positions[:, None] == openings[None, :], axis=1)
    picked = request[:, None] == jnp.arange(lengths.shape[0], dtype=jnp.int32)[None, :]
    adapter = jnp.sum(jnp.where(picked, adapter_ids[None, :], 0), axis=1)
    return (request, starts, adapter)


def block_local(query, key_rows, values, request, starts):
    scores = jnp.einsum("ihd,jhd->hij", query, key_rows, preferred_element_type=jnp.float32) * 0.25
    weights = 1.0 + scores + 0.5 * scores * scores
    indexes = jnp.arange(request.shape[0], dtype=jnp.int32)
    allowed = (indexes[None, :] <= indexes[:, None]) & (request[None, :] == request[:, None])
    weights = jnp.where(allowed[None], weights, 0.0).astype(jnp.bfloat16)
    within = jnp.einsum("hij,jhe->ihe", weights, values, preferred_element_type=jnp.float32)
    query_map = taylor(query.astype(jnp.float32)).astype(jnp.bfloat16)
    key_map = taylor(key_rows.astype(jnp.float32)).astype(jnp.bfloat16)
    tail_mask = (request == request[-1]).astype(jnp.bfloat16)
    masked_keys = key_map * tail_mask[:, None, None]
    summary = jnp.einsum("ihf,ihe->hfe", masked_keys, values, preferred_element_type=jnp.float32)
    return (within, query_map, summary)


def finish(within, query_map, carried, request, starts, gains):
    follows = ((request == request[0]) & jnp.logical_not(starts[0])).astype(jnp.float32)
    cross = jnp.einsum(
        "ihf,hfe->ihe", query_map, carried.astype(jnp.bfloat16), preferred_element_type=jnp.float32
    )
    combined = within + follows[:, None, None] * cross
    factor = lax.rsqrt(jnp.mean(combined * combined, axis=-1, keepdims=True) + EPSILON)
    return (combined * factor * gains[None]).astype(jnp.bfloat16)


def scan_masks(lengths, row_count, place, blocks, rounds):
    openings = jnp.cumsum(lengths) - lengths
    ids = jnp.arange(blocks, dtype=jnp.int32)
    firsts = ids * row_count
    inside = (openings[None, :] >= firsts[:, None]) & (openings[None, :] < firsts[:, None] + row_count)
    flags = jnp.any(inside, axis=1).astype(jnp.int32)
    spans = jnp.asarray([1 << (k // 2) for k in range(2 * rounds)], jnp.int32)
    tops = place - jnp.asarray([k % 2 for k in range(2 * rounds)], jnp.int32)
    lows = place - spans + 1
    covered = (ids[None, :] >= lows[:, None]) & (ids[None, :] <= tops[:, None])
    hits = jnp.sum(jnp.where(covered, flags[None, :], 0), axis=1)
    return (hits == 0).astype(jnp.float32)


def scan_kernel(n, rounds, s_ref, m_ref, e_ref, parts, recv, send_sem, recv_sem):
    me = lax.axis_index("dp")
    col = lax.axis_index("mp")
    barrier = pltpu.get_barrier_semaphore()
    for k in range(rounds):
        d = 1 << k

        @pl.when(me + d < n)
        def _():
            pl.semaphore_signal(barrier, 1, device_id=(me + d, col), device_id_type=MESH)

        @pl.when(me >= d)
        def _():
            pl.semaphore_signal(barrier, 1, device_id=(me - d, col), device_id_type=MESH)

    peers = 0
    for k in range(rounds):
        d = 1 << k
        peers = peers + (me // d + n - 1) // n + ((n - 1 - me) // d + n - 1) // n
    pl.semaphore_wait(barrier, peers)

    e_ref[...] = jnp.zeros_like(e_ref)
    copies = []
    for k in range(rounds):
        d = 1 << k
        src = s_ref if k == 0 else parts.at[k - 1]
        copy = pltpu.make_async_remote_copy(
            src_ref=src,
            dst_ref=recv.at[k],
            send_sem=send_sem.at[k],
            recv_sem=recv_sem.at[k],
            device_id=(me + d, col),
            device_id_type=MESH,
        )
        copies.append(copy)

        @pl.when(me + d < n)
        def _():
            copy.start()

        @pl.when(me >= d)
        def _():
            copy.wait_recv()
            got = recv[k].astype(jnp.float32)
            if k < rounds - 1:
                parts[k] = (src[...].astype(jnp.float32) + m_ref[2 * k] * got).astype(parts.dtype)
            e_ref[...] += m_ref[2 * k + 1] * got

        if k < rounds - 1:

            @pl.when(me < d)
            def _():
                parts[k] = src[...]

    for k in range(rounds):
        d = 1 << k

        @pl.when(me + d < n)
        def _():
            copies[k].wait_send()


def carried_scan(summary, masks, n, rounds):
    shape = summary.shape
    flat = summary.reshape(-1, shape[-1]).astype(jnp.bfloat16)
    size = flat.shape[0] * flat.shape[1]
    out = pl.pallas_call(
        functools.partial(scan_kernel, n, rounds),
        out_shape=jax.ShapeDtypeStruct(flat.shape, jnp.float32),
        in_specs=[
            pl.BlockSpec(memory_space=pltpu.VMEM),
            pl.BlockSpec(memory_space=pltpu.SMEM),
        ],
        out_specs=pl.BlockSpec(memory_space=pltpu.VMEM),
        scratch_shapes=[
            pltpu.VMEM((max(rounds - 1, 1),) + flat.shape, jnp.bfloat16),
            pltpu.VMEM((rounds,) + flat.shape, jnp.bfloat16),
            pltpu.SemaphoreType.DMA((rounds,)),
            pltpu.SemaphoreType.DMA((rounds,)),
        ],
        compiler_params=pltpu.CompilerParams(collective_id=0, has_side_effects=True),
        cost_estimate=pl.CostEstimate(
            flops=3 * rounds * size, bytes_accessed=6 * rounds * size, transcendentals=0
        ),
    )(flat, masks)
    return out.reshape(shape)


def gather_kernel(n, m, xd_ref, xm_ref, gd_ref, gm_ref, send_d, recv_d, send_x, recv_x, send_m, recv_m, own):
    me = lax.axis_index("dp")
    col = lax.axis_index("mp")
    chips = n // 2
    side = me % 2
    chip = me // 2
    mate = me + 1 - 2 * side
    barrier = pltpu.get_barrier_semaphore()

    def each(lo, hi, body):
        def step(k, carry):
            body(k)
            return carry

        lax.fori_loop(lo, hi, step, 0)

    each(1, chips, lambda k: pl.semaphore_signal(
        barrier, 1, device_id=((me + 2 * k) % n, col), device_id_type=MESH))
    pl.semaphore_signal(barrier, 1, device_id=(mate, col), device_id_type=MESH)
    each(1, m, lambda k: pl.semaphore_signal(
        barrier, 1, device_id=(me, (col + k) % m), device_id_type=MESH))
    pl.semaphore_wait(barrier, chips + m - 1)

    mine = pltpu.make_async_copy(xd_ref, gd_ref.at[side, chip], own)
    mine.start()

    def to_far(k):
        return pltpu.make_async_remote_copy(
            src_ref=xd_ref,
            dst_ref=gd_ref.at[side, chip],
            send_sem=send_d.at[k],
            recv_sem=recv_d.at[chip],
            device_id=((me + 2 * k) % n, col),
            device_id_type=MESH,
        )

    def from_far(k):
        other = (chip + chips - k) % chips
        return pltpu.make_async_remote_copy(
            src_ref=xd_ref,
            dst_ref=gd_ref.at[side, other],
            send_sem=send_d.at[k],
            recv_sem=recv_d.at[other],
            device_id=(2 * other + side, col),
            device_id_type=MESH,
        )

    swap_out = pltpu.make_async_remote_copy(
        src_ref=gd_ref.at[side],
        dst_ref=gd_ref.at[side],
        send_sem=send_x,
        recv_sem=recv_x,
        device_id=(mate, col),
        device_id_type=MESH,
    )
    swap_in = pltpu.make_async_remote_copy(
        src_ref=gd_ref.at[1 - side],
        dst_ref=gd_ref.at[1 - side],
        send_sem=send_x,
        recv_sem=recv_x,
        device_id=(mate, col),
        device_id_type=MESH,
    )

    def to_mp(k):
        return pltpu.make_async_remote_copy(
            src_ref=xm_ref,
            dst_ref=gm_ref.at[col],
            send_sem=send_m.at[k],
            recv_sem=recv_m.at[col],
            device_id=(me, (col + k) % m),
            device_id_type=MESH,
        )

    def from_mp(k):
        other = (col + m - k) % m
        return pltpu.make_async_remote_copy(
            src_ref=xm_ref,
            dst_ref=gm_ref.at[other],
            send_sem=send_m.at[k],
            recv_sem=recv_m.at[other],
            device_id=(me, other),
            device_id_type=MESH,
        )

    each(1, chips, lambda k: to_far(k).start())
    each(1, m, lambda k: to_mp(k).start())
    gm_ref[col] = xm_ref[...]
    each(1, chips, lambda k: from_far(k).wait_recv())
    mine.wait()
    swap_out.start()
    each(1, m, lambda k: from_mp(k).wait_recv())
    swap_in.wait_recv()
    each(1, chips, lambda k: to_far(k).wait_send())
    swap_out.wait_send()
    each(1, m, lambda k: to_mp(k).wait_send())


def direct_gather(xd, xm, n, m):
    moved = n * xd.size * 2 + m * xm.size * 2
    gd, gm = pl.pallas_call(
        functools.partial(gather_kernel, n, m),
        out_shape=(
            jax.ShapeDtypeStruct((2, n // 2) + xd.shape, xd.dtype),
            jax.ShapeDtypeStruct((m,) + xm.shape, xm.dtype),
        ),
        in_specs=[pl.BlockSpec(memory_space=pltpu.VMEM)] * 2,
        out_specs=(pl.BlockSpec(memory_space=pltpu.VMEM), pl.BlockSpec(memory_space=pltpu.VMEM)),
        scratch_shapes=[
            pltpu.SemaphoreType.DMA((n // 2,)),
            pltpu.SemaphoreType.DMA((n // 2,)),
            pltpu.SemaphoreType.DMA(()),
            pltpu.SemaphoreType.DMA(()),
            pltpu.SemaphoreType.DMA((m,)),
            pltpu.SemaphoreType.DMA((m,)),
            pltpu.SemaphoreType.DMA(()),
        ],
        compiler_params=pltpu.CompilerParams(collective_id=1, has_side_effects=True),
        cost_estimate=pl.CostEstimate(flops=0, bytes_accessed=moved, transcendentals=0),
    )(xd, xm)
    return jnp.transpose(gd, (1, 0, 2, 3)), gm


def ring_kernel(m, x_ref, o_ref, acc_a, acc_b, got_a, got_b, send_a, recv_a, send_b, recv_b):
    me = lax.axis_index("dp")
    col = lax.axis_index("mp")
    right = (col + 1) % m
    left = (col + m - 1) % m
    width = o_ref.shape[1]
    half = width // 2
    barrier = pltpu.get_barrier_semaphore()
    pl.semaphore_signal(barrier, 1, device_id=(me, right), device_id_type=MESH)
    pl.semaphore_signal(barrier, 1, device_id=(me, left), device_id_type=MESH)
    pl.semaphore_wait(barrier, 2)

    def piece(t, side):
        return pl.ds(pl.multiple_of(t * width + side * half, half), half)

    copies = []
    for s in range(m - 1):
        ta = (col + 2 * m - 1 - s) % m
        tb = (col + 1 + s) % m
        if s == 0:
            src_a = x_ref.at[:, piece(ta, 0)]
            src_b = x_ref.at[:, piece(tb, 1)]
        else:
            copies[-1][0].wait_recv()
            copies[-1][1].wait_recv()
            acc_a[s - 1] = (
                got_a[s - 1].astype(jnp.float32) + x_ref[:, piece(ta, 0)].astype(jnp.float32)
            ).astype(acc_a.dtype)
            acc_b[s - 1] = (
                got_b[s - 1].astype(jnp.float32) + x_ref[:, piece(tb, 1)].astype(jnp.float32)
            ).astype(acc_b.dtype)
            src_a = acc_a.at[s - 1]
            src_b = acc_b.at[s - 1]
        ca = pltpu.make_async_remote_copy(
            src_ref=src_a,
            dst_ref=got_a.at[s],
            send_sem=send_a.at[s],
            recv_sem=recv_a.at[s],
            device_id=(me, right),
            device_id_type=MESH,
        )
        cb = pltpu.make_async_remote_copy(
            src_ref=src_b,
            dst_ref=got_b.at[s],
            send_sem=send_b.at[s],
            recv_sem=recv_b.at[s],
            device_id=(me, left),
            device_id_type=MESH,
        )
        ca.start()
        cb.start()
        copies.append((ca, cb))
    copies[-1][0].wait_recv()
    copies[-1][1].wait_recv()
    last = m - 2
    o_ref[:, :half] = (
        got_a[last].astype(jnp.float32) + x_ref[:, piece(col, 0)].astype(jnp.float32)
    ).astype(o_ref.dtype)
    o_ref[:, half:] = (
        got_b[last].astype(jnp.float32) + x_ref[:, piece(col, 1)].astype(jnp.float32)
    ).astype(o_ref.dtype)
    for ca, cb in copies:
        ca.wait_send()
        cb.wait_send()


def ring_scatter(x, m):
    rows, total = x.shape
    width = total // m
    half = width // 2
    slot = (m - 1, rows, half)
    return pl.pallas_call(
        functools.partial(ring_kernel, m),
        out_shape=jax.ShapeDtypeStruct((rows, width), x.dtype),
        in_specs=[pl.BlockSpec(memory_space=pltpu.VMEM)],
        out_specs=pl.BlockSpec(memory_space=pltpu.VMEM),
        scratch_shapes=[
            pltpu.VMEM(slot, x.dtype),
            pltpu.VMEM(slot, x.dtype),
            pltpu.VMEM(slot, x.dtype),
            pltpu.VMEM(slot, x.dtype),
            pltpu.SemaphoreType.DMA((m - 1,)),
            pltpu.SemaphoreType.DMA((m - 1,)),
            pltpu.SemaphoreType.DMA((m - 1,)),
            pltpu.SemaphoreType.DMA((m - 1,)),
        ],
        compiler_params=pltpu.CompilerParams(collective_id=2, has_side_effects=True),
        cost_estimate=pl.CostEstimate(
            flops=2 * rows * total, bytes_accessed=4 * rows * total, transcendentals=0
        ),
    )(x)


def per_device(
    tokens,
    q_weight,
    k_weight,
    v_weight,
    adapter_down,
    adapter_up,
    lengths,
    adapter_ids,
    head_gain,
    out_weight,
):
    row_count = tokens.shape[0]
    qf = q_weight.shape[1]
    heads_here = qf // F
    vw = v_weight.shape[1]
    value_width = vw // heads_here
    blocks = lax.axis_size("dp")
    place = lax.axis_index("dp")
    positions = place * row_count + jnp.arange(row_count, dtype=jnp.int32)
    request, starts, adapter = token_tables(lengths, adapter_ids, positions)

    local = jnp.concatenate([q_weight, k_weight, v_weight], axis=1)
    out_t = lax.all_gather(out_weight.T, "dp", axis=0, tiled=True)
    part_low = jnp.dot(tokens, adapter_down, preferred_element_type=jnp.float32)
    owners = lax.axis_index("mp") * (adapter_down.shape[1] // R) + (
        jnp.arange(adapter_down.shape[1], dtype=jnp.int32) // R
    )
    part_low = jnp.where(adapter[:, None] == owners[None, :], part_low, 0.0).astype(jnp.bfloat16)
    cols = lax.axis_size("mp")
    gathered, low_parts = direct_gather(local, part_low, blocks, cols)
    gathered = gathered.reshape(blocks * local.shape[0], local.shape[1])
    q_full = gathered[:, :qf]
    k_full = gathered[:, qf : 2 * qf]
    v_full = gathered[:, 2 * qf :]
    low_rank = jnp.transpose(low_parts, (1, 0, 2)).reshape(row_count, cols * part_low.shape[1])

    query_sum = jnp.dot(tokens, q_full, preferred_element_type=jnp.float32)
    key_sum = jnp.dot(tokens, k_full, preferred_element_type=jnp.float32)
    value_sum = jnp.dot(tokens, v_full, preferred_element_type=jnp.float32)
    query = query_sum.astype(jnp.bfloat16).reshape(row_count, heads_here, F)
    key_rows = key_sum.astype(jnp.bfloat16).reshape(row_count, heads_here, F)
    values = value_sum + jnp.dot(low_rank, adapter_up, preferred_element_type=jnp.float32)
    values = values.astype(jnp.bfloat16).reshape(row_count, heads_here, value_width)
    within, query_map, summary = block_local(query, key_rows, values, request, starts)

    rounds = max(1, (blocks - 1).bit_length())
    masks = scan_masks(lengths, row_count, place, blocks, rounds)
    carried = carried_scan(summary, masks, blocks, rounds)

    gains = head_gain.reshape(heads_here, value_width)
    normed = finish(within, query_map, carried, request, starts, gains).reshape(
        row_count, heads_here * value_width
    )
    partial_terms = lax.dot_general(
        normed, out_t, (((1,), (1,)), ((), ())), preferred_element_type=jnp.float32
    )
    return ring_scatter(partial_terms.astype(jnp.bfloat16), cols)


def solution(mesh):
    placed = (
        P("dp", None),
        P("dp", "mp"),
        P("dp", "mp"),
        P("dp", "mp"),
        P(None, "mp"),
        P(None, "mp"),
        P(),
        P(),
        P("mp"),
        P("mp", "dp"),
    )
    return jax.shard_map(
        per_device, mesh=mesh, in_specs=placed, out_specs=P("dp", "mp"), check_vma=False
    )
```

```python
import math

import functools

import jax
import jax.numpy as jnp
from jax import lax
from jax.experimental import pallas as pl
from jax.experimental.pallas import tpu as pltpu
from jax.sharding import PartitionSpec as P

MESH = pl.DeviceIdType.MESH

F = 16
R = 16


EPSILON = 1e-05


def taylor(inputs):
    squares = (inputs[..., :, None] * inputs[..., None, :]).reshape(
        inputs.shape[:-1] + (inputs.shape[-1] * inputs.shape[-1],)
    )
    constant = jnp.ones(inputs.shape[:-1] + (1,), jnp.float32)
    return jnp.concatenate([constant, 0.5 * inputs, squares * (0.25 / math.sqrt(2.0))], axis=-1)


def request_of(bounds, positions):
    return jnp.sum((positions[:, None] >= bounds[None, :]).astype(jnp.int32), axis=1)


def token_tables(lengths, adapter_ids, positions):
    bounds = jnp.cumsum(lengths)
    request = request_of(bounds, positions)
    openings = bounds - lengths
    starts = jnp.any(positions[:, None] == openings[None, :], axis=1)
    picked = request[:, None] == jnp.arange(lengths.shape[0], dtype=jnp.int32)[None, :]
    adapter = jnp.sum(jnp.where(picked, adapter_ids[None, :], 0), axis=1)
    return (request, starts, adapter)


def block_local(query, key_rows, values, request, starts):
    scores = jnp.einsum("ihd,jhd->hij", query, key_rows, preferred_element_type=jnp.float32) * 0.25
    weights = 1.0 + scores + 0.5 * scores * scores
    indexes = jnp.arange(request.shape[0], dtype=jnp.int32)
    allowed = (indexes[None, :] <= indexes[:, None]) & (request[None, :] == request[:, None])
    weights = jnp.where(allowed[None], weights, 0.0).astype(jnp.bfloat16)
    within = jnp.einsum("hij,jhe->ihe", weights, values, preferred_element_type=jnp.float32)
    query_map = taylor(query.astype(jnp.float32)).astype(jnp.bfloat16)
    key_map = taylor(key_rows.astype(jnp.float32)).astype(jnp.bfloat16)
    tail_mask = (request == request[-1]).astype(jnp.bfloat16)
    masked_keys = key_map * tail_mask[:, None, None]
    summary = jnp.einsum("ihf,ihe->hfe", masked_keys, values, preferred_element_type=jnp.float32)
    return (within, query_map, summary)


def finish(within, query_map, carried, request, starts, gains):
    follows = ((request == request[0]) & jnp.logical_not(starts[0])).astype(jnp.float32)
    cross = jnp.einsum(
        "ihf,hfe->ihe", query_map, carried.astype(jnp.bfloat16), preferred_element_type=jnp.float32
    )
    combined = within + follows[:, None, None] * cross
    factor = lax.rsqrt(jnp.mean(combined * combined, axis=-1, keepdims=True) + EPSILON)
    return (combined * factor * gains[None]).astype(jnp.bfloat16)


def scan_masks(lengths, row_count, place, blocks, rounds):
    openings = jnp.cumsum(lengths) - lengths
    ids = jnp.arange(blocks, dtype=jnp.int32)
    firsts = ids * row_count
    inside = (openings[None, :] >= firsts[:, None]) & (openings[None, :] < firsts[:, None] + row_count)
    flags = jnp.any(inside, axis=1).astype(jnp.int32)
    spans = jnp.asarray([1 << (k // 2) for k in range(2 * rounds)], jnp.int32)
    tops = place - jnp.asarray([k % 2 for k in range(2 * rounds)], jnp.int32)
    lows = place - spans + 1
    covered = (ids[None, :] >= lows[:, None]) & (ids[None, :] <= tops[:, None])
    hits = jnp.sum(jnp.where(covered, flags[None, :], 0), axis=1)
    return (hits == 0).astype(jnp.float32)


def scan_kernel(n, rounds, s_ref, m_ref, xo_ref, e_ref, go_ref, parts, recv, send_sem, recv_sem,
                send_o, recv_o, send_x, recv_x, own):
    me = lax.axis_index("dp")
    col = lax.axis_index("mp")
    chips = n // 2
    side = me % 2
    chip = me // 2
    mate = me + 1 - 2 * side
    barrier = pltpu.get_barrier_semaphore()

    def each(lo, hi, body):
        def step(k, carry):
            body(k)
            return carry

        lax.fori_loop(lo, hi, step, 0)

    each(1, chips, lambda k: pl.semaphore_signal(
        barrier, 1, device_id=((me + 2 * k) % n, col), device_id_type=MESH))
    pl.semaphore_signal(barrier, 1, device_id=(mate, col), device_id_type=MESH)
    for k in range(rounds):
        d = 1 << k

        @pl.when(me + d < n)
        def _():
            pl.semaphore_signal(barrier, 1, device_id=(me + d, col), device_id_type=MESH)

        @pl.when(me >= d)
        def _():
            pl.semaphore_signal(barrier, 1, device_id=(me - d, col), device_id_type=MESH)

    peers = 0
    for k in range(rounds):
        d = 1 << k
        peers = peers + (me // d + n - 1) // n + ((n - 1 - me) // d + n - 1) // n
    pl.semaphore_wait(barrier, peers + chips)

    mine = pltpu.make_async_copy(xo_ref, go_ref.at[side, chip], own)
    mine.start()

    def to_far(k):
        return pltpu.make_async_remote_copy(
            src_ref=xo_ref,
            dst_ref=go_ref.at[side, chip],
            send_sem=send_o.at[k],
            recv_sem=recv_o.at[chip],
            device_id=((me + 2 * k) % n, col),
            device_id_type=MESH,
        )

    def from_far(k):
        other = (chip + chips - k) % chips
        return pltpu.make_async_remote_copy(
            src_ref=xo_ref,
            dst_ref=go_ref.at[side, other],
            send_sem=send_o.at[k],
            recv_sem=recv_o.at[other],
            device_id=(2 * other + side, col),
            device_id_type=MESH,
        )

    swap_out = pltpu.make_async_remote_copy(
        src_ref=go_ref.at[side],
        dst_ref=go_ref.at[side],
        send_sem=send_x,
        recv_sem=recv_x,
        device_id=(mate, col),
        device_id_type=MESH,
    )
    swap_in = pltpu.make_async_remote_copy(
        src_ref=go_ref.at[1 - side],
        dst_ref=go_ref.at[1 - side],
        send_sem=send_x,
        recv_sem=recv_x,
        device_id=(mate, col),
        device_id_type=MESH,
    )
    each(1, chips, lambda k: to_far(k).start())

    e_ref[...] = jnp.zeros_like(e_ref)
    copies = []
    for k in range(rounds):
        d = 1 << k
        src = s_ref if k == 0 else parts.at[k - 1]
        copy = pltpu.make_async_remote_copy(
            src_ref=src,
            dst_ref=recv.at[k],
            send_sem=send_sem.at[k],
            recv_sem=recv_sem.at[k],
            device_id=(me + d, col),
            device_id_type=MESH,
        )
        copies.append(copy)

        @pl.when(me + d < n)
        def _():
            copy.start()

        @pl.when(me >= d)
        def _():
            copy.wait_recv()
            got = recv[k].astype(jnp.float32)
            if k < rounds - 1:
                parts[k] = (src[...].astype(jnp.float32) + m_ref[2 * k] * got).astype(parts.dtype)
            e_ref[...] += m_ref[2 * k + 1] * got

        if k < rounds - 1:

            @pl.when(me < d)
            def _():
                parts[k] = src[...]

    each(1, chips, lambda k: from_far(k).wait_recv())
    mine.wait()
    swap_out.start()
    swap_in.wait_recv()
    each(1, chips, lambda k: to_far(k).wait_send())
    swap_out.wait_send()

    for k in range(rounds):
        d = 1 << k

        @pl.when(me + d < n)
        def _():
            copies[k].wait_send()


def carried_scan(summary, masks, piece, n, rounds):
    shape = summary.shape
    flat = summary.reshape(-1, shape[-1]).astype(jnp.bfloat16)
    size = flat.shape[0] * flat.shape[1]
    out, gathered = pl.pallas_call(
        functools.partial(scan_kernel, n, rounds),
        out_shape=(
            jax.ShapeDtypeStruct(flat.shape, jnp.float32),
            jax.ShapeDtypeStruct((2, n // 2) + piece.shape, piece.dtype),
        ),
        in_specs=[
            pl.BlockSpec(memory_space=pltpu.VMEM),
            pl.BlockSpec(memory_space=pltpu.SMEM),
            pl.BlockSpec(memory_space=pltpu.VMEM),
        ],
        out_specs=(pl.BlockSpec(memory_space=pltpu.VMEM), pl.BlockSpec(memory_space=pltpu.VMEM)),
        scratch_shapes=[
            pltpu.VMEM((max(rounds - 1, 1),) + flat.shape, jnp.bfloat16),
            pltpu.VMEM((rounds,) + flat.shape, jnp.bfloat16),
            pltpu.SemaphoreType.DMA((rounds,)),
            pltpu.SemaphoreType.DMA((rounds,)),
            pltpu.SemaphoreType.DMA((n // 2,)),
            pltpu.SemaphoreType.DMA((n // 2,)),
            pltpu.SemaphoreType.DMA(()),
            pltpu.SemaphoreType.DMA(()),
            pltpu.SemaphoreType.DMA(()),
        ],
        compiler_params=pltpu.CompilerParams(collective_id=0, has_side_effects=True),
        cost_estimate=pl.CostEstimate(
            flops=3 * rounds * size,
            bytes_accessed=6 * rounds * size + 2 * n * piece.size,
            transcendentals=0,
        ),
    )(flat, masks, piece)
    gathered = jnp.transpose(gathered, (1, 0, 2, 3)).reshape(n * piece.shape[0], piece.shape[1])
    return out.reshape(shape), gathered


def gather_kernel(n, m, xd_ref, xm_ref, gd_ref, gm_ref, send_d, recv_d, send_x, recv_x, send_m, recv_m, own):
    me = lax.axis_index("dp")
    col = lax.axis_index("mp")
    chips = n // 2
    side = me % 2
    chip = me // 2
    mate = me + 1 - 2 * side
    barrier = pltpu.get_barrier_semaphore()

    def each(lo, hi, body):
        def step(k, carry):
            body(k)
            return carry

        lax.fori_loop(lo, hi, step, 0)

    each(1, chips, lambda k: pl.semaphore_signal(
        barrier, 1, device_id=((me + 2 * k) % n, col), device_id_type=MESH))
    pl.semaphore_signal(barrier, 1, device_id=(mate, col), device_id_type=MESH)
    each(1, m, lambda k: pl.semaphore_signal(
        barrier, 1, device_id=(me, (col + k) % m), device_id_type=MESH))
    pl.semaphore_wait(barrier, chips + m - 1)

    mine = pltpu.make_async_copy(xd_ref, gd_ref.at[side, chip], own)
    mine.start()

    def to_far(k):
        return pltpu.make_async_remote_copy(
            src_ref=xd_ref,
            dst_ref=gd_ref.at[side, chip],
            send_sem=send_d.at[k],
            recv_sem=recv_d.at[chip],
            device_id=((me + 2 * k) % n, col),
            device_id_type=MESH,
        )

    def from_far(k):
        other = (chip + chips - k) % chips
        return pltpu.make_async_remote_copy(
            src_ref=xd_ref,
            dst_ref=gd_ref.at[side, other],
            send_sem=send_d.at[k],
            recv_sem=recv_d.at[other],
            device_id=(2 * other + side, col),
            device_id_type=MESH,
        )

    swap_out = pltpu.make_async_remote_copy(
        src_ref=gd_ref.at[side],
        dst_ref=gd_ref.at[side],
        send_sem=send_x,
        recv_sem=recv_x,
        device_id=(mate, col),
        device_id_type=MESH,
    )
    swap_in = pltpu.make_async_remote_copy(
        src_ref=gd_ref.at[1 - side],
        dst_ref=gd_ref.at[1 - side],
        send_sem=send_x,
        recv_sem=recv_x,
        device_id=(mate, col),
        device_id_type=MESH,
    )

    def to_mp(k):
        return pltpu.make_async_remote_copy(
            src_ref=xm_ref,
            dst_ref=gm_ref.at[col],
            send_sem=send_m.at[k],
            recv_sem=recv_m.at[col],
            device_id=(me, (col + k) % m),
            device_id_type=MESH,
        )

    def from_mp(k):
        other = (col + m - k) % m
        return pltpu.make_async_remote_copy(
            src_ref=xm_ref,
            dst_ref=gm_ref.at[other],
            send_sem=send_m.at[k],
            recv_sem=recv_m.at[other],
            device_id=(me, other),
            device_id_type=MESH,
        )

    each(1, chips, lambda k: to_far(k).start())
    each(1, m, lambda k: to_mp(k).start())
    gm_ref[col] = xm_ref[...]
    each(1, chips, lambda k: from_far(k).wait_recv())
    mine.wait()
    swap_out.start()
    each(1, m, lambda k: from_mp(k).wait_recv())
    swap_in.wait_recv()
    each(1, chips, lambda k: to_far(k).wait_send())
    swap_out.wait_send()
    each(1, m, lambda k: to_mp(k).wait_send())


def direct_gather(xd, xm, n, m):
    moved = n * xd.size * 2 + m * xm.size * 2
    gd, gm = pl.pallas_call(
        functools.partial(gather_kernel, n, m),
        out_shape=(
            jax.ShapeDtypeStruct((2, n // 2) + xd.shape, xd.dtype),
            jax.ShapeDtypeStruct((m,) + xm.shape, xm.dtype),
        ),
        in_specs=[pl.BlockSpec(memory_space=pltpu.VMEM)] * 2,
        out_specs=(pl.BlockSpec(memory_space=pltpu.VMEM), pl.BlockSpec(memory_space=pltpu.VMEM)),
        scratch_shapes=[
            pltpu.SemaphoreType.DMA((n // 2,)),
            pltpu.SemaphoreType.DMA((n // 2,)),
            pltpu.SemaphoreType.DMA(()),
            pltpu.SemaphoreType.DMA(()),
            pltpu.SemaphoreType.DMA((m,)),
            pltpu.SemaphoreType.DMA((m,)),
            pltpu.SemaphoreType.DMA(()),
        ],
        compiler_params=pltpu.CompilerParams(collective_id=1, has_side_effects=True),
        cost_estimate=pl.CostEstimate(flops=0, bytes_accessed=moved, transcendentals=0),
    )(xd, xm)
    return jnp.transpose(gd, (1, 0, 2, 3)), gm


def ring_kernel(m, x_ref, o_ref, acc_a, acc_b, got_a, got_b, send_a, recv_a, send_b, recv_b):
    me = lax.axis_index("dp")
    col = lax.axis_index("mp")
    right = (col + 1) % m
    left = (col + m - 1) % m
    width = o_ref.shape[1]
    half = width // 2
    barrier = pltpu.get_barrier_semaphore()
    pl.semaphore_signal(barrier, 1, device_id=(me, right), device_id_type=MESH)
    pl.semaphore_signal(barrier, 1, device_id=(me, left), device_id_type=MESH)
    pl.semaphore_wait(barrier, 2)

    def piece(t, side):
        return pl.ds(pl.multiple_of(t * width + side * half, half), half)

    copies = []
    for s in range(m - 1):
        ta = (col + 2 * m - 1 - s) % m
        tb = (col + 1 + s) % m
        if s == 0:
            src_a = x_ref.at[:, piece(ta, 0)]
            src_b = x_ref.at[:, piece(tb, 1)]
        else:
            copies[-1][0].wait_recv()
            copies[-1][1].wait_recv()
            acc_a[s - 1] = (
                got_a[s - 1].astype(jnp.float32) + x_ref[:, piece(ta, 0)].astype(jnp.float32)
            ).astype(acc_a.dtype)
            acc_b[s - 1] = (
                got_b[s - 1].astype(jnp.float32) + x_ref[:, piece(tb, 1)].astype(jnp.float32)
            ).astype(acc_b.dtype)
            src_a = acc_a.at[s - 1]
            src_b = acc_b.at[s - 1]
        ca = pltpu.make_async_remote_copy(
            src_ref=src_a,
            dst_ref=got_a.at[s],
            send_sem=send_a.at[s],
            recv_sem=recv_a.at[s],
            device_id=(me, right),
            device_id_type=MESH,
        )
        cb = pltpu.make_async_remote_copy(
            src_ref=src_b,
            dst_ref=got_b.at[s],
            send_sem=send_b.at[s],
            recv_sem=recv_b.at[s],
            device_id=(me, left),
            device_id_type=MESH,
        )
        ca.start()
        cb.start()
        copies.append((ca, cb))
    copies[-1][0].wait_recv()
    copies[-1][1].wait_recv()
    last = m - 2
    o_ref[:, :half] = (
        got_a[last].astype(jnp.float32) + x_ref[:, piece(col, 0)].astype(jnp.float32)
    ).astype(o_ref.dtype)
    o_ref[:, half:] = (
        got_b[last].astype(jnp.float32) + x_ref[:, piece(col, 1)].astype(jnp.float32)
    ).astype(o_ref.dtype)
    for ca, cb in copies:
        ca.wait_send()
        cb.wait_send()


def ring_scatter(x, m):
    rows, total = x.shape
    width = total // m
    half = width // 2
    slot = (m - 1, rows, half)
    return pl.pallas_call(
        functools.partial(ring_kernel, m),
        out_shape=jax.ShapeDtypeStruct((rows, width), x.dtype),
        in_specs=[pl.BlockSpec(memory_space=pltpu.VMEM)],
        out_specs=pl.BlockSpec(memory_space=pltpu.VMEM),
        scratch_shapes=[
            pltpu.VMEM(slot, x.dtype),
            pltpu.VMEM(slot, x.dtype),
            pltpu.VMEM(slot, x.dtype),
            pltpu.VMEM(slot, x.dtype),
            pltpu.SemaphoreType.DMA((m - 1,)),
            pltpu.SemaphoreType.DMA((m - 1,)),
            pltpu.SemaphoreType.DMA((m - 1,)),
            pltpu.SemaphoreType.DMA((m - 1,)),
        ],
        compiler_params=pltpu.CompilerParams(collective_id=2, has_side_effects=True),
        cost_estimate=pl.CostEstimate(
            flops=2 * rows * total, bytes_accessed=4 * rows * total, transcendentals=0
        ),
    )(x)


def per_device(
    tokens,
    q_weight,
    k_weight,
    v_weight,
    adapter_down,
    adapter_up,
    lengths,
    adapter_ids,
    head_gain,
    out_weight,
):
    row_count = tokens.shape[0]
    qf = q_weight.shape[1]
    heads_here = qf // F
    vw = v_weight.shape[1]
    value_width = vw // heads_here
    blocks = lax.axis_size("dp")
    place = lax.axis_index("dp")
    positions = place * row_count + jnp.arange(row_count, dtype=jnp.int32)
    request, starts, adapter = token_tables(lengths, adapter_ids, positions)

    local = jnp.concatenate([q_weight, k_weight, v_weight], axis=1)
    part_low = jnp.dot(tokens, adapter_down, preferred_element_type=jnp.float32)
    owners = lax.axis_index("mp") * (adapter_down.shape[1] // R) + (
        jnp.arange(adapter_down.shape[1], dtype=jnp.int32) // R
    )
    part_low = jnp.where(adapter[:, None] == owners[None, :], part_low, 0.0).astype(jnp.bfloat16)
    cols = lax.axis_size("mp")
    gathered, low_parts = direct_gather(local, part_low, blocks, cols)
    gathered = gathered.reshape(blocks * local.shape[0], local.shape[1])
    q_full = gathered[:, :qf]
    k_full = gathered[:, qf : 2 * qf]
    v_full = gathered[:, 2 * qf :]
    low_rank = jnp.transpose(low_parts, (1, 0, 2)).reshape(row_count, cols * part_low.shape[1])

    query_sum = jnp.dot(tokens, q_full, preferred_element_type=jnp.float32)
    key_sum = jnp.dot(tokens, k_full, preferred_element_type=jnp.float32)
    value_sum = jnp.dot(tokens, v_full, preferred_element_type=jnp.float32)
    query = query_sum.astype(jnp.bfloat16).reshape(row_count, heads_here, F)
    key_rows = key_sum.astype(jnp.bfloat16).reshape(row_count, heads_here, F)
    values = value_sum + jnp.dot(low_rank, adapter_up, preferred_element_type=jnp.float32)
    values = values.astype(jnp.bfloat16).reshape(row_count, heads_here, value_width)
    within, query_map, summary = block_local(query, key_rows, values, request, starts)

    rounds = max(1, (blocks - 1).bit_length())
    masks = scan_masks(lengths, row_count, place, blocks, rounds)
    carried, out_t = carried_scan(summary, masks, out_weight.T, blocks, rounds)

    gains = head_gain.reshape(heads_here, value_width)
    normed = finish(within, query_map, carried, request, starts, gains).reshape(
        row_count, heads_here * value_width
    )
    partial_terms = lax.dot_general(
        normed, out_t, (((1,), (1,)), ((), ())), preferred_element_type=jnp.float32
    )
    return ring_scatter(partial_terms.astype(jnp.bfloat16), cols)


def solution(mesh):
    placed = (
        P("dp", None),
        P("dp", "mp"),
        P("dp", "mp"),
        P("dp", "mp"),
        P(None, "mp"),
        P(None, "mp"),
        P(),
        P(),
        P("mp"),
        P("mp", "dp"),
    )
    return jax.shard_map(
        per_device, mesh=mesh, in_specs=placed, out_specs=P("dp", "mp"), check_vma=False
    )
```

```python
import math

import functools

import jax
import jax.numpy as jnp
import numpy as np
from jax import lax
from jax.experimental import pallas as pl
from jax.experimental.pallas import tpu as pltpu
from jax.sharding import PartitionSpec as P

MESH = pl.DeviceIdType.MESH

F = 16
R = 16


EPSILON = 1e-05


def taylor(inputs):
    squares = (inputs[..., :, None] * inputs[..., None, :]).reshape(
        inputs.shape[:-1] + (inputs.shape[-1] * inputs.shape[-1],)
    )
    constant = jnp.ones(inputs.shape[:-1] + (1,), jnp.float32)
    return jnp.concatenate([constant, 0.5 * inputs, squares * (0.25 / math.sqrt(2.0))], axis=-1)


def packed_features(width):
    index, weight = list(range(1 + width)), [1.0] * (1 + width)
    for a in range(width):
        for b in range(a, width):
            index.append(1 + width + a * width + b)
            weight.append(1.0 if a == b else 2.0)
    return np.asarray(index, np.int32), np.asarray(weight, np.float32)


def request_of(bounds, positions):
    return jnp.sum((positions[:, None] >= bounds[None, :]).astype(jnp.int32), axis=1)


def token_tables(lengths, adapter_ids, positions):
    bounds = jnp.cumsum(lengths)
    request = request_of(bounds, positions)
    openings = bounds - lengths
    starts = jnp.any(positions[:, None] == openings[None, :], axis=1)
    picked = request[:, None] == jnp.arange(lengths.shape[0], dtype=jnp.int32)[None, :]
    adapter = jnp.sum(jnp.where(picked, adapter_ids[None, :], 0), axis=1)
    return (request, starts, adapter)


def block_local(query, key_rows, values, request, starts):
    scores = jnp.einsum("ihd,jhd->hij", query, key_rows, preferred_element_type=jnp.float32) * 0.25
    weights = 1.0 + scores + 0.5 * scores * scores
    indexes = jnp.arange(request.shape[0], dtype=jnp.int32)
    allowed = (indexes[None, :] <= indexes[:, None]) & (request[None, :] == request[:, None])
    weights = jnp.where(allowed[None], weights, 0.0).astype(jnp.bfloat16)
    within = jnp.einsum("hij,jhe->ihe", weights, values, preferred_element_type=jnp.float32)
    index, weight = packed_features(query.shape[-1])
    query_map = taylor(query.astype(jnp.float32)).astype(jnp.bfloat16)
    query_map = query_map[..., index] * jnp.asarray(weight, jnp.bfloat16)
    key_map = taylor(key_rows.astype(jnp.float32)).astype(jnp.bfloat16)[..., index]
    tail_mask = (request == request[-1]).astype(jnp.bfloat16)
    masked_keys = key_map * tail_mask[:, None, None]
    summary = jnp.einsum("ihf,ihe->hfe", masked_keys, values, preferred_element_type=jnp.float32)
    return (within, query_map, summary)


def finish(within, query_map, carried, request, starts, gains):
    follows = ((request == request[0]) & jnp.logical_not(starts[0])).astype(jnp.float32)
    cross = jnp.einsum(
        "ihf,hfe->ihe", query_map, carried.astype(jnp.bfloat16), preferred_element_type=jnp.float32
    )
    combined = within + follows[:, None, None] * cross
    factor = lax.rsqrt(jnp.mean(combined * combined, axis=-1, keepdims=True) + EPSILON)
    return (combined * factor * gains[None]).astype(jnp.bfloat16)


def scan_masks(lengths, row_count, place, blocks, rounds):
    openings = jnp.cumsum(lengths) - lengths
    ids = jnp.arange(blocks, dtype=jnp.int32)
    firsts = ids * row_count
    inside = (openings[None, :] >= firsts[:, None]) & (openings[None, :] < firsts[:, None] + row_count)
    flags = jnp.any(inside, axis=1).astype(jnp.int32)
    spans = jnp.asarray([1 << (k // 2) for k in range(2 * rounds)], jnp.int32)
    tops = place - jnp.asarray([k % 2 for k in range(2 * rounds)], jnp.int32)
    lows = place - spans + 1
    covered = (ids[None, :] >= lows[:, None]) & (ids[None, :] <= tops[:, None])
    hits = jnp.sum(jnp.where(covered, flags[None, :], 0), axis=1)
    return (hits == 0).astype(jnp.float32)


def scan_kernel(n, rounds, s_ref, m_ref, xo_ref, e_ref, go_ref, parts, recv, send_sem, recv_sem,
                send_o, recv_o, send_x, recv_x, own):
    me = lax.axis_index("dp")
    col = lax.axis_index("mp")
    chips = n // 2
    side = me % 2
    chip = me // 2
    mate = me + 1 - 2 * side
    barrier = pltpu.get_barrier_semaphore()

    def each(lo, hi, body):
        def step(k, carry):
            body(k)
            return carry

        lax.fori_loop(lo, hi, step, 0)

    each(1, chips, lambda k: pl.semaphore_signal(
        barrier, 1, device_id=((me + 2 * k) % n, col), device_id_type=MESH))
    pl.semaphore_signal(barrier, 1, device_id=(mate, col), device_id_type=MESH)
    for k in range(rounds):
        d = 1 << k

        @pl.when(me + d < n)
        def _():
            pl.semaphore_signal(barrier, 1, device_id=(me + d, col), device_id_type=MESH)

        @pl.when(me >= d)
        def _():
            pl.semaphore_signal(barrier, 1, device_id=(me - d, col), device_id_type=MESH)

    peers = 0
    for k in range(rounds):
        d = 1 << k
        peers = peers + (me // d + n - 1) // n + ((n - 1 - me) // d + n - 1) // n
    pl.semaphore_wait(barrier, peers + chips)

    mine = pltpu.make_async_copy(xo_ref, go_ref.at[side, chip], own)
    mine.start()

    def to_far(k):
        return pltpu.make_async_remote_copy(
            src_ref=xo_ref,
            dst_ref=go_ref.at[side, chip],
            send_sem=send_o.at[k],
            recv_sem=recv_o.at[chip],
            device_id=((me + 2 * k) % n, col),
            device_id_type=MESH,
        )

    def from_far(k):
        other = (chip + chips - k) % chips
        return pltpu.make_async_remote_copy(
            src_ref=xo_ref,
            dst_ref=go_ref.at[side, other],
            send_sem=send_o.at[k],
            recv_sem=recv_o.at[other],
            device_id=(2 * other + side, col),
            device_id_type=MESH,
        )

    swap_out = pltpu.make_async_remote_copy(
        src_ref=go_ref.at[side],
        dst_ref=go_ref.at[side],
        send_sem=send_x,
        recv_sem=recv_x,
        device_id=(mate, col),
        device_id_type=MESH,
    )
    swap_in = pltpu.make_async_remote_copy(
        src_ref=go_ref.at[1 - side],
        dst_ref=go_ref.at[1 - side],
        send_sem=send_x,
        recv_sem=recv_x,
        device_id=(mate, col),
        device_id_type=MESH,
    )
    each(1, chips, lambda k: to_far(k).start())

    e_ref[...] = jnp.zeros_like(e_ref)
    copies = []
    for k in range(rounds):
        d = 1 << k
        src = s_ref if k == 0 else parts.at[k - 1]
        copy = pltpu.make_async_remote_copy(
            src_ref=src,
            dst_ref=recv.at[k],
            send_sem=send_sem.at[k],
            recv_sem=recv_sem.at[k],
            device_id=(me + d, col),
            device_id_type=MESH,
        )
        copies.append(copy)

        @pl.when(me + d < n)
        def _():
            copy.start()

        @pl.when(me >= d)
        def _():
            copy.wait_recv()
            got = recv[k].astype(jnp.float32)
            if k < rounds - 1:
                parts[k] = (src[...].astype(jnp.float32) + m_ref[2 * k] * got).astype(parts.dtype)
            e_ref[...] += m_ref[2 * k + 1] * got

        if k < rounds - 1:

            @pl.when(me < d)
            def _():
                parts[k] = src[...]

    each(1, chips, lambda k: from_far(k).wait_recv())
    mine.wait()
    swap_out.start()
    swap_in.wait_recv()
    each(1, chips, lambda k: to_far(k).wait_send())
    swap_out.wait_send()

    for k in range(rounds):
        d = 1 << k

        @pl.when(me + d < n)
        def _():
            copies[k].wait_send()


def carried_scan(summary, masks, piece, n, rounds):
    shape = summary.shape
    flat = summary.reshape(-1, shape[-1]).astype(jnp.bfloat16)
    size = flat.shape[0] * flat.shape[1]
    out, gathered = pl.pallas_call(
        functools.partial(scan_kernel, n, rounds),
        out_shape=(
            jax.ShapeDtypeStruct(flat.shape, jnp.float32),
            jax.ShapeDtypeStruct((2, n // 2) + piece.shape, piece.dtype),
        ),
        in_specs=[
            pl.BlockSpec(memory_space=pltpu.VMEM),
            pl.BlockSpec(memory_space=pltpu.SMEM),
            pl.BlockSpec(memory_space=pltpu.VMEM),
        ],
        out_specs=(pl.BlockSpec(memory_space=pltpu.VMEM), pl.BlockSpec(memory_space=pltpu.VMEM)),
        scratch_shapes=[
            pltpu.VMEM((max(rounds - 1, 1),) + flat.shape, jnp.bfloat16),
            pltpu.VMEM((rounds,) + flat.shape, jnp.bfloat16),
            pltpu.SemaphoreType.DMA((rounds,)),
            pltpu.SemaphoreType.DMA((rounds,)),
            pltpu.SemaphoreType.DMA((n // 2,)),
            pltpu.SemaphoreType.DMA((n // 2,)),
            pltpu.SemaphoreType.DMA(()),
            pltpu.SemaphoreType.DMA(()),
            pltpu.SemaphoreType.DMA(()),
        ],
        compiler_params=pltpu.CompilerParams(collective_id=0, has_side_effects=True),
        cost_estimate=pl.CostEstimate(
            flops=3 * rounds * size,
            bytes_accessed=6 * rounds * size + 2 * n * piece.size,
            transcendentals=0,
        ),
    )(flat, masks, piece)
    gathered = jnp.transpose(gathered, (1, 0, 2, 3)).reshape(n * piece.shape[0], piece.shape[1])
    return out.reshape(shape), gathered


def gather_kernel(n, m, xd_ref, xm_ref, gd_ref, gm_ref, send_d, recv_d, send_x, recv_x, send_m, recv_m, own):
    me = lax.axis_index("dp")
    col = lax.axis_index("mp")
    chips = n // 2
    side = me % 2
    chip = me // 2
    mate = me + 1 - 2 * side
    barrier = pltpu.get_barrier_semaphore()

    def each(lo, hi, body):
        def step(k, carry):
            body(k)
            return carry

        lax.fori_loop(lo, hi, step, 0)

    each(1, chips, lambda k: pl.semaphore_signal(
        barrier, 1, device_id=((me + 2 * k) % n, col), device_id_type=MESH))
    pl.semaphore_signal(barrier, 1, device_id=(mate, col), device_id_type=MESH)
    each(1, m, lambda k: pl.semaphore_signal(
        barrier, 1, device_id=(me, (col + k) % m), device_id_type=MESH))
    pl.semaphore_wait(barrier, chips + m - 1)

    mine = pltpu.make_async_copy(xd_ref, gd_ref.at[side, chip], own)
    mine.start()

    def to_far(k):
        return pltpu.make_async_remote_copy(
            src_ref=xd_ref,
            dst_ref=gd_ref.at[side, chip],
            send_sem=send_d.at[k],
            recv_sem=recv_d.at[chip],
            device_id=((me + 2 * k) % n, col),
            device_id_type=MESH,
        )

    def from_far(k):
        other = (chip + chips - k) % chips
        return pltpu.make_async_remote_copy(
            src_ref=xd_ref,
            dst_ref=gd_ref.at[side, other],
            send_sem=send_d.at[k],
            recv_sem=recv_d.at[other],
            device_id=(2 * other + side, col),
            device_id_type=MESH,
        )

    swap_out = pltpu.make_async_remote_copy(
        src_ref=gd_ref.at[side],
        dst_ref=gd_ref.at[side],
        send_sem=send_x,
        recv_sem=recv_x,
        device_id=(mate, col),
        device_id_type=MESH,
    )
    swap_in = pltpu.make_async_remote_copy(
        src_ref=gd_ref.at[1 - side],
        dst_ref=gd_ref.at[1 - side],
        send_sem=send_x,
        recv_sem=recv_x,
        device_id=(mate, col),
        device_id_type=MESH,
    )

    def to_mp(k):
        return pltpu.make_async_remote_copy(
            src_ref=xm_ref,
            dst_ref=gm_ref.at[col],
            send_sem=send_m.at[k],
            recv_sem=recv_m.at[col],
            device_id=(me, (col + k) % m),
            device_id_type=MESH,
        )

    def from_mp(k):
        other = (col + m - k) % m
        return pltpu.make_async_remote_copy(
            src_ref=xm_ref,
            dst_ref=gm_ref.at[other],
            send_sem=send_m.at[k],
            recv_sem=recv_m.at[other],
            device_id=(me, other),
            device_id_type=MESH,
        )

    each(1, chips, lambda k: to_far(k).start())
    each(1, m, lambda k: to_mp(k).start())
    gm_ref[col] = xm_ref[...]
    each(1, chips, lambda k: from_far(k).wait_recv())
    mine.wait()
    swap_out.start()
    each(1, m, lambda k: from_mp(k).wait_recv())
    swap_in.wait_recv()
    each(1, chips, lambda k: to_far(k).wait_send())
    swap_out.wait_send()
    each(1, m, lambda k: to_mp(k).wait_send())


def direct_gather(xd, xm, n, m):
    moved = n * xd.size * 2 + m * xm.size * 2
    gd, gm = pl.pallas_call(
        functools.partial(gather_kernel, n, m),
        out_shape=(
            jax.ShapeDtypeStruct((2, n // 2) + xd.shape, xd.dtype),
            jax.ShapeDtypeStruct((m,) + xm.shape, xm.dtype),
        ),
        in_specs=[pl.BlockSpec(memory_space=pltpu.VMEM)] * 2,
        out_specs=(pl.BlockSpec(memory_space=pltpu.VMEM), pl.BlockSpec(memory_space=pltpu.VMEM)),
        scratch_shapes=[
            pltpu.SemaphoreType.DMA((n // 2,)),
            pltpu.SemaphoreType.DMA((n // 2,)),
            pltpu.SemaphoreType.DMA(()),
            pltpu.SemaphoreType.DMA(()),
            pltpu.SemaphoreType.DMA((m,)),
            pltpu.SemaphoreType.DMA((m,)),
            pltpu.SemaphoreType.DMA(()),
        ],
        compiler_params=pltpu.CompilerParams(collective_id=1, has_side_effects=True),
        cost_estimate=pl.CostEstimate(flops=0, bytes_accessed=moved, transcendentals=0),
    )(xd, xm)
    return jnp.transpose(gd, (1, 0, 2, 3)), gm


def ring_kernel(m, x_ref, o_ref, acc_a, acc_b, got_a, got_b, send_a, recv_a, send_b, recv_b):
    me = lax.axis_index("dp")
    col = lax.axis_index("mp")
    right = (col + 1) % m
    left = (col + m - 1) % m
    width = o_ref.shape[1]
    half = width // 2
    barrier = pltpu.get_barrier_semaphore()
    pl.semaphore_signal(barrier, 1, device_id=(me, right), device_id_type=MESH)
    pl.semaphore_signal(barrier, 1, device_id=(me, left), device_id_type=MESH)
    pl.semaphore_wait(barrier, 2)

    def piece(t, side):
        return pl.ds(pl.multiple_of(t * width + side * half, half), half)

    copies = []
    for s in range(m - 1):
        ta = (col + 2 * m - 1 - s) % m
        tb = (col + 1 + s) % m
        if s == 0:
            src_a = x_ref.at[:, piece(ta, 0)]
            src_b = x_ref.at[:, piece(tb, 1)]
        else:
            copies[-1][0].wait_recv()
            copies[-1][1].wait_recv()
            acc_a[s - 1] = (
                got_a[s - 1].astype(jnp.float32) + x_ref[:, piece(ta, 0)].astype(jnp.float32)
            ).astype(acc_a.dtype)
            acc_b[s - 1] = (
                got_b[s - 1].astype(jnp.float32) + x_ref[:, piece(tb, 1)].astype(jnp.float32)
            ).astype(acc_b.dtype)
            src_a = acc_a.at[s - 1]
            src_b = acc_b.at[s - 1]
        ca = pltpu.make_async_remote_copy(
            src_ref=src_a,
            dst_ref=got_a.at[s],
            send_sem=send_a.at[s],
            recv_sem=recv_a.at[s],
            device_id=(me, right),
            device_id_type=MESH,
        )
        cb = pltpu.make_async_remote_copy(
            src_ref=src_b,
            dst_ref=got_b.at[s],
            send_sem=send_b.at[s],
            recv_sem=recv_b.at[s],
            device_id=(me, left),
            device_id_type=MESH,
        )
        ca.start()
        cb.start()
        copies.append((ca, cb))
    copies[-1][0].wait_recv()
    copies[-1][1].wait_recv()
    last = m - 2
    o_ref[:, :half] = (
        got_a[last].astype(jnp.float32) + x_ref[:, piece(col, 0)].astype(jnp.float32)
    ).astype(o_ref.dtype)
    o_ref[:, half:] = (
        got_b[last].astype(jnp.float32) + x_ref[:, piece(col, 1)].astype(jnp.float32)
    ).astype(o_ref.dtype)
    for ca, cb in copies:
        ca.wait_send()
        cb.wait_send()


def ring_scatter(x, m):
    rows, total = x.shape
    width = total // m
    half = width // 2
    slot = (m - 1, rows, half)
    return pl.pallas_call(
        functools.partial(ring_kernel, m),
        out_shape=jax.ShapeDtypeStruct((rows, width), x.dtype),
        in_specs=[pl.BlockSpec(memory_space=pltpu.VMEM)],
        out_specs=pl.BlockSpec(memory_space=pltpu.VMEM),
        scratch_shapes=[
            pltpu.VMEM(slot, x.dtype),
            pltpu.VMEM(slot, x.dtype),
            pltpu.VMEM(slot, x.dtype),
            pltpu.VMEM(slot, x.dtype),
            pltpu.SemaphoreType.DMA((m - 1,)),
            pltpu.SemaphoreType.DMA((m - 1,)),
            pltpu.SemaphoreType.DMA((m - 1,)),
            pltpu.SemaphoreType.DMA((m - 1,)),
        ],
        compiler_params=pltpu.CompilerParams(collective_id=2, has_side_effects=True),
        cost_estimate=pl.CostEstimate(
            flops=2 * rows * total, bytes_accessed=4 * rows * total, transcendentals=0
        ),
    )(x)


def per_device(
    tokens,
    q_weight,
    k_weight,
    v_weight,
    adapter_down,
    adapter_up,
    lengths,
    adapter_ids,
    head_gain,
    out_weight,
):
    row_count = tokens.shape[0]
    qf = q_weight.shape[1]
    heads_here = qf // F
    vw = v_weight.shape[1]
    value_width = vw // heads_here
    blocks = lax.axis_size("dp")
    place = lax.axis_index("dp")
    positions = place * row_count + jnp.arange(row_count, dtype=jnp.int32)
    request, starts, adapter = token_tables(lengths, adapter_ids, positions)

    local = jnp.concatenate([q_weight, k_weight, v_weight], axis=1)
    part_low = jnp.dot(tokens, adapter_down, preferred_element_type=jnp.float32)
    owners = lax.axis_index("mp") * (adapter_down.shape[1] // R) + (
        jnp.arange(adapter_down.shape[1], dtype=jnp.int32) // R
    )
    part_low = jnp.where(adapter[:, None] == owners[None, :], part_low, 0.0).astype(jnp.bfloat16)
    cols = lax.axis_size("mp")
    gathered, low_parts = direct_gather(local, part_low, blocks, cols)
    gathered = gathered.reshape(blocks * local.shape[0], local.shape[1])
    q_full = gathered[:, :qf]
    k_full = gathered[:, qf : 2 * qf]
    v_full = gathered[:, 2 * qf :]
    low_rank = jnp.transpose(low_parts, (1, 0, 2)).reshape(row_count, cols * part_low.shape[1])

    query_sum = jnp.dot(tokens, q_full, preferred_element_type=jnp.float32)
    key_sum = jnp.dot(tokens, k_full, preferred_element_type=jnp.float32)
    value_sum = jnp.dot(tokens, v_full, preferred_element_type=jnp.float32)
    query = query_sum.astype(jnp.bfloat16).reshape(row_count, heads_here, F)
    key_rows = key_sum.astype(jnp.bfloat16).reshape(row_count, heads_here, F)
    values = value_sum + jnp.dot(low_rank, adapter_up, preferred_element_type=jnp.float32)
    values = values.astype(jnp.bfloat16).reshape(row_count, heads_here, value_width)
    within, query_map, summary = block_local(query, key_rows, values, request, starts)

    rounds = max(1, (blocks - 1).bit_length())
    masks = scan_masks(lengths, row_count, place, blocks, rounds)
    carried, out_t = carried_scan(summary, masks, out_weight.T, blocks, rounds)

    gains = head_gain.reshape(heads_here, value_width)
    normed = finish(within, query_map, carried, request, starts, gains).reshape(
        row_count, heads_here * value_width
    )
    partial_terms = lax.dot_general(
        normed, out_t, (((1,), (1,)), ((), ())), preferred_element_type=jnp.float32
    )
    return ring_scatter(partial_terms.astype(jnp.bfloat16), cols)


def solution(mesh):
    placed = (
        P("dp", None),
        P("dp", "mp"),
        P("dp", "mp"),
        P("dp", "mp"),
        P(None, "mp"),
        P(None, "mp"),
        P(),
        P(),
        P("mp"),
        P("mp", "dp"),
    )
    return jax.shard_map(
        per_device, mesh=mesh, in_specs=placed, out_specs=P("dp", "mp"), check_vma=False
    )
```

```python
import math

import functools

import jax
import jax.numpy as jnp
import numpy as np
from jax import lax
from jax.experimental import pallas as pl
from jax.experimental.pallas import tpu as pltpu
from jax.sharding import PartitionSpec as P

MESH = pl.DeviceIdType.MESH

F = 16
R = 16


EPSILON = 1e-05


def taylor(inputs):
    squares = (inputs[..., :, None] * inputs[..., None, :]).reshape(
        inputs.shape[:-1] + (inputs.shape[-1] * inputs.shape[-1],)
    )
    constant = jnp.ones(inputs.shape[:-1] + (1,), jnp.float32)
    return jnp.concatenate([constant, 0.5 * inputs, squares * (0.25 / math.sqrt(2.0))], axis=-1)


def packed_features(width):
    index, weight = list(range(1 + width)), [1.0] * (1 + width)
    for a in range(width):
        for b in range(a, width):
            index.append(1 + width + a * width + b)
            weight.append(1.0 if a == b else 2.0)
    return np.asarray(index, np.int32), np.asarray(weight, np.float32)


def request_of(bounds, positions):
    return jnp.sum((positions[:, None] >= bounds[None, :]).astype(jnp.int32), axis=1)


def token_tables(lengths, adapter_ids, positions):
    bounds = jnp.cumsum(lengths)
    request = request_of(bounds, positions)
    openings = bounds - lengths
    starts = jnp.any(positions[:, None] == openings[None, :], axis=1)
    picked = request[:, None] == jnp.arange(lengths.shape[0], dtype=jnp.int32)[None, :]
    adapter = jnp.sum(jnp.where(picked, adapter_ids[None, :], 0), axis=1)
    return (request, starts, adapter)


def block_local(query, key_rows, values, request, starts):
    scores = jnp.einsum("ihd,jhd->hij", query, key_rows, preferred_element_type=jnp.float32) * 0.25
    weights = 1.0 + scores + 0.5 * scores * scores
    indexes = jnp.arange(request.shape[0], dtype=jnp.int32)
    allowed = (indexes[None, :] <= indexes[:, None]) & (request[None, :] == request[:, None])
    weights = jnp.where(allowed[None], weights, 0.0).astype(jnp.bfloat16)
    within = jnp.einsum("hij,jhe->ihe", weights, values, preferred_element_type=jnp.float32)
    index, weight = packed_features(query.shape[-1])
    query_map = taylor(query.astype(jnp.float32)).astype(jnp.bfloat16)
    query_map = query_map[..., index] * jnp.asarray(weight, jnp.bfloat16)
    key_map = taylor(key_rows.astype(jnp.float32)).astype(jnp.bfloat16)[..., index]
    tail_mask = (request == request[-1]).astype(jnp.bfloat16)
    masked_keys = key_map * tail_mask[:, None, None]
    summary = jnp.einsum("ihf,ihe->hfe", masked_keys, values, preferred_element_type=jnp.float32)
    return (within, query_map, summary)


def finish(within, query_map, carried, request, starts, gains):
    follows = ((request == request[0]) & jnp.logical_not(starts[0])).astype(jnp.float32)
    cross = jnp.einsum(
        "ihf,hfe->ihe", query_map, carried.astype(jnp.bfloat16), preferred_element_type=jnp.float32
    )
    combined = within + follows[:, None, None] * cross
    factor = lax.rsqrt(jnp.mean(combined * combined, axis=-1, keepdims=True) + EPSILON)
    return (combined * factor * gains[None]).astype(jnp.bfloat16)


def scan_masks(lengths, row_count, place, blocks, rounds):
    openings = jnp.cumsum(lengths) - lengths
    ids = jnp.arange(blocks, dtype=jnp.int32)
    firsts = ids * row_count
    inside = (openings[None, :] >= firsts[:, None]) & (openings[None, :] < firsts[:, None] + row_count)
    flags = jnp.any(inside, axis=1).astype(jnp.int32)
    spans = jnp.asarray([1 << (k // 2) for k in range(2 * rounds)], jnp.int32)
    tops = place - jnp.asarray([k % 2 for k in range(2 * rounds)], jnp.int32)
    lows = place - spans + 1
    covered = (ids[None, :] >= lows[:, None]) & (ids[None, :] <= tops[:, None])
    hits = jnp.sum(jnp.where(covered, flags[None, :], 0), axis=1)
    return (hits == 0).astype(jnp.float32)


def scan_kernel(n, rounds, s_ref, m_ref, xo_ref, e_ref, go_ref, parts, recv, send_sem, recv_sem,
                send_o, recv_o, send_x, recv_x, own):
    me = lax.axis_index("dp")
    col = lax.axis_index("mp")
    chips = n // 2
    side = me % 2
    chip = me // 2
    mate = me + 1 - 2 * side
    barrier = pltpu.get_barrier_semaphore()

    def each(lo, hi, body):
        def step(k, carry):
            body(k)
            return carry

        lax.fori_loop(lo, hi, step, 0)

    each(1, chips, lambda k: pl.semaphore_signal(
        barrier, 1, device_id=((me + 2 * k) % n, col), device_id_type=MESH))
    pl.semaphore_signal(barrier, 1, device_id=(mate, col), device_id_type=MESH)
    for k in range(rounds):
        d = 1 << k

        @pl.when(me + d < n)
        def _():
            pl.semaphore_signal(barrier, 1, device_id=(me + d, col), device_id_type=MESH)

        @pl.when(me >= d)
        def _():
            pl.semaphore_signal(barrier, 1, device_id=(me - d, col), device_id_type=MESH)

    peers = 0
    for k in range(rounds):
        d = 1 << k
        peers = peers + (me // d + n - 1) // n + ((n - 1 - me) // d + n - 1) // n
    pl.semaphore_wait(barrier, peers + chips)

    mine = pltpu.make_async_copy(xo_ref, go_ref.at[side, chip], own)
    mine.start()

    def to_far(k):
        return pltpu.make_async_remote_copy(
            src_ref=xo_ref,
            dst_ref=go_ref.at[side, chip],
            send_sem=send_o.at[k],
            recv_sem=recv_o.at[chip],
            device_id=((me + 2 * k) % n, col),
            device_id_type=MESH,
        )

    def from_far(k):
        other = (chip + chips - k) % chips
        return pltpu.make_async_remote_copy(
            src_ref=xo_ref,
            dst_ref=go_ref.at[side, other],
            send_sem=send_o.at[k],
            recv_sem=recv_o.at[other],
            device_id=(2 * other + side, col),
            device_id_type=MESH,
        )

    swap_out = pltpu.make_async_remote_copy(
        src_ref=go_ref.at[side],
        dst_ref=go_ref.at[side],
        send_sem=send_x,
        recv_sem=recv_x,
        device_id=(mate, col),
        device_id_type=MESH,
    )
    swap_in = pltpu.make_async_remote_copy(
        src_ref=go_ref.at[1 - side],
        dst_ref=go_ref.at[1 - side],
        send_sem=send_x,
        recv_sem=recv_x,
        device_id=(mate, col),
        device_id_type=MESH,
    )
    each(1, chips, lambda k: to_far(k).start())

    e_ref[...] = jnp.zeros_like(e_ref)
    copies = []
    for k in range(rounds):
        d = 1 << k
        src = s_ref if k == 0 else parts.at[k - 1]
        copy = pltpu.make_async_remote_copy(
            src_ref=src,
            dst_ref=recv.at[k],
            send_sem=send_sem.at[k],
            recv_sem=recv_sem.at[k],
            device_id=(me + d, col),
            device_id_type=MESH,
        )
        copies.append(copy)

        @pl.when(me + d < n)
        def _():
            copy.start()

        @pl.when(me >= d)
        def _():
            copy.wait_recv()
            got = recv[k].astype(jnp.float32)
            if k < rounds - 1:
                parts[k] = (src[...].astype(jnp.float32) + m_ref[2 * k] * got).astype(parts.dtype)
            e_ref[...] += m_ref[2 * k + 1] * got

        if k < rounds - 1:

            @pl.when(me < d)
            def _():
                parts[k] = src[...]

    each(1, chips, lambda k: from_far(k).wait_recv())
    mine.wait()
    swap_out.start()
    swap_in.wait_recv()
    each(1, chips, lambda k: to_far(k).wait_send())
    swap_out.wait_send()

    for k in range(rounds):
        d = 1 << k

        @pl.when(me + d < n)
        def _():
            copies[k].wait_send()


def carried_scan(summary, masks, piece, n, rounds):
    shape = summary.shape
    flat = summary.reshape(-1, shape[-1]).astype(jnp.bfloat16)
    size = flat.shape[0] * flat.shape[1]
    out, gathered = pl.pallas_call(
        functools.partial(scan_kernel, n, rounds),
        out_shape=(
            jax.ShapeDtypeStruct(flat.shape, jnp.float32),
            jax.ShapeDtypeStruct((2, n // 2) + piece.shape, piece.dtype),
        ),
        in_specs=[
            pl.BlockSpec(memory_space=pltpu.VMEM),
            pl.BlockSpec(memory_space=pltpu.SMEM),
            pl.BlockSpec(memory_space=pltpu.VMEM),
        ],
        out_specs=(pl.BlockSpec(memory_space=pltpu.VMEM), pl.BlockSpec(memory_space=pltpu.VMEM)),
        scratch_shapes=[
            pltpu.VMEM((max(rounds - 1, 1),) + flat.shape, jnp.bfloat16),
            pltpu.VMEM((rounds,) + flat.shape, jnp.bfloat16),
            pltpu.SemaphoreType.DMA((rounds,)),
            pltpu.SemaphoreType.DMA((rounds,)),
            pltpu.SemaphoreType.DMA((n // 2,)),
            pltpu.SemaphoreType.DMA((n // 2,)),
            pltpu.SemaphoreType.DMA(()),
            pltpu.SemaphoreType.DMA(()),
            pltpu.SemaphoreType.DMA(()),
        ],
        compiler_params=pltpu.CompilerParams(collective_id=0, has_side_effects=True),
        cost_estimate=pl.CostEstimate(
            flops=3 * rounds * size,
            bytes_accessed=6 * rounds * size + 2 * n * piece.size,
            transcendentals=0,
        ),
    )(flat, masks, piece)
    gathered = jnp.transpose(gathered, (1, 0, 2, 3)).reshape(n * piece.shape[0], piece.shape[1])
    return out.reshape(shape), gathered


def gather_kernel(n, m, xd_ref, xm_ref, early_ref, gd_ref, gm_ref, send_d, recv_d, send_x, recv_x, send_m, recv_m, own):
    me = lax.axis_index("dp")
    col = lax.axis_index("mp")
    chips = n // 2
    side = me % 2
    chip = me // 2
    mate = me + 1 - 2 * side
    barrier = pltpu.get_barrier_semaphore()

    def each(lo, hi, body):
        def step(k, carry):
            body(k)
            return carry

        lax.fori_loop(lo, hi, step, 0)

    each(1, chips, lambda k: pl.semaphore_signal(
        barrier, 1, device_id=((me + 2 * k) % n, col), device_id_type=MESH))
    pl.semaphore_signal(barrier, 1, device_id=(mate, col), device_id_type=MESH)
    each(1, m, lambda k: pl.semaphore_signal(
        barrier, 1, device_id=(me, (col + k) % m), device_id_type=MESH))
    pl.semaphore_wait(barrier, chips + m - 1)

    mine = pltpu.make_async_copy(xd_ref, gd_ref.at[side, chip], own)
    mine.start()

    def to_far(k):
        return pltpu.make_async_remote_copy(
            src_ref=xd_ref,
            dst_ref=gd_ref.at[side, chip],
            send_sem=send_d.at[k],
            recv_sem=recv_d.at[chip],
            device_id=((me + 2 * k) % n, col),
            device_id_type=MESH,
        )

    def from_far(k):
        other = (chip + chips - k) % chips
        return pltpu.make_async_remote_copy(
            src_ref=xd_ref,
            dst_ref=gd_ref.at[side, other],
            send_sem=send_d.at[k],
            recv_sem=recv_d.at[other],
            device_id=(2 * other + side, col),
            device_id_type=MESH,
        )

    swap_out = pltpu.make_async_remote_copy(
        src_ref=gd_ref.at[side],
        dst_ref=gd_ref.at[side],
        send_sem=send_x,
        recv_sem=recv_x,
        device_id=(mate, col),
        device_id_type=MESH,
    )
    swap_in = pltpu.make_async_remote_copy(
        src_ref=gd_ref.at[1 - side],
        dst_ref=gd_ref.at[1 - side],
        send_sem=send_x,
        recv_sem=recv_x,
        device_id=(mate, col),
        device_id_type=MESH,
    )

    def to_mp(k):
        return pltpu.make_async_remote_copy(
            src_ref=xm_ref,
            dst_ref=gm_ref.at[col],
            send_sem=send_m.at[k],
            recv_sem=recv_m.at[col],
            device_id=(me, (col + k) % m),
            device_id_type=MESH,
        )

    def from_mp(k):
        other = (col + m - k) % m
        return pltpu.make_async_remote_copy(
            src_ref=xm_ref,
            dst_ref=gm_ref.at[other],
            send_sem=send_m.at[k],
            recv_sem=recv_m.at[other],
            device_id=(me, other),
            device_id_type=MESH,
        )

    each(1, chips, lambda k: to_far(k).start())
    each(1, m, lambda k: to_mp(k).start())
    gm_ref[col] = xm_ref[...]
    each(1, chips, lambda k: from_far(k).wait_recv())
    mine.wait()
    swap_out.start()
    each(1, m, lambda k: from_mp(k).wait_recv())
    swap_in.wait_recv()
    each(1, chips, lambda k: to_far(k).wait_send())
    swap_out.wait_send()
    each(1, m, lambda k: to_mp(k).wait_send())


def direct_gather(xd, xm, early, n, m):
    moved = n * xd.size * 2 + m * xm.size * 2
    gd, gm = pl.pallas_call(
        functools.partial(gather_kernel, n, m),
        out_shape=(
            jax.ShapeDtypeStruct((2, n // 2) + xd.shape, xd.dtype),
            jax.ShapeDtypeStruct((m,) + xm.shape, xm.dtype),
        ),
        in_specs=[pl.BlockSpec(memory_space=pltpu.VMEM)] * 2 + [pl.BlockSpec(memory_space=pltpu.SMEM)],
        out_specs=(pl.BlockSpec(memory_space=pltpu.VMEM), pl.BlockSpec(memory_space=pltpu.VMEM)),
        scratch_shapes=[
            pltpu.SemaphoreType.DMA((n // 2,)),
            pltpu.SemaphoreType.DMA((n // 2,)),
            pltpu.SemaphoreType.DMA(()),
            pltpu.SemaphoreType.DMA(()),
            pltpu.SemaphoreType.DMA((m,)),
            pltpu.SemaphoreType.DMA((m,)),
            pltpu.SemaphoreType.DMA(()),
        ],
        compiler_params=pltpu.CompilerParams(collective_id=1, has_side_effects=True),
        cost_estimate=pl.CostEstimate(flops=0, bytes_accessed=moved, transcendentals=0),
    )(xd, xm, early)
    return jnp.transpose(gd, (1, 0, 2, 3)), gm


def ring_kernel(m, x_ref, o_ref, acc_a, acc_b, got_a, got_b, send_a, recv_a, send_b, recv_b):
    me = lax.axis_index("dp")
    col = lax.axis_index("mp")
    right = (col + 1) % m
    left = (col + m - 1) % m
    width = o_ref.shape[1]
    half = width // 2
    barrier = pltpu.get_barrier_semaphore()
    pl.semaphore_signal(barrier, 1, device_id=(me, right), device_id_type=MESH)
    pl.semaphore_signal(barrier, 1, device_id=(me, left), device_id_type=MESH)
    pl.semaphore_wait(barrier, 2)

    def piece(t, side):
        return pl.ds(pl.multiple_of(t * width + side * half, half), half)

    copies = []
    for s in range(m - 1):
        ta = (col + 2 * m - 1 - s) % m
        tb = (col + 1 + s) % m
        if s == 0:
            src_a = x_ref.at[:, piece(ta, 0)]
            src_b = x_ref.at[:, piece(tb, 1)]
        else:
            copies[-1][0].wait_recv()
            copies[-1][1].wait_recv()
            acc_a[s - 1] = (
                got_a[s - 1].astype(jnp.float32) + x_ref[:, piece(ta, 0)].astype(jnp.float32)
            ).astype(acc_a.dtype)
            acc_b[s - 1] = (
                got_b[s - 1].astype(jnp.float32) + x_ref[:, piece(tb, 1)].astype(jnp.float32)
            ).astype(acc_b.dtype)
            src_a = acc_a.at[s - 1]
            src_b = acc_b.at[s - 1]
        ca = pltpu.make_async_remote_copy(
            src_ref=src_a,
            dst_ref=got_a.at[s],
            send_sem=send_a.at[s],
            recv_sem=recv_a.at[s],
            device_id=(me, right),
            device_id_type=MESH,
        )
        cb = pltpu.make_async_remote_copy(
            src_ref=src_b,
            dst_ref=got_b.at[s],
            send_sem=send_b.at[s],
            recv_sem=recv_b.at[s],
            device_id=(me, left),
            device_id_type=MESH,
        )
        ca.start()
        cb.start()
        copies.append((ca, cb))
    copies[-1][0].wait_recv()
    copies[-1][1].wait_recv()
    last = m - 2
    o_ref[:, :half] = (
        got_a[last].astype(jnp.float32) + x_ref[:, piece(col, 0)].astype(jnp.float32)
    ).astype(o_ref.dtype)
    o_ref[:, half:] = (
        got_b[last].astype(jnp.float32) + x_ref[:, piece(col, 1)].astype(jnp.float32)
    ).astype(o_ref.dtype)
    for ca, cb in copies:
        ca.wait_send()
        cb.wait_send()


def ring_scatter(x, m):
    rows, total = x.shape
    width = total // m
    half = width // 2
    slot = (m - 1, rows, half)
    return pl.pallas_call(
        functools.partial(ring_kernel, m),
        out_shape=jax.ShapeDtypeStruct((rows, width), x.dtype),
        in_specs=[pl.BlockSpec(memory_space=pltpu.VMEM)],
        out_specs=pl.BlockSpec(memory_space=pltpu.VMEM),
        scratch_shapes=[
            pltpu.VMEM(slot, x.dtype),
            pltpu.VMEM(slot, x.dtype),
            pltpu.VMEM(slot, x.dtype),
            pltpu.VMEM(slot, x.dtype),
            pltpu.SemaphoreType.DMA((m - 1,)),
            pltpu.SemaphoreType.DMA((m - 1,)),
            pltpu.SemaphoreType.DMA((m - 1,)),
            pltpu.SemaphoreType.DMA((m - 1,)),
        ],
        compiler_params=pltpu.CompilerParams(collective_id=2, has_side_effects=True),
        cost_estimate=pl.CostEstimate(
            flops=2 * rows * total, bytes_accessed=4 * rows * total, transcendentals=0
        ),
    )(x)


def per_device(
    tokens,
    q_weight,
    k_weight,
    v_weight,
    adapter_down,
    adapter_up,
    lengths,
    adapter_ids,
    head_gain,
    out_weight,
):
    row_count = tokens.shape[0]
    qf = q_weight.shape[1]
    heads_here = qf // F
    vw = v_weight.shape[1]
    value_width = vw // heads_here
    blocks = lax.axis_size("dp")
    place = lax.axis_index("dp")
    positions = place * row_count + jnp.arange(row_count, dtype=jnp.int32)
    request, starts, adapter = token_tables(lengths, adapter_ids, positions)

    local = jnp.concatenate([q_weight, k_weight, v_weight], axis=1)
    part_low = jnp.dot(tokens, adapter_down, preferred_element_type=jnp.float32)
    owners = lax.axis_index("mp") * (adapter_down.shape[1] // R) + (
        jnp.arange(adapter_down.shape[1], dtype=jnp.int32) // R
    )
    part_low = jnp.where(adapter[:, None] == owners[None, :], part_low, 0.0).astype(jnp.bfloat16)
    cols = lax.axis_size("mp")
    rounds = max(1, (blocks - 1).bit_length())
    masks = scan_masks(lengths, row_count, place, blocks, rounds)
    gathered, low_parts = direct_gather(local, part_low, masks, blocks, cols)
    gathered = gathered.reshape(blocks * local.shape[0], local.shape[1])
    q_full = gathered[:, :qf]
    k_full = gathered[:, qf : 2 * qf]
    v_full = gathered[:, 2 * qf :]
    low_rank = jnp.transpose(low_parts, (1, 0, 2)).reshape(row_count, cols * part_low.shape[1])

    query_sum = jnp.dot(tokens, q_full, preferred_element_type=jnp.float32)
    key_sum = jnp.dot(tokens, k_full, preferred_element_type=jnp.float32)
    value_sum = jnp.dot(tokens, v_full, preferred_element_type=jnp.float32)
    query = query_sum.astype(jnp.bfloat16).reshape(row_count, heads_here, F)
    key_rows = key_sum.astype(jnp.bfloat16).reshape(row_count, heads_here, F)
    values = value_sum + jnp.dot(low_rank, adapter_up, preferred_element_type=jnp.float32)
    values = values.astype(jnp.bfloat16).reshape(row_count, heads_here, value_width)
    within, query_map, summary = block_local(query, key_rows, values, request, starts)

    carried, out_t = carried_scan(summary, masks, out_weight.T, blocks, rounds)

    gains = head_gain.reshape(heads_here, value_width)
    normed = finish(within, query_map, carried, request, starts, gains).reshape(
        row_count, heads_here * value_width
    )
    partial_terms = lax.dot_general(
        normed, out_t, (((1,), (1,)), ((), ())), preferred_element_type=jnp.float32
    )
    return ring_scatter(partial_terms.astype(jnp.bfloat16), cols)


def solution(mesh):
    placed = (
        P("dp", None),
        P("dp", "mp"),
        P("dp", "mp"),
        P("dp", "mp"),
        P(None, "mp"),
        P(None, "mp"),
        P(),
        P(),
        P("mp"),
        P("mp", "dp"),
    )
    return jax.shard_map(
        per_device, mesh=mesh, in_specs=placed, out_specs=P("dp", "mp"), check_vma=False
    )
```

```python
import math

import functools

import jax
import jax.numpy as jnp
import numpy as np
from jax import lax
from jax.experimental import pallas as pl
from jax.experimental.pallas import tpu as pltpu
from jax.sharding import PartitionSpec as P

MESH = pl.DeviceIdType.MESH

F = 16
R = 16


EPSILON = 1e-05


def taylor(inputs):
    squares = (inputs[..., :, None] * inputs[..., None, :]).reshape(
        inputs.shape[:-1] + (inputs.shape[-1] * inputs.shape[-1],)
    )
    constant = jnp.ones(inputs.shape[:-1] + (1,), jnp.float32)
    return jnp.concatenate([constant, 0.5 * inputs, squares * (0.25 / math.sqrt(2.0))], axis=-1)


def packed_features(width):
    index, weight = list(range(1 + width)), [1.0] * (1 + width)
    for a in range(width):
        for b in range(a, width):
            index.append(1 + width + a * width + b)
            weight.append(1.0 if a == b else 2.0)
    return np.asarray(index, np.int32), np.asarray(weight, np.float32)


def request_of(bounds, positions):
    return jnp.sum((positions[:, None] >= bounds[None, :]).astype(jnp.int32), axis=1)


def token_tables(lengths, adapter_ids, positions):
    bounds = jnp.cumsum(lengths)
    request = request_of(bounds, positions)
    openings = bounds - lengths
    starts = jnp.any(positions[:, None] == openings[None, :], axis=1)
    picked = request[:, None] == jnp.arange(lengths.shape[0], dtype=jnp.int32)[None, :]
    adapter = jnp.sum(jnp.where(picked, adapter_ids[None, :], 0), axis=1)
    return (request, starts, adapter)


def block_local(query, key_rows, values, request, starts):
    scores = jnp.einsum("ihd,jhd->hij", query, key_rows, preferred_element_type=jnp.float32) * 0.25
    weights = 1.0 + scores + 0.5 * scores * scores
    indexes = jnp.arange(request.shape[0], dtype=jnp.int32)
    allowed = (indexes[None, :] <= indexes[:, None]) & (request[None, :] == request[:, None])
    weights = jnp.where(allowed[None], weights, 0.0).astype(jnp.bfloat16)
    within = jnp.einsum("hij,jhe->ihe", weights, values, preferred_element_type=jnp.float32)
    index, weight = packed_features(query.shape[-1])
    query_map = taylor(query.astype(jnp.float32)).astype(jnp.bfloat16)
    query_map = query_map[..., index] * jnp.asarray(weight, jnp.bfloat16)
    key_map = taylor(key_rows.astype(jnp.float32)).astype(jnp.bfloat16)[..., index]
    tail_mask = (request == request[-1]).astype(jnp.bfloat16)
    masked_keys = key_map * tail_mask[:, None, None]
    summary = jnp.einsum("ihf,ihe->hfe", masked_keys, values, preferred_element_type=jnp.float32)
    return (within, query_map, summary)


def finish(within, query_map, carried, request, starts, gains):
    follows = ((request == request[0]) & jnp.logical_not(starts[0])).astype(jnp.float32)
    cross = jnp.einsum(
        "ihf,hfe->ihe", query_map, carried.astype(jnp.bfloat16), preferred_element_type=jnp.float32
    )
    combined = within + follows[:, None, None] * cross
    factor = lax.rsqrt(jnp.mean(combined * combined, axis=-1, keepdims=True) + EPSILON)
    return (combined * factor * gains[None]).astype(jnp.bfloat16)


def scan_rounds(n):
    rounds = 1
    while 4 ** rounds < n:
        rounds += 1
    return rounds


def scan_masks(lengths, row_count, place, blocks, rounds):
    openings = jnp.cumsum(lengths) - lengths
    ids = jnp.arange(blocks, dtype=jnp.int32)
    firsts = ids * row_count
    inside = (openings[None, :] >= firsts[:, None]) & (openings[None, :] < firsts[:, None] + row_count)
    flags = jnp.any(inside, axis=1).astype(jnp.int32)
    reach, drop = [], []
    for k in range(rounds):
        for j in range(1, 4):
            for top in (0, 1):
                reach.append(j * 4**k - 1)
                drop.append(top)
    lows = place - jnp.asarray(reach, jnp.int32)
    tops = place - jnp.asarray(drop, jnp.int32)
    covered = (ids[None, :] >= lows[:, None]) & (ids[None, :] <= tops[:, None])
    hits = jnp.sum(jnp.where(covered, flags[None, :], 0), axis=1)
    return (hits == 0).astype(jnp.float32)


def scan_kernel(n, rounds, s_ref, m_ref, xo_ref, e_ref, go_ref, parts, recv, acc, send_sem, recv_sem,
                send_o, recv_o, send_x, recv_x, own):
    me = lax.axis_index("dp")
    col = lax.axis_index("mp")
    chips = n // 2
    side = me % 2
    chip = me // 2
    mate = me + 1 - 2 * side
    barrier = pltpu.get_barrier_semaphore()

    def each(lo, hi, body):
        def step(k, carry):
            body(k)
            return carry

        lax.fori_loop(lo, hi, step, 0)

    each(1, chips, lambda k: pl.semaphore_signal(
        barrier, 1, device_id=((me + 2 * k) % n, col), device_id_type=MESH))
    pl.semaphore_signal(barrier, 1, device_id=(mate, col), device_id_type=MESH)
    peers = 0
    for k in range(rounds):
        for j in range(1, 4):
            d = j * 4**k

            @pl.when(me + d < n)
            def _():
                pl.semaphore_signal(barrier, 1, device_id=(me + d, col), device_id_type=MESH)

            @pl.when(me >= d)
            def _():
                pl.semaphore_signal(barrier, 1, device_id=(me - d, col), device_id_type=MESH)

            peers = peers + (me // d + n - 1) // n + ((n - 1 - me) // d + n - 1) // n
    pl.semaphore_wait(barrier, peers + chips)

    mine = pltpu.make_async_copy(xo_ref, go_ref.at[side, chip], own)
    mine.start()

    def to_far(k):
        return pltpu.make_async_remote_copy(
            src_ref=xo_ref,
            dst_ref=go_ref.at[side, chip],
            send_sem=send_o.at[k],
            recv_sem=recv_o.at[chip],
            device_id=((me + 2 * k) % n, col),
            device_id_type=MESH,
        )

    def from_far(k):
        other = (chip + chips - k) % chips
        return pltpu.make_async_remote_copy(
            src_ref=xo_ref,
            dst_ref=go_ref.at[side, other],
            send_sem=send_o.at[k],
            recv_sem=recv_o.at[other],
            device_id=(2 * other + side, col),
            device_id_type=MESH,
        )

    swap_out = pltpu.make_async_remote_copy(
        src_ref=go_ref.at[side],
        dst_ref=go_ref.at[side],
        send_sem=send_x,
        recv_sem=recv_x,
        device_id=(mate, col),
        device_id_type=MESH,
    )
    swap_in = pltpu.make_async_remote_copy(
        src_ref=go_ref.at[1 - side],
        dst_ref=go_ref.at[1 - side],
        send_sem=send_x,
        recv_sem=recv_x,
        device_id=(mate, col),
        device_id_type=MESH,
    )
    each(1, chips, lambda k: to_far(k).start())

    e_ref[...] = jnp.zeros_like(e_ref)
    copies = []
    for k in range(rounds):
        src = s_ref if k == 0 else parts.at[k - 1]
        if k < rounds - 1:
            acc[...] = src[...].astype(jnp.float32)
        for j in range(1, 4):
            d = j * 4**k
            copy = pltpu.make_async_remote_copy(
                src_ref=src,
                dst_ref=recv.at[k, j - 1],
                send_sem=send_sem.at[k, j - 1],
                recv_sem=recv_sem.at[k, j - 1],
                device_id=(me + d, col),
                device_id_type=MESH,
            )
            copies.append((copy, d))

            @pl.when(me + d < n)
            def _():
                copy.start()

        for j in range(1, 4):
            d = j * 4**k
            copy = copies[3 * k + j - 1][0]
            row = 6 * k + 2 * (j - 1)

            @pl.when(me >= d)
            def _():
                copy.wait_recv()
                got = recv[k, j - 1].astype(jnp.float32)
                if k < rounds - 1:
                    acc[...] += m_ref[row] * got
                e_ref[...] += m_ref[row + 1] * got

        if k < rounds - 1:
            parts[k] = acc[...].astype(parts.dtype)

    each(1, chips, lambda k: from_far(k).wait_recv())
    mine.wait()
    swap_out.start()
    swap_in.wait_recv()
    each(1, chips, lambda k: to_far(k).wait_send())
    swap_out.wait_send()

    for copy, d in copies:

        @pl.when(me + d < n)
        def _():
            copy.wait_send()


def carried_scan(summary, masks, piece, n, rounds):
    shape = summary.shape
    flat = summary.reshape(-1, shape[-1]).astype(jnp.bfloat16)
    size = flat.shape[0] * flat.shape[1]
    out, gathered = pl.pallas_call(
        functools.partial(scan_kernel, n, rounds),
        out_shape=(
            jax.ShapeDtypeStruct(flat.shape, jnp.float32),
            jax.ShapeDtypeStruct((2, n // 2) + piece.shape, piece.dtype),
        ),
        in_specs=[
            pl.BlockSpec(memory_space=pltpu.VMEM),
            pl.BlockSpec(memory_space=pltpu.SMEM),
            pl.BlockSpec(memory_space=pltpu.VMEM),
        ],
        out_specs=(pl.BlockSpec(memory_space=pltpu.VMEM), pl.BlockSpec(memory_space=pltpu.VMEM)),
        scratch_shapes=[
            pltpu.VMEM((max(rounds - 1, 1),) + flat.shape, jnp.bfloat16),
            pltpu.VMEM((rounds, 3) + flat.shape, jnp.bfloat16),
            pltpu.VMEM(flat.shape, jnp.float32),
            pltpu.SemaphoreType.DMA((rounds, 3)),
            pltpu.SemaphoreType.DMA((rounds, 3)),
            pltpu.SemaphoreType.DMA((n // 2,)),
            pltpu.SemaphoreType.DMA((n // 2,)),
            pltpu.SemaphoreType.DMA(()),
            pltpu.SemaphoreType.DMA(()),
            pltpu.SemaphoreType.DMA(()),
        ],
        compiler_params=pltpu.CompilerParams(collective_id=0, has_side_effects=True),
        cost_estimate=pl.CostEstimate(
            flops=3 * rounds * size,
            bytes_accessed=18 * rounds * size + 2 * n * piece.size,
            transcendentals=0,
        ),
    )(flat, masks, piece)
    gathered = jnp.transpose(gathered, (1, 0, 2, 3)).reshape(n * piece.shape[0], piece.shape[1])
    return out.reshape(shape), gathered


def gather_kernel(n, m, xd_ref, xm_ref, early_ref, gd_ref, gm_ref, send_d, recv_d, send_x, recv_x, send_m, recv_m, own):
    me = lax.axis_index("dp")
    col = lax.axis_index("mp")
    chips = n // 2
    side = me % 2
    chip = me // 2
    mate = me + 1 - 2 * side
    barrier = pltpu.get_barrier_semaphore()

    def each(lo, hi, body):
        def step(k, carry):
            body(k)
            return carry

        lax.fori_loop(lo, hi, step, 0)

    each(1, chips, lambda k: pl.semaphore_signal(
        barrier, 1, device_id=((me + 2 * k) % n, col), device_id_type=MESH))
    pl.semaphore_signal(barrier, 1, device_id=(mate, col), device_id_type=MESH)
    each(1, m, lambda k: pl.semaphore_signal(
        barrier, 1, device_id=(me, (col + k) % m), device_id_type=MESH))
    pl.semaphore_wait(barrier, chips + m - 1)

    mine = pltpu.make_async_copy(xd_ref, gd_ref.at[side, chip], own)
    mine.start()

    def to_far(k):
        return pltpu.make_async_remote_copy(
            src_ref=xd_ref,
            dst_ref=gd_ref.at[side, chip],
            send_sem=send_d.at[k],
            recv_sem=recv_d.at[chip],
            device_id=((me + 2 * k) % n, col),
            device_id_type=MESH,
        )

    def from_far(k):
        other = (chip + chips - k) % chips
        return pltpu.make_async_remote_copy(
            src_ref=xd_ref,
            dst_ref=gd_ref.at[side, other],
            send_sem=send_d.at[k],
            recv_sem=recv_d.at[other],
            device_id=(2 * other + side, col),
            device_id_type=MESH,
        )

    swap_out = pltpu.make_async_remote_copy(
        src_ref=gd_ref.at[side],
        dst_ref=gd_ref.at[side],
        send_sem=send_x,
        recv_sem=recv_x,
        device_id=(mate, col),
        device_id_type=MESH,
    )
    swap_in = pltpu.make_async_remote_copy(
        src_ref=gd_ref.at[1 - side],
        dst_ref=gd_ref.at[1 - side],
        send_sem=send_x,
        recv_sem=recv_x,
        device_id=(mate, col),
        device_id_type=MESH,
    )

    def to_mp(k):
        return pltpu.make_async_remote_copy(
            src_ref=xm_ref,
            dst_ref=gm_ref.at[col],
            send_sem=send_m.at[k],
            recv_sem=recv_m.at[col],
            device_id=(me, (col + k) % m),
            device_id_type=MESH,
        )

    def from_mp(k):
        other = (col + m - k) % m
        return pltpu.make_async_remote_copy(
            src_ref=xm_ref,
            dst_ref=gm_ref.at[other],
            send_sem=send_m.at[k],
            recv_sem=recv_m.at[other],
            device_id=(me, other),
            device_id_type=MESH,
        )

    each(1, chips, lambda k: to_far(k).start())
    each(1, m, lambda k: to_mp(k).start())
    gm_ref[col] = xm_ref[...]
    each(1, chips, lambda k: from_far(k).wait_recv())
    mine.wait()
    swap_out.start()
    each(1, m, lambda k: from_mp(k).wait_recv())
    swap_in.wait_recv()
    each(1, chips, lambda k: to_far(k).wait_send())
    swap_out.wait_send()
    each(1, m, lambda k: to_mp(k).wait_send())


def direct_gather(xd, xm, early, n, m):
    moved = n * xd.size * 2 + m * xm.size * 2
    gd, gm = pl.pallas_call(
        functools.partial(gather_kernel, n, m),
        out_shape=(
            jax.ShapeDtypeStruct((2, n // 2) + xd.shape, xd.dtype),
            jax.ShapeDtypeStruct((m,) + xm.shape, xm.dtype),
        ),
        in_specs=[pl.BlockSpec(memory_space=pltpu.VMEM)] * 2 + [pl.BlockSpec(memory_space=pltpu.SMEM)],
        out_specs=(pl.BlockSpec(memory_space=pltpu.VMEM), pl.BlockSpec(memory_space=pltpu.VMEM)),
        scratch_shapes=[
            pltpu.SemaphoreType.DMA((n // 2,)),
            pltpu.SemaphoreType.DMA((n // 2,)),
            pltpu.SemaphoreType.DMA(()),
            pltpu.SemaphoreType.DMA(()),
            pltpu.SemaphoreType.DMA((m,)),
            pltpu.SemaphoreType.DMA((m,)),
            pltpu.SemaphoreType.DMA(()),
        ],
        compiler_params=pltpu.CompilerParams(collective_id=1, has_side_effects=True),
        cost_estimate=pl.CostEstimate(flops=0, bytes_accessed=moved, transcendentals=0),
    )(xd, xm, early)
    return jnp.transpose(gd, (1, 0, 2, 3)), gm


def ring_kernel(m, x_ref, o_ref, acc_a, acc_b, got_a, got_b, send_a, recv_a, send_b, recv_b):
    me = lax.axis_index("dp")
    col = lax.axis_index("mp")
    right = (col + 1) % m
    left = (col + m - 1) % m
    width = o_ref.shape[1]
    half = width // 2
    barrier = pltpu.get_barrier_semaphore()
    pl.semaphore_signal(barrier, 1, device_id=(me, right), device_id_type=MESH)
    pl.semaphore_signal(barrier, 1, device_id=(me, left), device_id_type=MESH)
    pl.semaphore_wait(barrier, 2)

    def piece(t, side):
        return pl.ds(pl.multiple_of(t * width + side * half, half), half)

    copies = []
    for s in range(m - 1):
        ta = (col + 2 * m - 1 - s) % m
        tb = (col + 1 + s) % m
        if s == 0:
            src_a = x_ref.at[:, piece(ta, 0)]
            src_b = x_ref.at[:, piece(tb, 1)]
        else:
            copies[-1][0].wait_recv()
            copies[-1][1].wait_recv()
            acc_a[s - 1] = (
                got_a[s - 1].astype(jnp.float32) + x_ref[:, piece(ta, 0)].astype(jnp.float32)
            ).astype(acc_a.dtype)
            acc_b[s - 1] = (
                got_b[s - 1].astype(jnp.float32) + x_ref[:, piece(tb, 1)].astype(jnp.float32)
            ).astype(acc_b.dtype)
            src_a = acc_a.at[s - 1]
            src_b = acc_b.at[s - 1]
        ca = pltpu.make_async_remote_copy(
            src_ref=src_a,
            dst_ref=got_a.at[s],
            send_sem=send_a.at[s],
            recv_sem=recv_a.at[s],
            device_id=(me, right),
            device_id_type=MESH,
        )
        cb = pltpu.make_async_remote_copy(
            src_ref=src_b,
            dst_ref=got_b.at[s],
            send_sem=send_b.at[s],
            recv_sem=recv_b.at[s],
            device_id=(me, left),
            device_id_type=MESH,
        )
        ca.start()
        cb.start()
        copies.append((ca, cb))
    copies[-1][0].wait_recv()
    copies[-1][1].wait_recv()
    last = m - 2
    o_ref[:, :half] = (
        got_a[last].astype(jnp.float32) + x_ref[:, piece(col, 0)].astype(jnp.float32)
    ).astype(o_ref.dtype)
    o_ref[:, half:] = (
        got_b[last].astype(jnp.float32) + x_ref[:, piece(col, 1)].astype(jnp.float32)
    ).astype(o_ref.dtype)
    for ca, cb in copies:
        ca.wait_send()
        cb.wait_send()


def ring_scatter(x, m):
    rows, total = x.shape
    width = total // m
    half = width // 2
    slot = (m - 1, rows, half)
    return pl.pallas_call(
        functools.partial(ring_kernel, m),
        out_shape=jax.ShapeDtypeStruct((rows, width), x.dtype),
        in_specs=[pl.BlockSpec(memory_space=pltpu.VMEM)],
        out_specs=pl.BlockSpec(memory_space=pltpu.VMEM),
        scratch_shapes=[
            pltpu.VMEM(slot, x.dtype),
            pltpu.VMEM(slot, x.dtype),
            pltpu.VMEM(slot, x.dtype),
            pltpu.VMEM(slot, x.dtype),
            pltpu.SemaphoreType.DMA((m - 1,)),
            pltpu.SemaphoreType.DMA((m - 1,)),
            pltpu.SemaphoreType.DMA((m - 1,)),
            pltpu.SemaphoreType.DMA((m - 1,)),
        ],
        compiler_params=pltpu.CompilerParams(collective_id=2, has_side_effects=True),
        cost_estimate=pl.CostEstimate(
            flops=2 * rows * total, bytes_accessed=4 * rows * total, transcendentals=0
        ),
    )(x)


def per_device(
    tokens,
    q_weight,
    k_weight,
    v_weight,
    adapter_down,
    adapter_up,
    lengths,
    adapter_ids,
    head_gain,
    out_weight,
):
    row_count = tokens.shape[0]
    qf = q_weight.shape[1]
    heads_here = qf // F
    vw = v_weight.shape[1]
    value_width = vw // heads_here
    blocks = lax.axis_size("dp")
    place = lax.axis_index("dp")
    positions = place * row_count + jnp.arange(row_count, dtype=jnp.int32)
    request, starts, adapter = token_tables(lengths, adapter_ids, positions)

    local = jnp.concatenate([q_weight, k_weight, v_weight], axis=1)
    part_low = jnp.dot(tokens, adapter_down, preferred_element_type=jnp.float32)
    owners = lax.axis_index("mp") * (adapter_down.shape[1] // R) + (
        jnp.arange(adapter_down.shape[1], dtype=jnp.int32) // R
    )
    part_low = jnp.where(adapter[:, None] == owners[None, :], part_low, 0.0).astype(jnp.bfloat16)
    cols = lax.axis_size("mp")
    rounds = scan_rounds(blocks)
    masks = scan_masks(lengths, row_count, place, blocks, rounds)
    gathered, low_parts = direct_gather(local, part_low, masks, blocks, cols)
    gathered = gathered.reshape(blocks * local.shape[0], local.shape[1])
    q_full = gathered[:, :qf]
    k_full = gathered[:, qf : 2 * qf]
    v_full = gathered[:, 2 * qf :]
    low_rank = jnp.transpose(low_parts, (1, 0, 2)).reshape(row_count, cols * part_low.shape[1])

    query_sum = jnp.dot(tokens, q_full, preferred_element_type=jnp.float32)
    key_sum = jnp.dot(tokens, k_full, preferred_element_type=jnp.float32)
    value_sum = jnp.dot(tokens, v_full, preferred_element_type=jnp.float32)
    query = query_sum.astype(jnp.bfloat16).reshape(row_count, heads_here, F)
    key_rows = key_sum.astype(jnp.bfloat16).reshape(row_count, heads_here, F)
    values = value_sum + jnp.dot(low_rank, adapter_up, preferred_element_type=jnp.float32)
    values = values.astype(jnp.bfloat16).reshape(row_count, heads_here, value_width)
    within, query_map, summary = block_local(query, key_rows, values, request, starts)

    carried, out_t = carried_scan(summary, masks, out_weight.T, blocks, rounds)

    gains = head_gain.reshape(heads_here, value_width)
    normed = finish(within, query_map, carried, request, starts, gains).reshape(
        row_count, heads_here * value_width
    )
    partial_terms = lax.dot_general(
        normed, out_t, (((1,), (1,)), ((), ())), preferred_element_type=jnp.float32
    )
    return ring_scatter(partial_terms.astype(jnp.bfloat16), cols)


def solution(mesh):
    placed = (
        P("dp", None),
        P("dp", "mp"),
        P("dp", "mp"),
        P("dp", "mp"),
        P(None, "mp"),
        P(None, "mp"),
        P(),
        P(),
        P("mp"),
        P("mp", "dp"),
    )
    return jax.shard_map(
        per_device, mesh=mesh, in_specs=placed, out_specs=P("dp", "mp"), check_vma=False
    )
```

```python
import math

import functools

import jax
import jax.numpy as jnp
import numpy as np
from jax import lax
from jax.experimental import pallas as pl
from jax.experimental.pallas import tpu as pltpu
from jax.sharding import PartitionSpec as P

MESH = pl.DeviceIdType.MESH

F = 16
R = 16


EPSILON = 1e-05


def taylor(inputs):
    squares = (inputs[..., :, None] * inputs[..., None, :]).reshape(
        inputs.shape[:-1] + (inputs.shape[-1] * inputs.shape[-1],)
    )
    constant = jnp.ones(inputs.shape[:-1] + (1,), jnp.float32)
    return jnp.concatenate([constant, 0.5 * inputs, squares * (0.25 / math.sqrt(2.0))], axis=-1)


def packed_features(width):
    index, weight = list(range(1 + width)), [1.0] * (1 + width)
    for a in range(width):
        for b in range(a, width):
            index.append(1 + width + a * width + b)
            weight.append(1.0 if a == b else 2.0)
    return np.asarray(index, np.int32), np.asarray(weight, np.float32)


def request_of(bounds, positions):
    return jnp.sum((positions[:, None] >= bounds[None, :]).astype(jnp.int32), axis=1)


def token_tables(lengths, adapter_ids, positions):
    bounds = jnp.cumsum(lengths)
    request = request_of(bounds, positions)
    openings = bounds - lengths
    starts = jnp.any(positions[:, None] == openings[None, :], axis=1)
    picked = request[:, None] == jnp.arange(lengths.shape[0], dtype=jnp.int32)[None, :]
    adapter = jnp.sum(jnp.where(picked, adapter_ids[None, :], 0), axis=1)
    return (request, starts, adapter)


def block_local(query, key_rows, values, request, starts):
    scores = jnp.einsum("ihd,jhd->hij", query, key_rows, preferred_element_type=jnp.float32) * 0.25
    weights = 1.0 + scores + 0.5 * scores * scores
    indexes = jnp.arange(request.shape[0], dtype=jnp.int32)
    allowed = (indexes[None, :] <= indexes[:, None]) & (request[None, :] == request[:, None])
    weights = jnp.where(allowed[None], weights, 0.0).astype(jnp.bfloat16)
    within = jnp.einsum("hij,jhe->ihe", weights, values, preferred_element_type=jnp.float32)
    index, weight = packed_features(query.shape[-1])
    query_map = taylor(query.astype(jnp.float32)).astype(jnp.bfloat16)
    query_map = query_map[..., index] * jnp.asarray(weight, jnp.bfloat16)
    key_map = taylor(key_rows.astype(jnp.float32)).astype(jnp.bfloat16)[..., index]
    tail_mask = (request == request[-1]).astype(jnp.bfloat16)
    masked_keys = key_map * tail_mask[:, None, None]
    summary = jnp.einsum("ihf,ihe->hfe", masked_keys, values, preferred_element_type=jnp.float32)
    return (within, query_map, summary)


def finish(within, query_map, carried, request, starts, gains):
    follows = ((request == request[0]) & jnp.logical_not(starts[0])).astype(jnp.float32)
    cross = jnp.einsum(
        "ihf,hfe->ihe", query_map, carried.astype(jnp.bfloat16), preferred_element_type=jnp.float32
    )
    combined = within + follows[:, None, None] * cross
    factor = lax.rsqrt(jnp.mean(combined * combined, axis=-1, keepdims=True) + EPSILON)
    return (combined * factor * gains[None]).astype(jnp.bfloat16)


def scan_masks(lengths, row_count, place, blocks, rounds):
    openings = jnp.cumsum(lengths) - lengths
    ids = jnp.arange(blocks, dtype=jnp.int32)
    firsts = ids * row_count
    inside = (openings[None, :] >= firsts[:, None]) & (openings[None, :] < firsts[:, None] + row_count)
    flags = jnp.any(inside, axis=1).astype(jnp.int32)
    spans = jnp.asarray([1 << (k // 2) for k in range(2 * rounds)], jnp.int32)
    tops = place - jnp.asarray([k % 2 for k in range(2 * rounds)], jnp.int32)
    lows = place - spans + 1
    covered = (ids[None, :] >= lows[:, None]) & (ids[None, :] <= tops[:, None])
    hits = jnp.sum(jnp.where(covered, flags[None, :], 0), axis=1)
    return (hits == 0).astype(jnp.float32)


def scan_kernel(n, rounds, s_ref, m_ref, xo_ref, e_ref, go_ref, parts, recv, send_sem, recv_sem,
                send_o, recv_o, send_x, recv_x, own):
    me = lax.axis_index("dp")
    col = lax.axis_index("mp")
    chips = n // 2
    side = me % 2
    chip = me // 2
    mate = me + 1 - 2 * side
    barrier = pltpu.get_barrier_semaphore()

    def each(lo, hi, body):
        def step(k, carry):
            body(k)
            return carry

        lax.fori_loop(lo, hi, step, 0)

    each(1, chips, lambda k: pl.semaphore_signal(
        barrier, 1, device_id=((me + 2 * k) % n, col), device_id_type=MESH))
    pl.semaphore_signal(barrier, 1, device_id=(mate, col), device_id_type=MESH)
    for k in range(rounds):
        d = 1 << k

        @pl.when(me + d < n)
        def _():
            pl.semaphore_signal(barrier, 1, device_id=(me + d, col), device_id_type=MESH)

        @pl.when(me >= d)
        def _():
            pl.semaphore_signal(barrier, 1, device_id=(me - d, col), device_id_type=MESH)

    peers = 0
    for k in range(rounds):
        d = 1 << k
        peers = peers + (me // d + n - 1) // n + ((n - 1 - me) // d + n - 1) // n
    pl.semaphore_wait(barrier, peers + chips)

    mine = pltpu.make_async_copy(xo_ref, go_ref.at[side, chip], own)
    mine.start()

    def to_far(k):
        return pltpu.make_async_remote_copy(
            src_ref=xo_ref,
            dst_ref=go_ref.at[side, chip],
            send_sem=send_o.at[k],
            recv_sem=recv_o.at[chip],
            device_id=((me + 2 * k) % n, col),
            device_id_type=MESH,
        )

    def from_far(k):
        other = (chip + chips - k) % chips
        return pltpu.make_async_remote_copy(
            src_ref=xo_ref,
            dst_ref=go_ref.at[side, other],
            send_sem=send_o.at[k],
            recv_sem=recv_o.at[other],
            device_id=(2 * other + side, col),
            device_id_type=MESH,
        )

    swap_out = pltpu.make_async_remote_copy(
        src_ref=go_ref.at[side],
        dst_ref=go_ref.at[side],
        send_sem=send_x,
        recv_sem=recv_x,
        device_id=(mate, col),
        device_id_type=MESH,
    )
    swap_in = pltpu.make_async_remote_copy(
        src_ref=go_ref.at[1 - side],
        dst_ref=go_ref.at[1 - side],
        send_sem=send_x,
        recv_sem=recv_x,
        device_id=(mate, col),
        device_id_type=MESH,
    )
    each(1, chips, lambda k: to_far(k).start())

    e_ref[...] = jnp.zeros_like(e_ref)
    copies = []
    for k in range(rounds):
        d = 1 << k
        src = s_ref if k == 0 else parts.at[k - 1]
        copy = pltpu.make_async_remote_copy(
            src_ref=src,
            dst_ref=recv.at[k],
            send_sem=send_sem.at[k],
            recv_sem=recv_sem.at[k],
            device_id=(me + d, col),
            device_id_type=MESH,
        )
        copies.append(copy)

        @pl.when(me + d < n)
        def _():
            copy.start()

        @pl.when(me >= d)
        def _():
            copy.wait_recv()
            got = recv[k].astype(jnp.float32)
            if k < rounds - 1:
                parts[k] = (src[...].astype(jnp.float32) + m_ref[2 * k] * got).astype(parts.dtype)
            e_ref[...] += m_ref[2 * k + 1] * got

        if k < rounds - 1:

            @pl.when(me < d)
            def _():
                parts[k] = src[...]

    each(1, chips, lambda k: from_far(k).wait_recv())
    mine.wait()
    swap_out.start()
    swap_in.wait_recv()
    each(1, chips, lambda k: to_far(k).wait_send())
    swap_out.wait_send()

    for k in range(rounds):
        d = 1 << k

        @pl.when(me + d < n)
        def _():
            copies[k].wait_send()


def carried_scan(summary, masks, piece, n, rounds):
    shape = summary.shape
    flat = summary.reshape(-1, shape[-1]).astype(jnp.bfloat16)
    size = flat.shape[0] * flat.shape[1]
    out, gathered = pl.pallas_call(
        functools.partial(scan_kernel, n, rounds),
        out_shape=(
            jax.ShapeDtypeStruct(flat.shape, jnp.float32),
            jax.ShapeDtypeStruct((2, n // 2) + piece.shape, piece.dtype),
        ),
        in_specs=[
            pl.BlockSpec(memory_space=pltpu.VMEM),
            pl.BlockSpec(memory_space=pltpu.SMEM),
            pl.BlockSpec(memory_space=pltpu.VMEM),
        ],
        out_specs=(pl.BlockSpec(memory_space=pltpu.VMEM), pl.BlockSpec(memory_space=pltpu.VMEM)),
        scratch_shapes=[
            pltpu.VMEM((max(rounds - 1, 1),) + flat.shape, jnp.bfloat16),
            pltpu.VMEM((rounds,) + flat.shape, jnp.bfloat16),
            pltpu.SemaphoreType.DMA((rounds,)),
            pltpu.SemaphoreType.DMA((rounds,)),
            pltpu.SemaphoreType.DMA((n // 2,)),
            pltpu.SemaphoreType.DMA((n // 2,)),
            pltpu.SemaphoreType.DMA(()),
            pltpu.SemaphoreType.DMA(()),
            pltpu.SemaphoreType.DMA(()),
        ],
        compiler_params=pltpu.CompilerParams(collective_id=0, has_side_effects=True),
        cost_estimate=pl.CostEstimate(
            flops=3 * rounds * size,
            bytes_accessed=6 * rounds * size + 2 * n * piece.size,
            transcendentals=0,
        ),
    )(flat, masks, piece)
    gathered = jnp.transpose(gathered, (1, 0, 2, 3)).reshape(n * piece.shape[0], piece.shape[1])
    return out.reshape(shape), gathered


def gather_kernel(n, m, xd_ref, xm_ref, early_ref, gd_ref, gm_ref, send_d, recv_d, send_x, recv_x, send_m, recv_m, own):
    me = lax.axis_index("dp")
    col = lax.axis_index("mp")
    chips = n // 2
    side = me % 2
    chip = me // 2
    mate = me + 1 - 2 * side
    barrier = pltpu.get_barrier_semaphore()

    def each(lo, hi, body):
        def step(k, carry):
            body(k)
            return carry

        lax.fori_loop(lo, hi, step, 0)

    each(1, chips, lambda k: pl.semaphore_signal(
        barrier, 1, device_id=((me + 2 * k) % n, col), device_id_type=MESH))
    pl.semaphore_signal(barrier, 1, device_id=(mate, col), device_id_type=MESH)
    each(1, m, lambda k: pl.semaphore_signal(
        barrier, 1, device_id=(me, (col + k) % m), device_id_type=MESH))
    pl.semaphore_wait(barrier, chips + m - 1)

    mine = pltpu.make_async_copy(xd_ref, gd_ref.at[side, chip], own)
    mine.start()

    def to_far(k):
        return pltpu.make_async_remote_copy(
            src_ref=xd_ref,
            dst_ref=gd_ref.at[side, chip],
            send_sem=send_d.at[k],
            recv_sem=recv_d.at[chip],
            device_id=((me + 2 * k) % n, col),
            device_id_type=MESH,
        )

    def from_far(k):
        other = (chip + chips - k) % chips
        return pltpu.make_async_remote_copy(
            src_ref=xd_ref,
            dst_ref=gd_ref.at[side, other],
            send_sem=send_d.at[k],
            recv_sem=recv_d.at[other],
            device_id=(2 * other + side, col),
            device_id_type=MESH,
        )

    swap_out = pltpu.make_async_remote_copy(
        src_ref=gd_ref.at[side],
        dst_ref=gd_ref.at[side],
        send_sem=send_x,
        recv_sem=recv_x,
        device_id=(mate, col),
        device_id_type=MESH,
    )
    swap_in = pltpu.make_async_remote_copy(
        src_ref=gd_ref.at[1 - side],
        dst_ref=gd_ref.at[1 - side],
        send_sem=send_x,
        recv_sem=recv_x,
        device_id=(mate, col),
        device_id_type=MESH,
    )

    def to_mp(k):
        return pltpu.make_async_remote_copy(
            src_ref=xm_ref,
            dst_ref=gm_ref.at[col],
            send_sem=send_m.at[k],
            recv_sem=recv_m.at[col],
            device_id=(me, (col + k) % m),
            device_id_type=MESH,
        )

    def from_mp(k):
        other = (col + m - k) % m
        return pltpu.make_async_remote_copy(
            src_ref=xm_ref,
            dst_ref=gm_ref.at[other],
            send_sem=send_m.at[k],
            recv_sem=recv_m.at[other],
            device_id=(me, other),
            device_id_type=MESH,
        )

    each(1, chips, lambda k: to_far(k).start())
    each(1, m, lambda k: to_mp(k).start())
    gm_ref[col] = xm_ref[...]
    each(1, chips, lambda k: from_far(k).wait_recv())
    mine.wait()
    swap_out.start()
    each(1, m, lambda k: from_mp(k).wait_recv())
    swap_in.wait_recv()
    each(1, chips, lambda k: to_far(k).wait_send())
    swap_out.wait_send()
    each(1, m, lambda k: to_mp(k).wait_send())


def direct_gather(xd, xm, early, n, m):
    moved = n * xd.size * 2 + m * xm.size * 2
    gd, gm = pl.pallas_call(
        functools.partial(gather_kernel, n, m),
        out_shape=(
            jax.ShapeDtypeStruct((2, n // 2) + xd.shape, xd.dtype),
            jax.ShapeDtypeStruct((m,) + xm.shape, xm.dtype),
        ),
        in_specs=[pl.BlockSpec(memory_space=pltpu.VMEM)] * 2 + [pl.BlockSpec(memory_space=pltpu.SMEM)],
        out_specs=(pl.BlockSpec(memory_space=pltpu.VMEM), pl.BlockSpec(memory_space=pltpu.VMEM)),
        scratch_shapes=[
            pltpu.SemaphoreType.DMA((n // 2,)),
            pltpu.SemaphoreType.DMA((n // 2,)),
            pltpu.SemaphoreType.DMA(()),
            pltpu.SemaphoreType.DMA(()),
            pltpu.SemaphoreType.DMA((m,)),
            pltpu.SemaphoreType.DMA((m,)),
            pltpu.SemaphoreType.DMA(()),
        ],
        compiler_params=pltpu.CompilerParams(collective_id=1, has_side_effects=True),
        cost_estimate=pl.CostEstimate(flops=0, bytes_accessed=moved, transcendentals=0),
    )(xd, xm, early)
    return jnp.transpose(gd, (1, 0, 2, 3)), gm


def ring_kernel(m, n_ref, w_ref, o_ref, acc_a, acc_b, got_a, got_b, send_a, recv_a, send_b, recv_b):
    me = lax.axis_index("dp")
    col = lax.axis_index("mp")
    right = (col + 1) % m
    left = (col + m - 1) % m
    half = o_ref.shape[2]
    width = 2 * half
    barrier = pltpu.get_barrier_semaphore()
    pl.semaphore_signal(barrier, 1, device_id=(me, right), device_id_type=MESH)
    pl.semaphore_signal(barrier, 1, device_id=(me, left), device_id_type=MESH)
    pl.semaphore_wait(barrier, 2)

    def own(t, side):
        rows = w_ref[pl.ds(pl.multiple_of(t * width + side * half, half), half), :]
        return lax.dot_general(
            n_ref[...], rows, (((1,), (1,)), ((), ())), preferred_element_type=jnp.float32
        )

    copies = []
    for s in range(m - 1):
        ta = (col + 2 * m - 1 - s) % m
        tb = (col + 1 + s) % m
        part_a = own(ta, 0)
        part_b = own(tb, 1)
        if s > 0:
            copies[-1][0].wait_recv()
            part_a = part_a + got_a[s - 1].astype(jnp.float32)
        acc_a[s] = part_a.astype(acc_a.dtype)
        ca = pltpu.make_async_remote_copy(
            src_ref=acc_a.at[s],
            dst_ref=got_a.at[s],
            send_sem=send_a.at[s],
            recv_sem=recv_a.at[s],
            device_id=(me, right),
            device_id_type=MESH,
        )
        ca.start()
        if s > 0:
            copies[-1][1].wait_recv()
            part_b = part_b + got_b[s - 1].astype(jnp.float32)
        acc_b[s] = part_b.astype(acc_b.dtype)
        cb = pltpu.make_async_remote_copy(
            src_ref=acc_b.at[s],
            dst_ref=got_b.at[s],
            send_sem=send_b.at[s],
            recv_sem=recv_b.at[s],
            device_id=(me, left),
            device_id_type=MESH,
        )
        cb.start()
        copies.append((ca, cb))
    copies[-1][0].wait_recv()
    copies[-1][1].wait_recv()
    o_ref[0] = got_a[m - 2]
    o_ref[1] = got_b[m - 2]
    for ca, cb in copies:
        ca.wait_send()
        cb.wait_send()


def ring_scatter(normed, out_t, m):
    rows = normed.shape[0]
    total = out_t.shape[0]
    width = total // m
    half = width // 2
    slot = (m - 1, rows, half)
    got = pl.pallas_call(
        functools.partial(ring_kernel, m),
        out_shape=jax.ShapeDtypeStruct((2, rows, half), jnp.bfloat16),
        in_specs=[pl.BlockSpec(memory_space=pltpu.VMEM)] * 2,
        out_specs=pl.BlockSpec(memory_space=pltpu.VMEM),
        scratch_shapes=[
            pltpu.VMEM(slot, jnp.bfloat16),
            pltpu.VMEM(slot, jnp.bfloat16),
            pltpu.VMEM(slot, jnp.bfloat16),
            pltpu.VMEM(slot, jnp.bfloat16),
            pltpu.SemaphoreType.DMA((m - 1,)),
            pltpu.SemaphoreType.DMA((m - 1,)),
            pltpu.SemaphoreType.DMA((m - 1,)),
            pltpu.SemaphoreType.DMA((m - 1,)),
        ],
        compiler_params=pltpu.CompilerParams(collective_id=2, has_side_effects=True),
        cost_estimate=pl.CostEstimate(
            flops=2 * rows * normed.shape[1] * total,
            bytes_accessed=2 * (normed.size + out_t.size) + 4 * rows * total,
            transcendentals=0,
        ),
    )(normed, out_t)
    col = lax.axis_index("mp")
    mine = lax.dynamic_slice_in_dim(out_t, col * width, width, axis=0)
    own = lax.dot_general(normed, mine, (((1,), (1,)), ((), ())), preferred_element_type=jnp.float32)
    got = jnp.concatenate([got[0], got[1]], axis=1).astype(jnp.float32)
    return (got + own).astype(jnp.bfloat16)


def per_device(
    tokens,
    q_weight,
    k_weight,
    v_weight,
    adapter_down,
    adapter_up,
    lengths,
    adapter_ids,
    head_gain,
    out_weight,
):
    row_count = tokens.shape[0]
    qf = q_weight.shape[1]
    heads_here = qf // F
    vw = v_weight.shape[1]
    value_width = vw // heads_here
    blocks = lax.axis_size("dp")
    place = lax.axis_index("dp")
    positions = place * row_count + jnp.arange(row_count, dtype=jnp.int32)
    request, starts, adapter = token_tables(lengths, adapter_ids, positions)

    local = jnp.concatenate([q_weight, k_weight, v_weight], axis=1)
    part_low = jnp.dot(tokens, adapter_down, preferred_element_type=jnp.float32)
    owners = lax.axis_index("mp") * (adapter_down.shape[1] // R) + (
        jnp.arange(adapter_down.shape[1], dtype=jnp.int32) // R
    )
    part_low = jnp.where(adapter[:, None] == owners[None, :], part_low, 0.0).astype(jnp.bfloat16)
    cols = lax.axis_size("mp")
    rounds = max(1, (blocks - 1).bit_length())
    masks = scan_masks(lengths, row_count, place, blocks, rounds)
    gathered, low_parts = direct_gather(local, part_low, masks, blocks, cols)
    gathered = gathered.reshape(blocks * local.shape[0], local.shape[1])
    q_full = gathered[:, :qf]
    k_full = gathered[:, qf : 2 * qf]
    v_full = gathered[:, 2 * qf :]
    low_rank = jnp.transpose(low_parts, (1, 0, 2)).reshape(row_count, cols * part_low.shape[1])

    query_sum = jnp.dot(tokens, q_full, preferred_element_type=jnp.float32)
    key_sum = jnp.dot(tokens, k_full, preferred_element_type=jnp.float32)
    value_sum = jnp.dot(tokens, v_full, preferred_element_type=jnp.float32)
    query = query_sum.astype(jnp.bfloat16).reshape(row_count, heads_here, F)
    key_rows = key_sum.astype(jnp.bfloat16).reshape(row_count, heads_here, F)
    values = value_sum + jnp.dot(low_rank, adapter_up, preferred_element_type=jnp.float32)
    values = values.astype(jnp.bfloat16).reshape(row_count, heads_here, value_width)
    within, query_map, summary = block_local(query, key_rows, values, request, starts)

    carried, out_t = carried_scan(summary, masks, out_weight.T, blocks, rounds)

    gains = head_gain.reshape(heads_here, value_width)
    normed = finish(within, query_map, carried, request, starts, gains).reshape(
        row_count, heads_here * value_width
    )
    return ring_scatter(normed, out_t, cols)


def solution(mesh):
    placed = (
        P("dp", None),
        P("dp", "mp"),
        P("dp", "mp"),
        P("dp", "mp"),
        P(None, "mp"),
        P(None, "mp"),
        P(),
        P(),
        P("mp"),
        P("mp", "dp"),
    )
    return jax.shard_map(
        per_device, mesh=mesh, in_specs=placed, out_specs=P("dp", "mp"), check_vma=False
    )
```

```python
import math

import functools

import jax
import jax.numpy as jnp
import numpy as np
from jax import lax
from jax.experimental import pallas as pl
from jax.experimental.pallas import tpu as pltpu
from jax.sharding import PartitionSpec as P

MESH = pl.DeviceIdType.MESH

F = 16
R = 16


EPSILON = 1e-05


def taylor(inputs):
    squares = (inputs[..., :, None] * inputs[..., None, :]).reshape(
        inputs.shape[:-1] + (inputs.shape[-1] * inputs.shape[-1],)
    )
    constant = jnp.ones(inputs.shape[:-1] + (1,), jnp.float32)
    return jnp.concatenate([constant, 0.5 * inputs, squares * (0.25 / math.sqrt(2.0))], axis=-1)


def packed_taylor(inputs):
    width = inputs.shape[-1]
    squares = [inputs[..., a : a + 1] * inputs[..., a:] for a in range(width)]
    constant = jnp.ones(inputs.shape[:-1] + (1,), jnp.float32)
    return jnp.concatenate(
        [constant, 0.5 * inputs] + [s * (0.25 / math.sqrt(2.0)) for s in squares], axis=-1
    )


def packed_features(width):
    index, weight = list(range(1 + width)), [1.0] * (1 + width)
    for a in range(width):
        for b in range(a, width):
            index.append(1 + width + a * width + b)
            weight.append(1.0 if a == b else 2.0)
    return np.asarray(index, np.int32), np.asarray(weight, np.float32)


def request_of(bounds, positions):
    return jnp.sum((positions[:, None] >= bounds[None, :]).astype(jnp.int32), axis=1)


def token_tables(lengths, adapter_ids, positions):
    bounds = jnp.cumsum(lengths)
    request = request_of(bounds, positions)
    openings = bounds - lengths
    starts = jnp.any(positions[:, None] == openings[None, :], axis=1)
    picked = request[:, None] == jnp.arange(lengths.shape[0], dtype=jnp.int32)[None, :]
    adapter = jnp.sum(jnp.where(picked, adapter_ids[None, :], 0), axis=1)
    return (request, starts, adapter)


def block_local(query, key_rows, values, request, starts):
    scores = jnp.einsum("ihd,jhd->hij", query, key_rows, preferred_element_type=jnp.float32) * 0.25
    weights = 1.0 + scores + 0.5 * scores * scores
    indexes = jnp.arange(request.shape[0], dtype=jnp.int32)
    allowed = (indexes[None, :] <= indexes[:, None]) & (request[None, :] == request[:, None])
    weights = jnp.where(allowed[None], weights, 0.0).astype(jnp.bfloat16)
    within = jnp.einsum("hij,jhe->ihe", weights, values, preferred_element_type=jnp.float32)
    _, weight = packed_features(query.shape[-1])
    query_map = packed_taylor(query.astype(jnp.float32)).astype(jnp.bfloat16)
    query_map = query_map * jnp.asarray(weight, jnp.bfloat16)
    key_map = packed_taylor(key_rows.astype(jnp.float32)).astype(jnp.bfloat16)
    tail_mask = (request == request[-1]).astype(jnp.bfloat16)
    masked_keys = key_map * tail_mask[:, None, None]
    summary = jnp.einsum("ihf,ihe->hfe", masked_keys, values, preferred_element_type=jnp.float32)
    return (within, query_map, summary)


def finish(within, query_map, carried, request, starts, gains):
    follows = ((request == request[0]) & jnp.logical_not(starts[0])).astype(jnp.float32)
    cross = jnp.einsum(
        "ihf,hfe->ihe", query_map, carried.astype(jnp.bfloat16), preferred_element_type=jnp.float32
    )
    combined = within + follows[:, None, None] * cross
    factor = lax.rsqrt(jnp.mean(combined * combined, axis=-1, keepdims=True) + EPSILON)
    return (combined * factor * gains[None]).astype(jnp.bfloat16)


def scan_masks(lengths, row_count, place, blocks, rounds):
    openings = jnp.cumsum(lengths) - lengths
    ids = jnp.arange(blocks, dtype=jnp.int32)
    firsts = ids * row_count
    inside = (openings[None, :] >= firsts[:, None]) & (openings[None, :] < firsts[:, None] + row_count)
    flags = jnp.any(inside, axis=1).astype(jnp.int32)
    spans = jnp.asarray([1 << (k // 2) for k in range(2 * rounds)], jnp.int32)
    tops = place - jnp.asarray([k % 2 for k in range(2 * rounds)], jnp.int32)
    lows = place - spans + 1
    covered = (ids[None, :] >= lows[:, None]) & (ids[None, :] <= tops[:, None])
    hits = jnp.sum(jnp.where(covered, flags[None, :], 0), axis=1)
    return (hits == 0).astype(jnp.float32)


def scan_kernel(n, rounds, s_ref, m_ref, xo_ref, e_ref, go_ref, parts, recv, send_sem, recv_sem,
                send_o, recv_o, send_x, recv_x, own):
    me = lax.axis_index("dp")
    col = lax.axis_index("mp")
    chips = n // 2
    side = me % 2
    chip = me // 2
    mate = me + 1 - 2 * side
    barrier = pltpu.get_barrier_semaphore()

    def each(lo, hi, body):
        def step(k, carry):
            body(k)
            return carry

        lax.fori_loop(lo, hi, step, 0)

    each(1, chips, lambda k: pl.semaphore_signal(
        barrier, 1, device_id=((me + 2 * k) % n, col), device_id_type=MESH))
    pl.semaphore_signal(barrier, 1, device_id=(mate, col), device_id_type=MESH)
    for k in range(rounds):
        d = 1 << k

        @pl.when(me + d < n)
        def _():
            pl.semaphore_signal(barrier, 1, device_id=(me + d, col), device_id_type=MESH)

        @pl.when(me >= d)
        def _():
            pl.semaphore_signal(barrier, 1, device_id=(me - d, col), device_id_type=MESH)

    peers = 0
    for k in range(rounds):
        d = 1 << k
        peers = peers + (me // d + n - 1) // n + ((n - 1 - me) // d + n - 1) // n
    pl.semaphore_wait(barrier, peers + chips)

    mine = pltpu.make_async_copy(xo_ref, go_ref.at[side, chip], own)
    mine.start()

    def to_far(k):
        return pltpu.make_async_remote_copy(
            src_ref=xo_ref,
            dst_ref=go_ref.at[side, chip],
            send_sem=send_o.at[k],
            recv_sem=recv_o.at[chip],
            device_id=((me + 2 * k) % n, col),
            device_id_type=MESH,
        )

    def from_far(k):
        other = (chip + chips - k) % chips
        return pltpu.make_async_remote_copy(
            src_ref=xo_ref,
            dst_ref=go_ref.at[side, other],
            send_sem=send_o.at[k],
            recv_sem=recv_o.at[other],
            device_id=(2 * other + side, col),
            device_id_type=MESH,
        )

    swap_out = pltpu.make_async_remote_copy(
        src_ref=go_ref.at[side],
        dst_ref=go_ref.at[side],
        send_sem=send_x,
        recv_sem=recv_x,
        device_id=(mate, col),
        device_id_type=MESH,
    )
    swap_in = pltpu.make_async_remote_copy(
        src_ref=go_ref.at[1 - side],
        dst_ref=go_ref.at[1 - side],
        send_sem=send_x,
        recv_sem=recv_x,
        device_id=(mate, col),
        device_id_type=MESH,
    )
    each(1, chips, lambda k: to_far(k).start())

    e_ref[...] = jnp.zeros_like(e_ref)
    copies = []
    for k in range(rounds):
        d = 1 << k
        src = s_ref if k == 0 else parts.at[k - 1]
        copy = pltpu.make_async_remote_copy(
            src_ref=src,
            dst_ref=recv.at[k],
            send_sem=send_sem.at[k],
            recv_sem=recv_sem.at[k],
            device_id=(me + d, col),
            device_id_type=MESH,
        )
        copies.append(copy)

        @pl.when(me + d < n)
        def _():
            copy.start()

        @pl.when(me >= d)
        def _():
            copy.wait_recv()
            got = recv[k].astype(jnp.float32)
            if k < rounds - 1:
                parts[k] = (src[...].astype(jnp.float32) + m_ref[2 * k] * got).astype(parts.dtype)
            e_ref[...] += m_ref[2 * k + 1] * got

        if k < rounds - 1:

            @pl.when(me < d)
            def _():
                parts[k] = src[...]

    each(1, chips, lambda k: from_far(k).wait_recv())
    mine.wait()
    swap_out.start()
    swap_in.wait_recv()
    each(1, chips, lambda k: to_far(k).wait_send())
    swap_out.wait_send()

    for k in range(rounds):
        d = 1 << k

        @pl.when(me + d < n)
        def _():
            copies[k].wait_send()


def carried_scan(summary, masks, piece, n, rounds):
    shape = summary.shape
    flat = summary.reshape(-1, shape[-1]).astype(jnp.bfloat16)
    size = flat.shape[0] * flat.shape[1]
    out, gathered = pl.pallas_call(
        functools.partial(scan_kernel, n, rounds),
        out_shape=(
            jax.ShapeDtypeStruct(flat.shape, jnp.float32),
            jax.ShapeDtypeStruct((2, n // 2) + piece.shape, piece.dtype),
        ),
        in_specs=[
            pl.BlockSpec(memory_space=pltpu.VMEM),
            pl.BlockSpec(memory_space=pltpu.SMEM),
            pl.BlockSpec(memory_space=pltpu.VMEM),
        ],
        out_specs=(pl.BlockSpec(memory_space=pltpu.VMEM), pl.BlockSpec(memory_space=pltpu.VMEM)),
        scratch_shapes=[
            pltpu.VMEM((max(rounds - 1, 1),) + flat.shape, jnp.bfloat16),
            pltpu.VMEM((rounds,) + flat.shape, jnp.bfloat16),
            pltpu.SemaphoreType.DMA((rounds,)),
            pltpu.SemaphoreType.DMA((rounds,)),
            pltpu.SemaphoreType.DMA((n // 2,)),
            pltpu.SemaphoreType.DMA((n // 2,)),
            pltpu.SemaphoreType.DMA(()),
            pltpu.SemaphoreType.DMA(()),
            pltpu.SemaphoreType.DMA(()),
        ],
        compiler_params=pltpu.CompilerParams(collective_id=0, has_side_effects=True),
        cost_estimate=pl.CostEstimate(
            flops=3 * rounds * size,
            bytes_accessed=6 * rounds * size + 2 * n * piece.size,
            transcendentals=0,
        ),
    )(flat, masks, piece)
    gathered = jnp.transpose(gathered, (1, 0, 2, 3)).reshape(n * piece.shape[0], piece.shape[1])
    return out.reshape(shape), gathered


def gather_kernel(n, m, xd_ref, xm_ref, early_ref, gd_ref, gm_ref, send_d, recv_d, send_x, recv_x, send_m, recv_m, own):
    me = lax.axis_index("dp")
    col = lax.axis_index("mp")
    chips = n // 2
    side = me % 2
    chip = me // 2
    mate = me + 1 - 2 * side
    barrier = pltpu.get_barrier_semaphore()

    def each(lo, hi, body):
        def step(k, carry):
            body(k)
            return carry

        lax.fori_loop(lo, hi, step, 0)

    each(1, chips, lambda k: pl.semaphore_signal(
        barrier, 1, device_id=((me + 2 * k) % n, col), device_id_type=MESH))
    pl.semaphore_signal(barrier, 1, device_id=(mate, col), device_id_type=MESH)
    each(1, m, lambda k: pl.semaphore_signal(
        barrier, 1, device_id=(me, (col + k) % m), device_id_type=MESH))
    pl.semaphore_wait(barrier, chips + m - 1)

    mine = pltpu.make_async_copy(xd_ref, gd_ref.at[side, chip], own)
    mine.start()

    def to_far(k):
        return pltpu.make_async_remote_copy(
            src_ref=xd_ref,
            dst_ref=gd_ref.at[side, chip],
            send_sem=send_d.at[k],
            recv_sem=recv_d.at[chip],
            device_id=((me + 2 * k) % n, col),
            device_id_type=MESH,
        )

    def from_far(k):
        other = (chip + chips - k) % chips
        return pltpu.make_async_remote_copy(
            src_ref=xd_ref,
            dst_ref=gd_ref.at[side, other],
            send_sem=send_d.at[k],
            recv_sem=recv_d.at[other],
            device_id=(2 * other + side, col),
            device_id_type=MESH,
        )

    swap_out = pltpu.make_async_remote_copy(
        src_ref=gd_ref.at[side],
        dst_ref=gd_ref.at[side],
        send_sem=send_x,
        recv_sem=recv_x,
        device_id=(mate, col),
        device_id_type=MESH,
    )
    swap_in = pltpu.make_async_remote_copy(
        src_ref=gd_ref.at[1 - side],
        dst_ref=gd_ref.at[1 - side],
        send_sem=send_x,
        recv_sem=recv_x,
        device_id=(mate, col),
        device_id_type=MESH,
    )

    def to_mp(k):
        return pltpu.make_async_remote_copy(
            src_ref=xm_ref,
            dst_ref=gm_ref.at[col],
            send_sem=send_m.at[k],
            recv_sem=recv_m.at[col],
            device_id=(me, (col + k) % m),
            device_id_type=MESH,
        )

    def from_mp(k):
        other = (col + m - k) % m
        return pltpu.make_async_remote_copy(
            src_ref=xm_ref,
            dst_ref=gm_ref.at[other],
            send_sem=send_m.at[k],
            recv_sem=recv_m.at[other],
            device_id=(me, other),
            device_id_type=MESH,
        )

    each(1, chips, lambda k: to_far(k).start())
    each(1, m, lambda k: to_mp(k).start())
    gm_ref[col] = xm_ref[...]
    each(1, chips, lambda k: from_far(k).wait_recv())
    mine.wait()
    swap_out.start()
    each(1, m, lambda k: from_mp(k).wait_recv())
    swap_in.wait_recv()
    each(1, chips, lambda k: to_far(k).wait_send())
    swap_out.wait_send()
    each(1, m, lambda k: to_mp(k).wait_send())


def direct_gather(xd, xm, early, n, m):
    moved = n * xd.size * 2 + m * xm.size * 2
    gd, gm = pl.pallas_call(
        functools.partial(gather_kernel, n, m),
        out_shape=(
            jax.ShapeDtypeStruct((2, n // 2) + xd.shape, xd.dtype),
            jax.ShapeDtypeStruct((m,) + xm.shape, xm.dtype),
        ),
        in_specs=[pl.BlockSpec(memory_space=pltpu.VMEM)] * 2 + [pl.BlockSpec(memory_space=pltpu.SMEM)],
        out_specs=(pl.BlockSpec(memory_space=pltpu.VMEM), pl.BlockSpec(memory_space=pltpu.VMEM)),
        scratch_shapes=[
            pltpu.SemaphoreType.DMA((n // 2,)),
            pltpu.SemaphoreType.DMA((n // 2,)),
            pltpu.SemaphoreType.DMA(()),
            pltpu.SemaphoreType.DMA(()),
            pltpu.SemaphoreType.DMA((m,)),
            pltpu.SemaphoreType.DMA((m,)),
            pltpu.SemaphoreType.DMA(()),
        ],
        compiler_params=pltpu.CompilerParams(collective_id=1, has_side_effects=True),
        cost_estimate=pl.CostEstimate(flops=0, bytes_accessed=moved, transcendentals=0),
    )(xd, xm, early)
    return jnp.transpose(gd, (1, 0, 2, 3)), gm


def ring_kernel(m, n_ref, w_ref, o_ref, acc_a, acc_b, got_a, got_b, send_a, recv_a, send_b, recv_b):
    me = lax.axis_index("dp")
    col = lax.axis_index("mp")
    right = (col + 1) % m
    left = (col + m - 1) % m
    half = o_ref.shape[2]
    width = 2 * half
    barrier = pltpu.get_barrier_semaphore()
    pl.semaphore_signal(barrier, 1, device_id=(me, right), device_id_type=MESH)
    pl.semaphore_signal(barrier, 1, device_id=(me, left), device_id_type=MESH)
    pl.semaphore_wait(barrier, 2)

    def own(t, side):
        rows = w_ref[pl.ds(pl.multiple_of(t * width + side * half, half), half), :]
        return lax.dot_general(
            n_ref[...], rows, (((1,), (1,)), ((), ())), preferred_element_type=jnp.float32
        )

    copies = []
    for s in range(m - 1):
        ta = (col + 2 * m - 1 - s) % m
        tb = (col + 1 + s) % m
        part_a = own(ta, 0)
        part_b = own(tb, 1)
        if s > 0:
            copies[-1][0].wait_recv()
            part_a = part_a + got_a[s - 1].astype(jnp.float32)
        acc_a[s] = part_a.astype(acc_a.dtype)
        ca = pltpu.make_async_remote_copy(
            src_ref=acc_a.at[s],
            dst_ref=got_a.at[s],
            send_sem=send_a.at[s],
            recv_sem=recv_a.at[s],
            device_id=(me, right),
            device_id_type=MESH,
        )
        ca.start()
        if s > 0:
            copies[-1][1].wait_recv()
            part_b = part_b + got_b[s - 1].astype(jnp.float32)
        acc_b[s] = part_b.astype(acc_b.dtype)
        cb = pltpu.make_async_remote_copy(
            src_ref=acc_b.at[s],
            dst_ref=got_b.at[s],
            send_sem=send_b.at[s],
            recv_sem=recv_b.at[s],
            device_id=(me, left),
            device_id_type=MESH,
        )
        cb.start()
        copies.append((ca, cb))
    copies[-1][0].wait_recv()
    copies[-1][1].wait_recv()
    o_ref[0] = got_a[m - 2]
    o_ref[1] = got_b[m - 2]
    for ca, cb in copies:
        ca.wait_send()
        cb.wait_send()


def ring_scatter(normed, out_t, m):
    rows = normed.shape[0]
    total = out_t.shape[0]
    width = total // m
    half = width // 2
    slot = (m - 1, rows, half)
    got = pl.pallas_call(
        functools.partial(ring_kernel, m),
        out_shape=jax.ShapeDtypeStruct((2, rows, half), jnp.bfloat16),
        in_specs=[pl.BlockSpec(memory_space=pltpu.VMEM)] * 2,
        out_specs=pl.BlockSpec(memory_space=pltpu.VMEM),
        scratch_shapes=[
            pltpu.VMEM(slot, jnp.bfloat16),
            pltpu.VMEM(slot, jnp.bfloat16),
            pltpu.VMEM(slot, jnp.bfloat16),
            pltpu.VMEM(slot, jnp.bfloat16),
            pltpu.SemaphoreType.DMA((m - 1,)),
            pltpu.SemaphoreType.DMA((m - 1,)),
            pltpu.SemaphoreType.DMA((m - 1,)),
            pltpu.SemaphoreType.DMA((m - 1,)),
        ],
        compiler_params=pltpu.CompilerParams(collective_id=2, has_side_effects=True),
        cost_estimate=pl.CostEstimate(
            flops=2 * rows * normed.shape[1] * total,
            bytes_accessed=2 * (normed.size + out_t.size) + 4 * rows * total,
            transcendentals=0,
        ),
    )(normed, out_t)
    col = lax.axis_index("mp")
    mine = lax.dynamic_slice_in_dim(out_t, col * width, width, axis=0)
    own = lax.dot_general(normed, mine, (((1,), (1,)), ((), ())), preferred_element_type=jnp.float32)
    got = jnp.concatenate([got[0], got[1]], axis=1).astype(jnp.float32)
    return (got + own).astype(jnp.bfloat16)


def per_device(
    tokens,
    q_weight,
    k_weight,
    v_weight,
    adapter_down,
    adapter_up,
    lengths,
    adapter_ids,
    head_gain,
    out_weight,
):
    row_count = tokens.shape[0]
    qf = q_weight.shape[1]
    heads_here = qf // F
    vw = v_weight.shape[1]
    value_width = vw // heads_here
    blocks = lax.axis_size("dp")
    place = lax.axis_index("dp")
    positions = place * row_count + jnp.arange(row_count, dtype=jnp.int32)
    request, starts, adapter = token_tables(lengths, adapter_ids, positions)

    local = jnp.concatenate([q_weight, k_weight, v_weight], axis=1)
    part_low = jnp.dot(tokens, adapter_down, preferred_element_type=jnp.float32)
    owners = lax.axis_index("mp") * (adapter_down.shape[1] // R) + (
        jnp.arange(adapter_down.shape[1], dtype=jnp.int32) // R
    )
    part_low = jnp.where(adapter[:, None] == owners[None, :], part_low, 0.0).astype(jnp.bfloat16)
    cols = lax.axis_size("mp")
    rounds = max(1, (blocks - 1).bit_length())
    masks = scan_masks(lengths, row_count, place, blocks, rounds)
    gathered, low_parts = direct_gather(local, part_low, masks, blocks, cols)
    gathered = gathered.reshape(blocks * local.shape[0], local.shape[1])
    q_full = gathered[:, :qf]
    k_full = gathered[:, qf : 2 * qf]
    v_full = gathered[:, 2 * qf :]
    low_rank = jnp.transpose(low_parts, (1, 0, 2)).reshape(row_count, cols * part_low.shape[1])

    query_sum = jnp.dot(tokens, q_full, preferred_element_type=jnp.float32)
    key_sum = jnp.dot(tokens, k_full, preferred_element_type=jnp.float32)
    value_sum = jnp.dot(tokens, v_full, preferred_element_type=jnp.float32)
    query = query_sum.astype(jnp.bfloat16).reshape(row_count, heads_here, F)
    key_rows = key_sum.astype(jnp.bfloat16).reshape(row_count, heads_here, F)
    values = value_sum + jnp.dot(low_rank, adapter_up, preferred_element_type=jnp.float32)
    values = values.astype(jnp.bfloat16).reshape(row_count, heads_here, value_width)
    within, query_map, summary = block_local(query, key_rows, values, request, starts)

    carried, out_t = carried_scan(summary, masks, out_weight.T, blocks, rounds)

    gains = head_gain.reshape(heads_here, value_width)
    normed = finish(within, query_map, carried, request, starts, gains).reshape(
        row_count, heads_here * value_width
    )
    return ring_scatter(normed, out_t, cols)


def solution(mesh):
    placed = (
        P("dp", None),
        P("dp", "mp"),
        P("dp", "mp"),
        P("dp", "mp"),
        P(None, "mp"),
        P(None, "mp"),
        P(),
        P(),
        P("mp"),
        P("mp", "dp"),
    )
    return jax.shard_map(
        per_device, mesh=mesh, in_specs=placed, out_specs=P("dp", "mp"), check_vma=False
    )
```

```python
import math

import functools

import jax
import jax.numpy as jnp
import numpy as np
from jax import lax
from jax.experimental import pallas as pl
from jax.experimental.pallas import tpu as pltpu
from jax.sharding import PartitionSpec as P

MESH = pl.DeviceIdType.MESH

F = 16
R = 16


EPSILON = 1e-05


def taylor(inputs):
    squares = (inputs[..., :, None] * inputs[..., None, :]).reshape(
        inputs.shape[:-1] + (inputs.shape[-1] * inputs.shape[-1],)
    )
    constant = jnp.ones(inputs.shape[:-1] + (1,), jnp.float32)
    return jnp.concatenate([constant, 0.5 * inputs, squares * (0.25 / math.sqrt(2.0))], axis=-1)


def packed_taylor(inputs):
    width = inputs.shape[-1]
    squares = [inputs[..., a : a + 1] * inputs[..., a:] for a in range(width)]
    constant = jnp.ones(inputs.shape[:-1] + (1,), jnp.float32)
    return jnp.concatenate(
        [constant, 0.5 * inputs] + [s * (0.25 / math.sqrt(2.0)) for s in squares], axis=-1
    )


def packed_features(width):
    index, weight = list(range(1 + width)), [1.0] * (1 + width)
    for a in range(width):
        for b in range(a, width):
            index.append(1 + width + a * width + b)
            weight.append(1.0 if a == b else 2.0)
    return np.asarray(index, np.int32), np.asarray(weight, np.float32)


def request_of(bounds, positions):
    return jnp.sum((positions[:, None] >= bounds[None, :]).astype(jnp.int32), axis=1)


def token_tables(lengths, adapter_ids, positions):
    bounds = jnp.cumsum(lengths)
    request = request_of(bounds, positions)
    openings = bounds - lengths
    starts = jnp.any(positions[:, None] == openings[None, :], axis=1)
    picked = request[:, None] == jnp.arange(lengths.shape[0], dtype=jnp.int32)[None, :]
    adapter = jnp.sum(jnp.where(picked, adapter_ids[None, :], 0), axis=1)
    return (request, starts, adapter)


def block_local(query, key_rows, values, request, starts):
    scores = jnp.einsum("ihd,jhd->hij", query, key_rows, preferred_element_type=jnp.float32) * 0.25
    weights = 1.0 + scores + 0.5 * scores * scores
    indexes = jnp.arange(request.shape[0], dtype=jnp.int32)
    allowed = (indexes[None, :] <= indexes[:, None]) & (request[None, :] == request[:, None])
    weights = jnp.where(allowed[None], weights, 0.0).astype(jnp.bfloat16)
    within = jnp.einsum("hij,jhe->ihe", weights, values, preferred_element_type=jnp.float32)
    index, weight = packed_features(query.shape[-1])
    query_map = taylor(query.astype(jnp.float32)).astype(jnp.bfloat16)
    query_map = query_map[..., index] * jnp.asarray(weight, jnp.bfloat16)
    key_map = packed_taylor(key_rows.astype(jnp.float32)).astype(jnp.bfloat16)
    tail_mask = (request == request[-1]).astype(jnp.bfloat16)
    masked_keys = key_map * tail_mask[:, None, None]
    summary = jnp.einsum("ihf,ihe->hfe", masked_keys, values, preferred_element_type=jnp.float32)
    return (within, query_map, summary)


def finish(within, query_map, carried, request, starts, gains):
    follows = ((request == request[0]) & jnp.logical_not(starts[0])).astype(jnp.float32)
    cross = jnp.einsum(
        "ihf,hfe->ihe", query_map, carried.astype(jnp.bfloat16), preferred_element_type=jnp.float32
    )
    combined = within + follows[:, None, None] * cross
    factor = lax.rsqrt(jnp.mean(combined * combined, axis=-1, keepdims=True) + EPSILON)
    return (combined * factor * gains[None]).astype(jnp.bfloat16)


def scan_masks(lengths, row_count, place, blocks, rounds):
    openings = jnp.cumsum(lengths) - lengths
    ids = jnp.arange(blocks, dtype=jnp.int32)
    firsts = ids * row_count
    inside = (openings[None, :] >= firsts[:, None]) & (openings[None, :] < firsts[:, None] + row_count)
    flags = jnp.any(inside, axis=1).astype(jnp.int32)
    spans = jnp.asarray([1 << (k // 2) for k in range(2 * rounds)], jnp.int32)
    tops = place - jnp.asarray([k % 2 for k in range(2 * rounds)], jnp.int32)
    lows = place - spans + 1
    covered = (ids[None, :] >= lows[:, None]) & (ids[None, :] <= tops[:, None])
    hits = jnp.sum(jnp.where(covered, flags[None, :], 0), axis=1)
    return (hits == 0).astype(jnp.float32)


def scan_kernel(n, rounds, s_ref, m_ref, xo_ref, e_ref, go_ref, parts, recv, send_sem, recv_sem,
                send_o, recv_o, send_x, recv_x, own):
    me = lax.axis_index("dp")
    col = lax.axis_index("mp")
    chips = n // 2
    side = me % 2
    chip = me // 2
    mate = me + 1 - 2 * side
    barrier = pltpu.get_barrier_semaphore()

    def each(lo, hi, body):
        def step(k, carry):
            body(k)
            return carry

        lax.fori_loop(lo, hi, step, 0)

    each(1, chips, lambda k: pl.semaphore_signal(
        barrier, 1, device_id=((me + 2 * k) % n, col), device_id_type=MESH))
    pl.semaphore_signal(barrier, 1, device_id=(mate, col), device_id_type=MESH)
    for k in range(rounds):
        d = 1 << k

        @pl.when(me + d < n)
        def _():
            pl.semaphore_signal(barrier, 1, device_id=(me + d, col), device_id_type=MESH)

        @pl.when(me >= d)
        def _():
            pl.semaphore_signal(barrier, 1, device_id=(me - d, col), device_id_type=MESH)

    peers = 0
    for k in range(rounds):
        d = 1 << k
        peers = peers + (me // d + n - 1) // n + ((n - 1 - me) // d + n - 1) // n
    pl.semaphore_wait(barrier, peers + chips)

    mine = pltpu.make_async_copy(xo_ref, go_ref.at[side, chip], own)
    mine.start()

    def to_far(k):
        return pltpu.make_async_remote_copy(
            src_ref=xo_ref,
            dst_ref=go_ref.at[side, chip],
            send_sem=send_o.at[k],
            recv_sem=recv_o.at[chip],
            device_id=((me + 2 * k) % n, col),
            device_id_type=MESH,
        )

    def from_far(k):
        other = (chip + chips - k) % chips
        return pltpu.make_async_remote_copy(
            src_ref=xo_ref,
            dst_ref=go_ref.at[side, other],
            send_sem=send_o.at[k],
            recv_sem=recv_o.at[other],
            device_id=(2 * other + side, col),
            device_id_type=MESH,
        )

    swap_out = pltpu.make_async_remote_copy(
        src_ref=go_ref.at[side],
        dst_ref=go_ref.at[side],
        send_sem=send_x,
        recv_sem=recv_x,
        device_id=(mate, col),
        device_id_type=MESH,
    )
    swap_in = pltpu.make_async_remote_copy(
        src_ref=go_ref.at[1 - side],
        dst_ref=go_ref.at[1 - side],
        send_sem=send_x,
        recv_sem=recv_x,
        device_id=(mate, col),
        device_id_type=MESH,
    )
    each(1, chips, lambda k: to_far(k).start())

    e_ref[...] = jnp.zeros_like(e_ref)
    copies = []
    for k in range(rounds):
        d = 1 << k
        src = s_ref if k == 0 else parts.at[k - 1]
        copy = pltpu.make_async_remote_copy(
            src_ref=src,
            dst_ref=recv.at[k],
            send_sem=send_sem.at[k],
            recv_sem=recv_sem.at[k],
            device_id=(me + d, col),
            device_id_type=MESH,
        )
        copies.append(copy)

        @pl.when(me + d < n)
        def _():
            copy.start()

        @pl.when(me >= d)
        def _():
            copy.wait_recv()
            got = recv[k].astype(jnp.float32)
            if k < rounds - 1:
                parts[k] = (src[...].astype(jnp.float32) + m_ref[2 * k] * got).astype(parts.dtype)
            e_ref[...] += m_ref[2 * k + 1] * got

        if k < rounds - 1:

            @pl.when(me < d)
            def _():
                parts[k] = src[...]

    each(1, chips, lambda k: from_far(k).wait_recv())
    mine.wait()
    swap_out.start()
    swap_in.wait_recv()
    each(1, chips, lambda k: to_far(k).wait_send())
    swap_out.wait_send()

    for k in range(rounds):
        d = 1 << k

        @pl.when(me + d < n)
        def _():
            copies[k].wait_send()


def carried_scan(summary, masks, piece, n, rounds):
    shape = summary.shape
    flat = summary.reshape(-1, shape[-1]).astype(jnp.bfloat16)
    size = flat.shape[0] * flat.shape[1]
    out, gathered = pl.pallas_call(
        functools.partial(scan_kernel, n, rounds),
        out_shape=(
            jax.ShapeDtypeStruct(flat.shape, jnp.float32),
            jax.ShapeDtypeStruct((2, n // 2) + piece.shape, piece.dtype),
        ),
        in_specs=[
            pl.BlockSpec(memory_space=pltpu.VMEM),
            pl.BlockSpec(memory_space=pltpu.SMEM),
            pl.BlockSpec(memory_space=pltpu.VMEM),
        ],
        out_specs=(pl.BlockSpec(memory_space=pltpu.VMEM), pl.BlockSpec(memory_space=pltpu.VMEM)),
        scratch_shapes=[
            pltpu.VMEM((max(rounds - 1, 1),) + flat.shape, jnp.bfloat16),
            pltpu.VMEM((rounds,) + flat.shape, jnp.bfloat16),
            pltpu.SemaphoreType.DMA((rounds,)),
            pltpu.SemaphoreType.DMA((rounds,)),
            pltpu.SemaphoreType.DMA((n // 2,)),
            pltpu.SemaphoreType.DMA((n // 2,)),
            pltpu.SemaphoreType.DMA(()),
            pltpu.SemaphoreType.DMA(()),
            pltpu.SemaphoreType.DMA(()),
        ],
        compiler_params=pltpu.CompilerParams(collective_id=0, has_side_effects=True),
        cost_estimate=pl.CostEstimate(
            flops=3 * rounds * size,
            bytes_accessed=6 * rounds * size + 2 * n * piece.size,
            transcendentals=0,
        ),
    )(flat, masks, piece)
    gathered = jnp.transpose(gathered, (1, 0, 2, 3)).reshape(n * piece.shape[0], piece.shape[1])
    return out.reshape(shape), gathered


def gather_kernel(n, m, xd_ref, xm_ref, early_ref, gd_ref, gm_ref, send_d, recv_d, send_x, recv_x, send_m, recv_m, own):
    me = lax.axis_index("dp")
    col = lax.axis_index("mp")
    chips = n // 2
    side = me % 2
    chip = me // 2
    mate = me + 1 - 2 * side
    barrier = pltpu.get_barrier_semaphore()

    def each(lo, hi, body):
        def step(k, carry):
            body(k)
            return carry

        lax.fori_loop(lo, hi, step, 0)

    each(1, chips, lambda k: pl.semaphore_signal(
        barrier, 1, device_id=((me + 2 * k) % n, col), device_id_type=MESH))
    pl.semaphore_signal(barrier, 1, device_id=(mate, col), device_id_type=MESH)
    each(1, m, lambda k: pl.semaphore_signal(
        barrier, 1, device_id=(me, (col + k) % m), device_id_type=MESH))
    pl.semaphore_wait(barrier, chips + m - 1)

    mine = pltpu.make_async_copy(xd_ref, gd_ref.at[side, chip], own)
    mine.start()

    def to_far(k):
        return pltpu.make_async_remote_copy(
            src_ref=xd_ref,
            dst_ref=gd_ref.at[side, chip],
            send_sem=send_d.at[k],
            recv_sem=recv_d.at[chip],
            device_id=((me + 2 * k) % n, col),
            device_id_type=MESH,
        )

    def from_far(k):
        other = (chip + chips - k) % chips
        return pltpu.make_async_remote_copy(
            src_ref=xd_ref,
            dst_ref=gd_ref.at[side, other],
            send_sem=send_d.at[k],
            recv_sem=recv_d.at[other],
            device_id=(2 * other + side, col),
            device_id_type=MESH,
        )

    swap_out = pltpu.make_async_remote_copy(
        src_ref=gd_ref.at[side],
        dst_ref=gd_ref.at[side],
        send_sem=send_x,
        recv_sem=recv_x,
        device_id=(mate, col),
        device_id_type=MESH,
    )
    swap_in = pltpu.make_async_remote_copy(
        src_ref=gd_ref.at[1 - side],
        dst_ref=gd_ref.at[1 - side],
        send_sem=send_x,
        recv_sem=recv_x,
        device_id=(mate, col),
        device_id_type=MESH,
    )

    def to_mp(k):
        return pltpu.make_async_remote_copy(
            src_ref=xm_ref,
            dst_ref=gm_ref.at[col],
            send_sem=send_m.at[k],
            recv_sem=recv_m.at[col],
            device_id=(me, (col + k) % m),
            device_id_type=MESH,
        )

    def from_mp(k):
        other = (col + m - k) % m
        return pltpu.make_async_remote_copy(
            src_ref=xm_ref,
            dst_ref=gm_ref.at[other],
            send_sem=send_m.at[k],
            recv_sem=recv_m.at[other],
            device_id=(me, other),
            device_id_type=MESH,
        )

    each(1, chips, lambda k: to_far(k).start())
    each(1, m, lambda k: to_mp(k).start())
    gm_ref[col] = xm_ref[...]
    each(1, chips, lambda k: from_far(k).wait_recv())
    mine.wait()
    swap_out.start()
    each(1, m, lambda k: from_mp(k).wait_recv())
    swap_in.wait_recv()
    each(1, chips, lambda k: to_far(k).wait_send())
    swap_out.wait_send()
    each(1, m, lambda k: to_mp(k).wait_send())


def direct_gather(xd, xm, early, n, m):
    moved = n * xd.size * 2 + m * xm.size * 2
    gd, gm = pl.pallas_call(
        functools.partial(gather_kernel, n, m),
        out_shape=(
            jax.ShapeDtypeStruct((2, n // 2) + xd.shape, xd.dtype),
            jax.ShapeDtypeStruct((m,) + xm.shape, xm.dtype),
        ),
        in_specs=[pl.BlockSpec(memory_space=pltpu.VMEM)] * 2 + [pl.BlockSpec(memory_space=pltpu.SMEM)],
        out_specs=(pl.BlockSpec(memory_space=pltpu.VMEM), pl.BlockSpec(memory_space=pltpu.VMEM)),
        scratch_shapes=[
            pltpu.SemaphoreType.DMA((n // 2,)),
            pltpu.SemaphoreType.DMA((n // 2,)),
            pltpu.SemaphoreType.DMA(()),
            pltpu.SemaphoreType.DMA(()),
            pltpu.SemaphoreType.DMA((m,)),
            pltpu.SemaphoreType.DMA((m,)),
            pltpu.SemaphoreType.DMA(()),
        ],
        compiler_params=pltpu.CompilerParams(collective_id=1, has_side_effects=True),
        cost_estimate=pl.CostEstimate(flops=0, bytes_accessed=moved, transcendentals=0),
    )(xd, xm, early)
    return jnp.transpose(gd, (1, 0, 2, 3)), gm


def ring_kernel(m, n_ref, w_ref, o_ref, acc_a, acc_b, got_a, got_b, send_a, recv_a, send_b, recv_b):
    me = lax.axis_index("dp")
    col = lax.axis_index("mp")
    right = (col + 1) % m
    left = (col + m - 1) % m
    half = o_ref.shape[2]
    width = 2 * half
    barrier = pltpu.get_barrier_semaphore()
    pl.semaphore_signal(barrier, 1, device_id=(me, right), device_id_type=MESH)
    pl.semaphore_signal(barrier, 1, device_id=(me, left), device_id_type=MESH)
    pl.semaphore_wait(barrier, 2)

    def own(t, side):
        rows = w_ref[pl.ds(pl.multiple_of(t * width + side * half, half), half), :]
        return lax.dot_general(
            n_ref[...], rows, (((1,), (1,)), ((), ())), preferred_element_type=jnp.float32
        )

    copies = []
    for s in range(m - 1):
        ta = (col + 2 * m - 1 - s) % m
        tb = (col + 1 + s) % m
        part_a = own(ta, 0)
        part_b = own(tb, 1)
        if s > 0:
            copies[-1][0].wait_recv()
            part_a = part_a + got_a[s - 1].astype(jnp.float32)
        acc_a[s] = part_a.astype(acc_a.dtype)
        ca = pltpu.make_async_remote_copy(
            src_ref=acc_a.at[s],
            dst_ref=got_a.at[s],
            send_sem=send_a.at[s],
            recv_sem=recv_a.at[s],
            device_id=(me, right),
            device_id_type=MESH,
        )
        ca.start()
        if s > 0:
            copies[-1][1].wait_recv()
            part_b = part_b + got_b[s - 1].astype(jnp.float32)
        acc_b[s] = part_b.astype(acc_b.dtype)
        cb = pltpu.make_async_remote_copy(
            src_ref=acc_b.at[s],
            dst_ref=got_b.at[s],
            send_sem=send_b.at[s],
            recv_sem=recv_b.at[s],
            device_id=(me, left),
            device_id_type=MESH,
        )
        cb.start()
        copies.append((ca, cb))
    copies[-1][0].wait_recv()
    copies[-1][1].wait_recv()
    o_ref[0] = got_a[m - 2]
    o_ref[1] = got_b[m - 2]
    for ca, cb in copies:
        ca.wait_send()
        cb.wait_send()


def ring_scatter(normed, out_t, m):
    rows = normed.shape[0]
    total = out_t.shape[0]
    width = total // m
    half = width // 2
    slot = (m - 1, rows, half)
    got = pl.pallas_call(
        functools.partial(ring_kernel, m),
        out_shape=jax.ShapeDtypeStruct((2, rows, half), jnp.bfloat16),
        in_specs=[pl.BlockSpec(memory_space=pltpu.VMEM)] * 2,
        out_specs=pl.BlockSpec(memory_space=pltpu.VMEM),
        scratch_shapes=[
            pltpu.VMEM(slot, jnp.bfloat16),
            pltpu.VMEM(slot, jnp.bfloat16),
            pltpu.VMEM(slot, jnp.bfloat16),
            pltpu.VMEM(slot, jnp.bfloat16),
            pltpu.SemaphoreType.DMA((m - 1,)),
            pltpu.SemaphoreType.DMA((m - 1,)),
            pltpu.SemaphoreType.DMA((m - 1,)),
            pltpu.SemaphoreType.DMA((m - 1,)),
        ],
        compiler_params=pltpu.CompilerParams(collective_id=2, has_side_effects=True),
        cost_estimate=pl.CostEstimate(
            flops=2 * rows * normed.shape[1] * total,
            bytes_accessed=2 * (normed.size + out_t.size) + 4 * rows * total,
            transcendentals=0,
        ),
    )(normed, out_t)
    col = lax.axis_index("mp")
    mine = lax.dynamic_slice_in_dim(out_t, col * width, width, axis=0)
    own = lax.dot_general(normed, mine, (((1,), (1,)), ((), ())), preferred_element_type=jnp.float32)
    got = jnp.concatenate([got[0], got[1]], axis=1).astype(jnp.float32)
    return (got + own).astype(jnp.bfloat16)


def per_device(
    tokens,
    q_weight,
    k_weight,
    v_weight,
    adapter_down,
    adapter_up,
    lengths,
    adapter_ids,
    head_gain,
    out_weight,
):
    row_count = tokens.shape[0]
    qf = q_weight.shape[1]
    heads_here = qf // F
    vw = v_weight.shape[1]
    value_width = vw // heads_here
    blocks = lax.axis_size("dp")
    place = lax.axis_index("dp")
    positions = place * row_count + jnp.arange(row_count, dtype=jnp.int32)
    request, starts, adapter = token_tables(lengths, adapter_ids, positions)

    local = jnp.concatenate([q_weight, k_weight, v_weight], axis=1)
    part_low = jnp.dot(tokens, adapter_down, preferred_element_type=jnp.float32)
    owners = lax.axis_index("mp") * (adapter_down.shape[1] // R) + (
        jnp.arange(adapter_down.shape[1], dtype=jnp.int32) // R
    )
    part_low = jnp.where(adapter[:, None] == owners[None, :], part_low, 0.0).astype(jnp.bfloat16)
    cols = lax.axis_size("mp")
    rounds = max(1, (blocks - 1).bit_length())
    masks = scan_masks(lengths, row_count, place, blocks, rounds)
    gathered, low_parts = direct_gather(local, part_low, masks, blocks, cols)
    gathered = gathered.reshape(blocks * local.shape[0], local.shape[1])
    q_full = gathered[:, :qf]
    k_full = gathered[:, qf : 2 * qf]
    v_full = gathered[:, 2 * qf :]
    low_rank = jnp.transpose(low_parts, (1, 0, 2)).reshape(row_count, cols * part_low.shape[1])

    query_sum = jnp.dot(tokens, q_full, preferred_element_type=jnp.float32)
    key_sum = jnp.dot(tokens, k_full, preferred_element_type=jnp.float32)
    value_sum = jnp.dot(tokens, v_full, preferred_element_type=jnp.float32)
    query = query_sum.astype(jnp.bfloat16).reshape(row_count, heads_here, F)
    key_rows = key_sum.astype(jnp.bfloat16).reshape(row_count, heads_here, F)
    values = value_sum + jnp.dot(low_rank, adapter_up, preferred_element_type=jnp.float32)
    values = values.astype(jnp.bfloat16).reshape(row_count, heads_here, value_width)
    within, query_map, summary = block_local(query, key_rows, values, request, starts)

    carried, out_t = carried_scan(summary, masks, out_weight.T, blocks, rounds)

    gains = head_gain.reshape(heads_here, value_width)
    normed = finish(within, query_map, carried, request, starts, gains).reshape(
        row_count, heads_here * value_width
    )
    return ring_scatter(normed, out_t, cols)


def solution(mesh):
    placed = (
        P("dp", None),
        P("dp", "mp"),
        P("dp", "mp"),
        P("dp", "mp"),
        P(None, "mp"),
        P(None, "mp"),
        P(),
        P(),
        P("mp"),
        P("mp", "dp"),
    )
    return jax.shard_map(
        per_device, mesh=mesh, in_specs=placed, out_specs=P("dp", "mp"), check_vma=False
    )
```

```python
import math

import functools

import jax
import jax.numpy as jnp
import numpy as np
from jax import lax
from jax.experimental import pallas as pl
from jax.experimental.pallas import tpu as pltpu
from jax.sharding import PartitionSpec as P

MESH = pl.DeviceIdType.MESH

F = 16
R = 16


EPSILON = 1e-05


def taylor(inputs):
    squares = (inputs[..., :, None] * inputs[..., None, :]).reshape(
        inputs.shape[:-1] + (inputs.shape[-1] * inputs.shape[-1],)
    )
    constant = jnp.ones(inputs.shape[:-1] + (1,), jnp.float32)
    return jnp.concatenate([constant, 0.5 * inputs, squares * (0.25 / math.sqrt(2.0))], axis=-1)


def packed_taylor(inputs):
    width = inputs.shape[-1]
    squares = [inputs[..., a : a + 1] * inputs[..., a:] for a in range(width)]
    constant = jnp.ones(inputs.shape[:-1] + (1,), jnp.float32)
    return jnp.concatenate(
        [constant, 0.5 * inputs] + [s * (0.25 / math.sqrt(2.0)) for s in squares], axis=-1
    )


def packed_features(width):
    index, weight = list(range(1 + width)), [1.0] * (1 + width)
    for a in range(width):
        for b in range(a, width):
            index.append(1 + width + a * width + b)
            weight.append(1.0 if a == b else 2.0)
    return np.asarray(index, np.int32), np.asarray(weight, np.float32)


def request_of(bounds, positions):
    return jnp.sum((positions[:, None] >= bounds[None, :]).astype(jnp.int32), axis=1)


def token_tables(lengths, adapter_ids, positions):
    bounds = jnp.cumsum(lengths)
    request = request_of(bounds, positions)
    openings = bounds - lengths
    starts = jnp.any(positions[:, None] == openings[None, :], axis=1)
    picked = request[:, None] == jnp.arange(lengths.shape[0], dtype=jnp.int32)[None, :]
    adapter = jnp.sum(jnp.where(picked, adapter_ids[None, :], 0), axis=1)
    return (request, starts, adapter)


def block_local(query, key_rows, values, request, starts):
    scores = jnp.einsum("ihd,jhd->hij", query, key_rows, preferred_element_type=jnp.float32) * 0.25
    weights = 1.0 + scores + 0.5 * scores * scores
    indexes = jnp.arange(request.shape[0], dtype=jnp.int32)
    allowed = (indexes[None, :] <= indexes[:, None]) & (request[None, :] == request[:, None])
    weights = jnp.where(allowed[None], weights, 0.0).astype(jnp.bfloat16)
    within = jnp.einsum("hij,jhe->ihe", weights, values, preferred_element_type=jnp.float32)
    query_map = packed_taylor(query.astype(jnp.float32)).astype(jnp.bfloat16)
    key_map = packed_taylor(key_rows.astype(jnp.float32)).astype(jnp.bfloat16)
    tail_mask = (request == request[-1]).astype(jnp.bfloat16)
    masked_keys = key_map * tail_mask[:, None, None]
    summary = jnp.einsum("ihf,ihe->hfe", masked_keys, values, preferred_element_type=jnp.float32)
    return (within, query_map, summary)


def finish(within, query_map, carried, request, starts, gains):
    follows = ((request == request[0]) & jnp.logical_not(starts[0])).astype(jnp.float32)
    _, weight = packed_features(F)
    pairs = carried.astype(jnp.bfloat16) * jnp.asarray(weight, jnp.bfloat16)[None, :, None]
    cross = jnp.einsum("ihf,hfe->ihe", query_map, pairs, preferred_element_type=jnp.float32)
    combined = within + follows[:, None, None] * cross
    factor = lax.rsqrt(jnp.mean(combined * combined, axis=-1, keepdims=True) + EPSILON)
    return (combined * factor * gains[None]).astype(jnp.bfloat16)


def scan_masks(lengths, row_count, place, blocks, rounds):
    openings = jnp.cumsum(lengths) - lengths
    ids = jnp.arange(blocks, dtype=jnp.int32)
    firsts = ids * row_count
    inside = (openings[None, :] >= firsts[:, None]) & (openings[None, :] < firsts[:, None] + row_count)
    flags = jnp.any(inside, axis=1).astype(jnp.int32)
    spans = jnp.asarray([1 << (k // 2) for k in range(2 * rounds)], jnp.int32)
    tops = place - jnp.asarray([k % 2 for k in range(2 * rounds)], jnp.int32)
    lows = place - spans + 1
    covered = (ids[None, :] >= lows[:, None]) & (ids[None, :] <= tops[:, None])
    hits = jnp.sum(jnp.where(covered, flags[None, :], 0), axis=1)
    return (hits == 0).astype(jnp.float32)


def scan_kernel(n, rounds, s_ref, m_ref, xo_ref, e_ref, go_ref, parts, recv, send_sem, recv_sem,
                send_o, recv_o, send_x, recv_x, own):
    me = lax.axis_index("dp")
    col = lax.axis_index("mp")
    chips = n // 2
    side = me % 2
    chip = me // 2
    mate = me + 1 - 2 * side
    barrier = pltpu.get_barrier_semaphore()

    def each(lo, hi, body):
        def step(k, carry):
            body(k)
            return carry

        lax.fori_loop(lo, hi, step, 0)

    each(1, chips, lambda k: pl.semaphore_signal(
        barrier, 1, device_id=((me + 2 * k) % n, col), device_id_type=MESH))
    pl.semaphore_signal(barrier, 1, device_id=(mate, col), device_id_type=MESH)
    for k in range(rounds):
        d = 1 << k

        @pl.when(me + d < n)
        def _():
            pl.semaphore_signal(barrier, 1, device_id=(me + d, col), device_id_type=MESH)

        @pl.when(me >= d)
        def _():
            pl.semaphore_signal(barrier, 1, device_id=(me - d, col), device_id_type=MESH)

    peers = 0
    for k in range(rounds):
        d = 1 << k
        peers = peers + (me // d + n - 1) // n + ((n - 1 - me) // d + n - 1) // n
    pl.semaphore_wait(barrier, peers + chips)

    mine = pltpu.make_async_copy(xo_ref, go_ref.at[side, chip], own)
    mine.start()

    def to_far(k):
        return pltpu.make_async_remote_copy(
            src_ref=xo_ref,
            dst_ref=go_ref.at[side, chip],
            send_sem=send_o.at[k],
            recv_sem=recv_o.at[chip],
            device_id=((me + 2 * k) % n, col),
            device_id_type=MESH,
        )

    def from_far(k):
        other = (chip + chips - k) % chips
        return pltpu.make_async_remote_copy(
            src_ref=xo_ref,
            dst_ref=go_ref.at[side, other],
            send_sem=send_o.at[k],
            recv_sem=recv_o.at[other],
            device_id=(2 * other + side, col),
            device_id_type=MESH,
        )

    swap_out = pltpu.make_async_remote_copy(
        src_ref=go_ref.at[side],
        dst_ref=go_ref.at[side],
        send_sem=send_x,
        recv_sem=recv_x,
        device_id=(mate, col),
        device_id_type=MESH,
    )
    swap_in = pltpu.make_async_remote_copy(
        src_ref=go_ref.at[1 - side],
        dst_ref=go_ref.at[1 - side],
        send_sem=send_x,
        recv_sem=recv_x,
        device_id=(mate, col),
        device_id_type=MESH,
    )
    each(1, chips, lambda k: to_far(k).start())

    e_ref[...] = jnp.zeros_like(e_ref)
    copies = []
    for k in range(rounds):
        d = 1 << k
        src = s_ref if k == 0 else parts.at[k - 1]
        copy = pltpu.make_async_remote_copy(
            src_ref=src,
            dst_ref=recv.at[k],
            send_sem=send_sem.at[k],
            recv_sem=recv_sem.at[k],
            device_id=(me + d, col),
            device_id_type=MESH,
        )
        copies.append(copy)

        @pl.when(me + d < n)
        def _():
            copy.start()

        @pl.when(me >= d)
        def _():
            copy.wait_recv()
            got = recv[k].astype(jnp.float32)
            if k < rounds - 1:
                parts[k] = (src[...].astype(jnp.float32) + m_ref[2 * k] * got).astype(parts.dtype)
            e_ref[...] += m_ref[2 * k + 1] * got

        if k < rounds - 1:

            @pl.when(me < d)
            def _():
                parts[k] = src[...]

    each(1, chips, lambda k: from_far(k).wait_recv())
    mine.wait()
    swap_out.start()
    swap_in.wait_recv()
    each(1, chips, lambda k: to_far(k).wait_send())
    swap_out.wait_send()

    for k in range(rounds):
        d = 1 << k

        @pl.when(me + d < n)
        def _():
            copies[k].wait_send()


def carried_scan(summary, masks, piece, n, rounds):
    shape = summary.shape
    flat = summary.reshape(-1, shape[-1]).astype(jnp.bfloat16)
    size = flat.shape[0] * flat.shape[1]
    out, gathered = pl.pallas_call(
        functools.partial(scan_kernel, n, rounds),
        out_shape=(
            jax.ShapeDtypeStruct(flat.shape, jnp.float32),
            jax.ShapeDtypeStruct((2, n // 2) + piece.shape, piece.dtype),
        ),
        in_specs=[
            pl.BlockSpec(memory_space=pltpu.VMEM),
            pl.BlockSpec(memory_space=pltpu.SMEM),
            pl.BlockSpec(memory_space=pltpu.VMEM),
        ],
        out_specs=(pl.BlockSpec(memory_space=pltpu.VMEM), pl.BlockSpec(memory_space=pltpu.VMEM)),
        scratch_shapes=[
            pltpu.VMEM((max(rounds - 1, 1),) + flat.shape, jnp.bfloat16),
            pltpu.VMEM((rounds,) + flat.shape, jnp.bfloat16),
            pltpu.SemaphoreType.DMA((rounds,)),
            pltpu.SemaphoreType.DMA((rounds,)),
            pltpu.SemaphoreType.DMA((n // 2,)),
            pltpu.SemaphoreType.DMA((n // 2,)),
            pltpu.SemaphoreType.DMA(()),
            pltpu.SemaphoreType.DMA(()),
            pltpu.SemaphoreType.DMA(()),
        ],
        compiler_params=pltpu.CompilerParams(collective_id=0, has_side_effects=True),
        cost_estimate=pl.CostEstimate(
            flops=3 * rounds * size,
            bytes_accessed=6 * rounds * size + 2 * n * piece.size,
            transcendentals=0,
        ),
    )(flat, masks, piece)
    gathered = jnp.transpose(gathered, (1, 0, 2, 3)).reshape(n * piece.shape[0], piece.shape[1])
    return out.reshape(shape), gathered


def gather_kernel(n, m, xd_ref, xm_ref, early_ref, gd_ref, gm_ref, send_d, recv_d, send_x, recv_x, send_m, recv_m, own):
    me = lax.axis_index("dp")
    col = lax.axis_index("mp")
    chips = n // 2
    side = me % 2
    chip = me // 2
    mate = me + 1 - 2 * side
    barrier = pltpu.get_barrier_semaphore()

    def each(lo, hi, body):
        def step(k, carry):
            body(k)
            return carry

        lax.fori_loop(lo, hi, step, 0)

    each(1, chips, lambda k: pl.semaphore_signal(
        barrier, 1, device_id=((me + 2 * k) % n, col), device_id_type=MESH))
    pl.semaphore_signal(barrier, 1, device_id=(mate, col), device_id_type=MESH)
    each(1, m, lambda k: pl.semaphore_signal(
        barrier, 1, device_id=(me, (col + k) % m), device_id_type=MESH))
    pl.semaphore_wait(barrier, chips + m - 1)

    mine = pltpu.make_async_copy(xd_ref, gd_ref.at[side, chip], own)
    mine.start()

    def to_far(k):
        return pltpu.make_async_remote_copy(
            src_ref=xd_ref,
            dst_ref=gd_ref.at[side, chip],
            send_sem=send_d.at[k],
            recv_sem=recv_d.at[chip],
            device_id=((me + 2 * k) % n, col),
            device_id_type=MESH,
        )

    def from_far(k):
        other = (chip + chips - k) % chips
        return pltpu.make_async_remote_copy(
            src_ref=xd_ref,
            dst_ref=gd_ref.at[side, other],
            send_sem=send_d.at[k],
            recv_sem=recv_d.at[other],
            device_id=(2 * other + side, col),
            device_id_type=MESH,
        )

    swap_out = pltpu.make_async_remote_copy(
        src_ref=gd_ref.at[side],
        dst_ref=gd_ref.at[side],
        send_sem=send_x,
        recv_sem=recv_x,
        device_id=(mate, col),
        device_id_type=MESH,
    )
    swap_in = pltpu.make_async_remote_copy(
        src_ref=gd_ref.at[1 - side],
        dst_ref=gd_ref.at[1 - side],
        send_sem=send_x,
        recv_sem=recv_x,
        device_id=(mate, col),
        device_id_type=MESH,
    )

    def to_mp(k):
        return pltpu.make_async_remote_copy(
            src_ref=xm_ref,
            dst_ref=gm_ref.at[col],
            send_sem=send_m.at[k],
            recv_sem=recv_m.at[col],
            device_id=(me, (col + k) % m),
            device_id_type=MESH,
        )

    def from_mp(k):
        other = (col + m - k) % m
        return pltpu.make_async_remote_copy(
            src_ref=xm_ref,
            dst_ref=gm_ref.at[other],
            send_sem=send_m.at[k],
            recv_sem=recv_m.at[other],
            device_id=(me, other),
            device_id_type=MESH,
        )

    each(1, chips, lambda k: to_far(k).start())
    each(1, m, lambda k: to_mp(k).start())
    gm_ref[col] = xm_ref[...]
    each(1, chips, lambda k: from_far(k).wait_recv())
    mine.wait()
    swap_out.start()
    each(1, m, lambda k: from_mp(k).wait_recv())
    swap_in.wait_recv()
    each(1, chips, lambda k: to_far(k).wait_send())
    swap_out.wait_send()
    each(1, m, lambda k: to_mp(k).wait_send())


def direct_gather(xd, xm, early, n, m):
    moved = n * xd.size * 2 + m * xm.size * 2
    gd, gm = pl.pallas_call(
        functools.partial(gather_kernel, n, m),
        out_shape=(
            jax.ShapeDtypeStruct((2, n // 2) + xd.shape, xd.dtype),
            jax.ShapeDtypeStruct((m,) + xm.shape, xm.dtype),
        ),
        in_specs=[pl.BlockSpec(memory_space=pltpu.VMEM)] * 2 + [pl.BlockSpec(memory_space=pltpu.SMEM)],
        out_specs=(pl.BlockSpec(memory_space=pltpu.VMEM), pl.BlockSpec(memory_space=pltpu.VMEM)),
        scratch_shapes=[
            pltpu.SemaphoreType.DMA((n // 2,)),
            pltpu.SemaphoreType.DMA((n // 2,)),
            pltpu.SemaphoreType.DMA(()),
            pltpu.SemaphoreType.DMA(()),
            pltpu.SemaphoreType.DMA((m,)),
            pltpu.SemaphoreType.DMA((m,)),
            pltpu.SemaphoreType.DMA(()),
        ],
        compiler_params=pltpu.CompilerParams(collective_id=1, has_side_effects=True),
        cost_estimate=pl.CostEstimate(flops=0, bytes_accessed=moved, transcendentals=0),
    )(xd, xm, early)
    return jnp.transpose(gd, (1, 0, 2, 3)), gm


def ring_kernel(m, n_ref, w_ref, o_ref, acc_a, acc_b, got_a, got_b, send_a, recv_a, send_b, recv_b):
    me = lax.axis_index("dp")
    col = lax.axis_index("mp")
    right = (col + 1) % m
    left = (col + m - 1) % m
    half = o_ref.shape[2]
    width = 2 * half
    barrier = pltpu.get_barrier_semaphore()
    pl.semaphore_signal(barrier, 1, device_id=(me, right), device_id_type=MESH)
    pl.semaphore_signal(barrier, 1, device_id=(me, left), device_id_type=MESH)
    pl.semaphore_wait(barrier, 2)

    def own(t, side):
        rows = w_ref[pl.ds(pl.multiple_of(t * width + side * half, half), half), :]
        return lax.dot_general(
            n_ref[...], rows, (((1,), (1,)), ((), ())), preferred_element_type=jnp.float32
        )

    copies = []
    for s in range(m - 1):
        ta = (col + 2 * m - 1 - s) % m
        tb = (col + 1 + s) % m
        part_a = own(ta, 0)
        part_b = own(tb, 1)
        if s > 0:
            copies[-1][0].wait_recv()
            part_a = part_a + got_a[s - 1].astype(jnp.float32)
        acc_a[s] = part_a.astype(acc_a.dtype)
        ca = pltpu.make_async_remote_copy(
            src_ref=acc_a.at[s],
            dst_ref=got_a.at[s],
            send_sem=send_a.at[s],
            recv_sem=recv_a.at[s],
            device_id=(me, right),
            device_id_type=MESH,
        )
        ca.start()
        if s > 0:
            copies[-1][1].wait_recv()
            part_b = part_b + got_b[s - 1].astype(jnp.float32)
        acc_b[s] = part_b.astype(acc_b.dtype)
        cb = pltpu.make_async_remote_copy(
            src_ref=acc_b.at[s],
            dst_ref=got_b.at[s],
            send_sem=send_b.at[s],
            recv_sem=recv_b.at[s],
            device_id=(me, left),
            device_id_type=MESH,
        )
        cb.start()
        copies.append((ca, cb))
    copies[-1][0].wait_recv()
    copies[-1][1].wait_recv()
    o_ref[0] = got_a[m - 2]
    o_ref[1] = got_b[m - 2]
    for ca, cb in copies:
        ca.wait_send()
        cb.wait_send()


def ring_scatter(normed, out_t, m):
    rows = normed.shape[0]
    total = out_t.shape[0]
    width = total // m
    half = width // 2
    slot = (m - 1, rows, half)
    got = pl.pallas_call(
        functools.partial(ring_kernel, m),
        out_shape=jax.ShapeDtypeStruct((2, rows, half), jnp.bfloat16),
        in_specs=[pl.BlockSpec(memory_space=pltpu.VMEM)] * 2,
        out_specs=pl.BlockSpec(memory_space=pltpu.VMEM),
        scratch_shapes=[
            pltpu.VMEM(slot, jnp.bfloat16),
            pltpu.VMEM(slot, jnp.bfloat16),
            pltpu.VMEM(slot, jnp.bfloat16),
            pltpu.VMEM(slot, jnp.bfloat16),
            pltpu.SemaphoreType.DMA((m - 1,)),
            pltpu.SemaphoreType.DMA((m - 1,)),
            pltpu.SemaphoreType.DMA((m - 1,)),
            pltpu.SemaphoreType.DMA((m - 1,)),
        ],
        compiler_params=pltpu.CompilerParams(collective_id=2, has_side_effects=True),
        cost_estimate=pl.CostEstimate(
            flops=2 * rows * normed.shape[1] * total,
            bytes_accessed=2 * (normed.size + out_t.size) + 4 * rows * total,
            transcendentals=0,
        ),
    )(normed, out_t)
    col = lax.axis_index("mp")
    mine = lax.dynamic_slice_in_dim(out_t, col * width, width, axis=0)
    own = lax.dot_general(normed, mine, (((1,), (1,)), ((), ())), preferred_element_type=jnp.float32)
    got = jnp.concatenate([got[0], got[1]], axis=1).astype(jnp.float32)
    return (got + own).astype(jnp.bfloat16)


def per_device(
    tokens,
    q_weight,
    k_weight,
    v_weight,
    adapter_down,
    adapter_up,
    lengths,
    adapter_ids,
    head_gain,
    out_weight,
):
    row_count = tokens.shape[0]
    qf = q_weight.shape[1]
    heads_here = qf // F
    vw = v_weight.shape[1]
    value_width = vw // heads_here
    blocks = lax.axis_size("dp")
    place = lax.axis_index("dp")
    positions = place * row_count + jnp.arange(row_count, dtype=jnp.int32)
    request, starts, adapter = token_tables(lengths, adapter_ids, positions)

    local = jnp.concatenate([q_weight, k_weight, v_weight], axis=1)
    part_low = jnp.dot(tokens, adapter_down, preferred_element_type=jnp.float32)
    owners = lax.axis_index("mp") * (adapter_down.shape[1] // R) + (
        jnp.arange(adapter_down.shape[1], dtype=jnp.int32) // R
    )
    part_low = jnp.where(adapter[:, None] == owners[None, :], part_low, 0.0).astype(jnp.bfloat16)
    cols = lax.axis_size("mp")
    rounds = max(1, (blocks - 1).bit_length())
    masks = scan_masks(lengths, row_count, place, blocks, rounds)
    gathered, low_parts = direct_gather(local, part_low, masks, blocks, cols)
    gathered = gathered.reshape(blocks * local.shape[0], local.shape[1])
    q_full = gathered[:, :qf]
    k_full = gathered[:, qf : 2 * qf]
    v_full = gathered[:, 2 * qf :]
    low_rank = jnp.transpose(low_parts, (1, 0, 2)).reshape(row_count, cols * part_low.shape[1])

    query_sum = jnp.dot(tokens, q_full, preferred_element_type=jnp.float32)
    key_sum = jnp.dot(tokens, k_full, preferred_element_type=jnp.float32)
    value_sum = jnp.dot(tokens, v_full, preferred_element_type=jnp.float32)
    query = query_sum.astype(jnp.bfloat16).reshape(row_count, heads_here, F)
    key_rows = key_sum.astype(jnp.bfloat16).reshape(row_count, heads_here, F)
    values = value_sum + jnp.dot(low_rank, adapter_up, preferred_element_type=jnp.float32)
    values = values.astype(jnp.bfloat16).reshape(row_count, heads_here, value_width)
    within, query_map, summary = block_local(query, key_rows, values, request, starts)

    carried, out_t = carried_scan(summary, masks, out_weight.T, blocks, rounds)

    gains = head_gain.reshape(heads_here, value_width)
    normed = finish(within, query_map, carried, request, starts, gains).reshape(
        row_count, heads_here * value_width
    )
    return ring_scatter(normed, out_t, cols)


def solution(mesh):
    placed = (
        P("dp", None),
        P("dp", "mp"),
        P("dp", "mp"),
        P("dp", "mp"),
        P(None, "mp"),
        P(None, "mp"),
        P(),
        P(),
        P("mp"),
        P("mp", "dp"),
    )
    return jax.shard_map(
        per_device, mesh=mesh, in_specs=placed, out_specs=P("dp", "mp"), check_vma=False
    )
```

```python
import math

import functools

import jax
import jax.numpy as jnp
import numpy as np
from jax import lax
from jax.experimental import pallas as pl
from jax.experimental.pallas import tpu as pltpu
from jax.sharding import PartitionSpec as P

MESH = pl.DeviceIdType.MESH

F = 16
R = 16


EPSILON = 1e-05


def taylor(inputs):
    squares = (inputs[..., :, None] * inputs[..., None, :]).reshape(
        inputs.shape[:-1] + (inputs.shape[-1] * inputs.shape[-1],)
    )
    constant = jnp.ones(inputs.shape[:-1] + (1,), jnp.float32)
    return jnp.concatenate([constant, 0.5 * inputs, squares * (0.25 / math.sqrt(2.0))], axis=-1)


def packed_taylor(inputs):
    width = inputs.shape[-1]
    squares = [inputs[..., a : a + 1] * inputs[..., a:] for a in range(width)]
    constant = jnp.ones(inputs.shape[:-1] + (1,), jnp.float32)
    return jnp.concatenate(
        [constant, 0.5 * inputs] + [s * (0.25 / math.sqrt(2.0)) for s in squares], axis=-1
    )


def packed_features(width):
    index, weight = list(range(1 + width)), [1.0] * (1 + width)
    for a in range(width):
        for b in range(a, width):
            index.append(1 + width + a * width + b)
            weight.append(1.0 if a == b else 2.0)
    return np.asarray(index, np.int32), np.asarray(weight, np.float32)


def request_of(bounds, positions):
    return jnp.sum((positions[:, None] >= bounds[None, :]).astype(jnp.int32), axis=1)


def token_tables(lengths, adapter_ids, positions):
    bounds = jnp.cumsum(lengths)
    request = request_of(bounds, positions)
    openings = bounds - lengths
    starts = jnp.any(positions[:, None] == openings[None, :], axis=1)
    picked = request[:, None] == jnp.arange(lengths.shape[0], dtype=jnp.int32)[None, :]
    adapter = jnp.sum(jnp.where(picked, adapter_ids[None, :], 0), axis=1)
    return (request, starts, adapter)


def block_local(query, key_rows, values, request, starts):
    scores = jnp.einsum("ihd,jhd->hij", query, key_rows, preferred_element_type=jnp.float32) * 0.25
    weights = 1.0 + scores + 0.5 * scores * scores
    indexes = jnp.arange(request.shape[0], dtype=jnp.int32)
    allowed = (indexes[None, :] <= indexes[:, None]) & (request[None, :] == request[:, None])
    weights = jnp.where(allowed[None], weights, 0.0).astype(jnp.bfloat16)
    within = jnp.einsum("hij,jhe->ihe", weights, values, preferred_element_type=jnp.float32)
    index, weight = packed_features(query.shape[-1])
    query_map = taylor(query.astype(jnp.float32)).astype(jnp.bfloat16)
    query_map = query_map[..., index] * jnp.asarray(weight, jnp.bfloat16)
    key_map = packed_taylor(key_rows.astype(jnp.float32)).astype(jnp.bfloat16)
    tail_mask = (request == request[-1]).astype(jnp.bfloat16)
    masked_keys = key_map * tail_mask[:, None, None]
    summary = jnp.einsum("ihf,ihe->hfe", masked_keys, values, preferred_element_type=jnp.float32)
    return (within, query_map, summary)


def finish(within, query_map, carried, request, starts, gains):
    follows = ((request == request[0]) & jnp.logical_not(starts[0])).astype(jnp.float32)
    cross = jnp.einsum(
        "ihf,hfe->ihe", query_map, carried.astype(jnp.bfloat16), preferred_element_type=jnp.float32
    )
    combined = within + follows[:, None, None] * cross
    factor = lax.rsqrt(jnp.mean(combined * combined, axis=-1, keepdims=True) + EPSILON)
    return (combined * factor * gains[None]).astype(jnp.bfloat16)


def scan_masks(lengths, row_count, place, blocks, rounds):
    openings = jnp.cumsum(lengths) - lengths
    ids = jnp.arange(blocks, dtype=jnp.int32)
    firsts = ids * row_count
    inside = (openings[None, :] >= firsts[:, None]) & (openings[None, :] < firsts[:, None] + row_count)
    flags = jnp.any(inside, axis=1).astype(jnp.int32)
    spans = jnp.asarray([1 << (k // 2) for k in range(2 * rounds)], jnp.int32)
    tops = place - jnp.asarray([k % 2 for k in range(2 * rounds)], jnp.int32)
    lows = place - spans + 1
    covered = (ids[None, :] >= lows[:, None]) & (ids[None, :] <= tops[:, None])
    hits = jnp.sum(jnp.where(covered, flags[None, :], 0), axis=1)
    return (hits == 0).astype(jnp.float32)


def scan_kernel(n, rounds, s_ref, m_ref, xo_ref, e_ref, go_ref, parts, recv, send_sem, recv_sem,
                send_o, recv_o, send_x, recv_x, own):
    me = lax.axis_index("dp")
    col = lax.axis_index("mp")
    chips = n // 2
    side = me % 2
    chip = me // 2
    mate = me + 1 - 2 * side
    barrier = pltpu.get_barrier_semaphore()

    def each(lo, hi, body):
        def step(k, carry):
            body(k)
            return carry

        lax.fori_loop(lo, hi, step, 0)

    each(1, chips, lambda k: pl.semaphore_signal(
        barrier, 1, device_id=((me + 2 * k) % n, col), device_id_type=MESH))
    pl.semaphore_signal(barrier, 1, device_id=(mate, col), device_id_type=MESH)
    for k in range(rounds):
        d = 1 << k

        @pl.when(me + d < n)
        def _():
            pl.semaphore_signal(barrier, 1, device_id=(me + d, col), device_id_type=MESH)

        @pl.when(me >= d)
        def _():
            pl.semaphore_signal(barrier, 1, device_id=(me - d, col), device_id_type=MESH)

    peers = 0
    for k in range(rounds):
        d = 1 << k
        peers = peers + (me // d + n - 1) // n + ((n - 1 - me) // d + n - 1) // n
    pl.semaphore_wait(barrier, peers + chips)

    mine = pltpu.make_async_copy(xo_ref, go_ref.at[side, chip], own)
    mine.start()

    def to_far(k):
        return pltpu.make_async_remote_copy(
            src_ref=xo_ref,
            dst_ref=go_ref.at[side, chip],
            send_sem=send_o.at[k],
            recv_sem=recv_o.at[chip],
            device_id=((me + 2 * k) % n, col),
            device_id_type=MESH,
        )

    def from_far(k):
        other = (chip + chips - k) % chips
        return pltpu.make_async_remote_copy(
            src_ref=xo_ref,
            dst_ref=go_ref.at[side, other],
            send_sem=send_o.at[k],
            recv_sem=recv_o.at[other],
            device_id=(2 * other + side, col),
            device_id_type=MESH,
        )

    swap_out = pltpu.make_async_remote_copy(
        src_ref=go_ref.at[side],
        dst_ref=go_ref.at[side],
        send_sem=send_x,
        recv_sem=recv_x,
        device_id=(mate, col),
        device_id_type=MESH,
    )
    swap_in = pltpu.make_async_remote_copy(
        src_ref=go_ref.at[1 - side],
        dst_ref=go_ref.at[1 - side],
        send_sem=send_x,
        recv_sem=recv_x,
        device_id=(mate, col),
        device_id_type=MESH,
    )
    each(1, chips, lambda k: to_far(k).start())

    e_ref[...] = jnp.zeros_like(e_ref)
    copies = []
    for k in range(rounds):
        d = 1 << k
        src = s_ref if k == 0 else parts.at[k - 1]
        copy = pltpu.make_async_remote_copy(
            src_ref=src,
            dst_ref=recv.at[k],
            send_sem=send_sem.at[k],
            recv_sem=recv_sem.at[k],
            device_id=(me + d, col),
            device_id_type=MESH,
        )
        copies.append(copy)

        @pl.when(me + d < n)
        def _():
            copy.start()

        @pl.when(me >= d)
        def _():
            copy.wait_recv()
            got = recv[k].astype(jnp.float32)
            if k < rounds - 1:
                parts[k] = (src[...].astype(jnp.float32) + m_ref[2 * k] * got).astype(parts.dtype)
            e_ref[...] += m_ref[2 * k + 1] * got

        if k < rounds - 1:

            @pl.when(me < d)
            def _():
                parts[k] = src[...]

    each(1, chips, lambda k: from_far(k).wait_recv())
    mine.wait()
    swap_out.start()
    swap_in.wait_recv()
    each(1, chips, lambda k: to_far(k).wait_send())
    swap_out.wait_send()

    for k in range(rounds):
        d = 1 << k

        @pl.when(me + d < n)
        def _():
            copies[k].wait_send()


def carried_scan(summary, masks, piece, n, rounds):
    shape = summary.shape
    flat = summary.reshape(-1, shape[-1]).astype(jnp.bfloat16)
    size = flat.shape[0] * flat.shape[1]
    out, gathered = pl.pallas_call(
        functools.partial(scan_kernel, n, rounds),
        out_shape=(
            jax.ShapeDtypeStruct(flat.shape, jnp.float32),
            jax.ShapeDtypeStruct((2, n // 2) + piece.shape, piece.dtype),
        ),
        in_specs=[
            pl.BlockSpec(memory_space=pltpu.VMEM),
            pl.BlockSpec(memory_space=pltpu.SMEM),
            pl.BlockSpec(memory_space=pltpu.VMEM),
        ],
        out_specs=(pl.BlockSpec(memory_space=pltpu.VMEM), pl.BlockSpec(memory_space=pltpu.VMEM)),
        scratch_shapes=[
            pltpu.VMEM((max(rounds - 1, 1),) + flat.shape, jnp.bfloat16),
            pltpu.VMEM((rounds,) + flat.shape, jnp.bfloat16),
            pltpu.SemaphoreType.DMA((rounds,)),
            pltpu.SemaphoreType.DMA((rounds,)),
            pltpu.SemaphoreType.DMA((n // 2,)),
            pltpu.SemaphoreType.DMA((n // 2,)),
            pltpu.SemaphoreType.DMA(()),
            pltpu.SemaphoreType.DMA(()),
            pltpu.SemaphoreType.DMA(()),
        ],
        compiler_params=pltpu.CompilerParams(collective_id=0, has_side_effects=True),
        cost_estimate=pl.CostEstimate(
            flops=3 * rounds * size,
            bytes_accessed=6 * rounds * size + 2 * n * piece.size,
            transcendentals=0,
        ),
    )(flat, masks, piece)
    gathered = jnp.transpose(gathered, (1, 0, 2, 3)).reshape(n * piece.shape[0], piece.shape[1])
    return out.reshape(shape), gathered


def gather_kernel(n, m, xd_ref, xm_ref, early_ref, gd_ref, gm_ref, send_d, recv_d, send_x, recv_x, send_m, recv_m, own):
    me = lax.axis_index("dp")
    col = lax.axis_index("mp")
    chips = n // 2
    side = me % 2
    chip = me // 2
    mate = me + 1 - 2 * side
    barrier = pltpu.get_barrier_semaphore()

    def each(lo, hi, body):
        def step(k, carry):
            body(k)
            return carry

        lax.fori_loop(lo, hi, step, 0)

    each(1, chips, lambda k: pl.semaphore_signal(
        barrier, 1, device_id=((me + 2 * k) % n, col), device_id_type=MESH))
    pl.semaphore_signal(barrier, 1, device_id=(mate, col), device_id_type=MESH)
    each(1, m, lambda k: pl.semaphore_signal(
        barrier, 1, device_id=(me, (col + k) % m), device_id_type=MESH))
    pl.semaphore_wait(barrier, chips + m - 1)

    mine = pltpu.make_async_copy(xd_ref, gd_ref.at[side, chip], own)
    mine.start()

    def to_far(k):
        return pltpu.make_async_remote_copy(
            src_ref=xd_ref,
            dst_ref=gd_ref.at[side, chip],
            send_sem=send_d.at[k],
            recv_sem=recv_d.at[chip],
            device_id=((me + 2 * k) % n, col),
            device_id_type=MESH,
        )

    def from_far(k):
        other = (chip + chips - k) % chips
        return pltpu.make_async_remote_copy(
            src_ref=xd_ref,
            dst_ref=gd_ref.at[side, other],
            send_sem=send_d.at[k],
            recv_sem=recv_d.at[other],
            device_id=(2 * other + side, col),
            device_id_type=MESH,
        )

    swap_out = pltpu.make_async_remote_copy(
        src_ref=gd_ref.at[side],
        dst_ref=gd_ref.at[side],
        send_sem=send_x,
        recv_sem=recv_x,
        device_id=(mate, col),
        device_id_type=MESH,
    )
    swap_in = pltpu.make_async_remote_copy(
        src_ref=gd_ref.at[1 - side],
        dst_ref=gd_ref.at[1 - side],
        send_sem=send_x,
        recv_sem=recv_x,
        device_id=(mate, col),
        device_id_type=MESH,
    )

    def to_mp(k):
        return pltpu.make_async_remote_copy(
            src_ref=xm_ref,
            dst_ref=gm_ref.at[col],
            send_sem=send_m.at[k],
            recv_sem=recv_m.at[col],
            device_id=(me, (col + k) % m),
            device_id_type=MESH,
        )

    def from_mp(k):
        other = (col + m - k) % m
        return pltpu.make_async_remote_copy(
            src_ref=xm_ref,
            dst_ref=gm_ref.at[other],
            send_sem=send_m.at[k],
            recv_sem=recv_m.at[other],
            device_id=(me, other),
            device_id_type=MESH,
        )

    each(1, chips, lambda k: to_far(k).start())
    each(1, m, lambda k: to_mp(k).start())
    gm_ref[col] = xm_ref[...]
    each(1, chips, lambda k: from_far(k).wait_recv())
    mine.wait()
    swap_out.start()
    each(1, m, lambda k: from_mp(k).wait_recv())
    swap_in.wait_recv()
    each(1, chips, lambda k: to_far(k).wait_send())
    swap_out.wait_send()
    each(1, m, lambda k: to_mp(k).wait_send())


def direct_gather(xd, xm, early, n, m):
    moved = n * xd.size * 2 + m * xm.size * 2
    gd, gm = pl.pallas_call(
        functools.partial(gather_kernel, n, m),
        out_shape=(
            jax.ShapeDtypeStruct((2, n // 2) + xd.shape, xd.dtype),
            jax.ShapeDtypeStruct((m,) + xm.shape, xm.dtype),
        ),
        in_specs=[pl.BlockSpec(memory_space=pltpu.VMEM)] * 2 + [pl.BlockSpec(memory_space=pltpu.SMEM)],
        out_specs=(pl.BlockSpec(memory_space=pltpu.VMEM), pl.BlockSpec(memory_space=pltpu.VMEM)),
        scratch_shapes=[
            pltpu.SemaphoreType.DMA((n // 2,)),
            pltpu.SemaphoreType.DMA((n // 2,)),
            pltpu.SemaphoreType.DMA(()),
            pltpu.SemaphoreType.DMA(()),
            pltpu.SemaphoreType.DMA((m,)),
            pltpu.SemaphoreType.DMA((m,)),
            pltpu.SemaphoreType.DMA(()),
        ],
        compiler_params=pltpu.CompilerParams(collective_id=1, has_side_effects=True),
        cost_estimate=pl.CostEstimate(flops=0, bytes_accessed=moved, transcendentals=0),
    )(xd, xm, early)
    return jnp.transpose(gd, (1, 0, 2, 3)), gm


def ring_kernel(m, n_ref, w_ref, o_ref, acc_a, acc_b, got_a, got_b, send_a, recv_a, send_b, recv_b):
    me = lax.axis_index("dp")
    col = lax.axis_index("mp")
    right = (col + 1) % m
    left = (col + m - 1) % m
    half = o_ref.shape[2]
    width = 2 * half
    barrier = pltpu.get_barrier_semaphore()
    pl.semaphore_signal(barrier, 1, device_id=(me, right), device_id_type=MESH)
    pl.semaphore_signal(barrier, 1, device_id=(me, left), device_id_type=MESH)
    pl.semaphore_wait(barrier, 2)

    def own(t, side):
        rows = w_ref[pl.ds(pl.multiple_of(t * width + side * half, half), half), :]
        return lax.dot_general(
            n_ref[...], rows, (((1,), (1,)), ((), ())), preferred_element_type=jnp.float32
        )

    copies = []
    for s in range(m - 1):
        ta = (col + 2 * m - 1 - s) % m
        tb = (col + 1 + s) % m
        part_a = own(ta, 0)
        part_b = own(tb, 1)
        if s > 0:
            copies[-1][0].wait_recv()
            part_a = part_a + got_a[s - 1].astype(jnp.float32)
        acc_a[s] = part_a.astype(acc_a.dtype)
        ca = pltpu.make_async_remote_copy(
            src_ref=acc_a.at[s],
            dst_ref=got_a.at[s],
            send_sem=send_a.at[s],
            recv_sem=recv_a.at[s],
            device_id=(me, right),
            device_id_type=MESH,
        )
        ca.start()
        if s > 0:
            copies[-1][1].wait_recv()
            part_b = part_b + got_b[s - 1].astype(jnp.float32)
        acc_b[s] = part_b.astype(acc_b.dtype)
        cb = pltpu.make_async_remote_copy(
            src_ref=acc_b.at[s],
            dst_ref=got_b.at[s],
            send_sem=send_b.at[s],
            recv_sem=recv_b.at[s],
            device_id=(me, left),
            device_id_type=MESH,
        )
        cb.start()
        copies.append((ca, cb))
    copies[-1][0].wait_recv()
    copies[-1][1].wait_recv()
    o_ref[0] = got_a[m - 2]
    o_ref[1] = got_b[m - 2]
    for ca, cb in copies:
        ca.wait_send()
        cb.wait_send()


def ring_scatter(normed, out_t, m):
    rows = normed.shape[0]
    total = out_t.shape[0]
    width = total // m
    half = width // 2
    slot = (m - 1, rows, half)
    got = pl.pallas_call(
        functools.partial(ring_kernel, m),
        out_shape=jax.ShapeDtypeStruct((2, rows, half), jnp.bfloat16),
        in_specs=[pl.BlockSpec(memory_space=pltpu.VMEM)] * 2,
        out_specs=pl.BlockSpec(memory_space=pltpu.VMEM),
        scratch_shapes=[
            pltpu.VMEM(slot, jnp.bfloat16),
            pltpu.VMEM(slot, jnp.bfloat16),
            pltpu.VMEM(slot, jnp.bfloat16),
            pltpu.VMEM(slot, jnp.bfloat16),
            pltpu.SemaphoreType.DMA((m - 1,)),
            pltpu.SemaphoreType.DMA((m - 1,)),
            pltpu.SemaphoreType.DMA((m - 1,)),
            pltpu.SemaphoreType.DMA((m - 1,)),
        ],
        compiler_params=pltpu.CompilerParams(collective_id=2, has_side_effects=True),
        cost_estimate=pl.CostEstimate(
            flops=2 * rows * normed.shape[1] * total,
            bytes_accessed=2 * (normed.size + out_t.size) + 4 * rows * total,
            transcendentals=0,
        ),
    )(normed, out_t)
    col = lax.axis_index("mp")
    mine = lax.dynamic_slice_in_dim(out_t, col * width, width, axis=0)
    own = lax.dot_general(normed, mine, (((1,), (1,)), ((), ())), preferred_element_type=jnp.float32)
    got = jnp.concatenate([got[0], got[1]], axis=1).astype(jnp.float32)
    return (got + own).astype(jnp.bfloat16)


def per_device(
    tokens,
    q_weight,
    k_weight,
    v_weight,
    adapter_down,
    adapter_up,
    lengths,
    adapter_ids,
    head_gain,
    out_weight,
):
    row_count = tokens.shape[0]
    qf = q_weight.shape[1]
    heads_here = qf // F
    vw = v_weight.shape[1]
    value_width = vw // heads_here
    blocks = lax.axis_size("dp")
    place = lax.axis_index("dp")
    positions = place * row_count + jnp.arange(row_count, dtype=jnp.int32)
    request, starts, adapter = token_tables(lengths, adapter_ids, positions)

    local = jnp.concatenate([q_weight, k_weight, v_weight], axis=1)
    part_low = jnp.dot(tokens, adapter_down, preferred_element_type=jnp.float32)
    owners = lax.axis_index("mp") * (adapter_down.shape[1] // R) + (
        jnp.arange(adapter_down.shape[1], dtype=jnp.int32) // R
    )
    part_low = jnp.where(adapter[:, None] == owners[None, :], part_low, 0.0).astype(jnp.bfloat16)
    cols = lax.axis_size("mp")
    rounds = max(1, (blocks - 1).bit_length())
    masks = scan_masks(lengths, row_count, place, blocks, rounds)
    gathered, low_parts = direct_gather(local, part_low, masks, blocks, cols)
    gathered = gathered.reshape(blocks * local.shape[0], local.shape[1])
    q_full = gathered[:, :qf]
    k_full = gathered[:, qf : 2 * qf]
    v_full = gathered[:, 2 * qf :]

    query_sum = jnp.dot(tokens, q_full, preferred_element_type=jnp.float32)
    key_sum = jnp.dot(tokens, k_full, preferred_element_type=jnp.float32)
    value_sum = jnp.dot(tokens, v_full, preferred_element_type=jnp.float32)
    query = query_sum.astype(jnp.bfloat16).reshape(row_count, heads_here, F)
    key_rows = key_sum.astype(jnp.bfloat16).reshape(row_count, heads_here, F)
    ups = adapter_up.reshape(cols, part_low.shape[1], adapter_up.shape[1])
    values = value_sum + jnp.einsum("mtc,mce->te", low_parts, ups, preferred_element_type=jnp.float32)
    values = values.astype(jnp.bfloat16).reshape(row_count, heads_here, value_width)
    within, query_map, summary = block_local(query, key_rows, values, request, starts)

    carried, out_t = carried_scan(summary, masks, out_weight.T, blocks, rounds)

    gains = head_gain.reshape(heads_here, value_width)
    normed = finish(within, query_map, carried, request, starts, gains).reshape(
        row_count, heads_here * value_width
    )
    return ring_scatter(normed, out_t, cols)


def solution(mesh):
    placed = (
        P("dp", None),
        P("dp", "mp"),
        P("dp", "mp"),
        P("dp", "mp"),
        P(None, "mp"),
        P(None, "mp"),
        P(),
        P(),
        P("mp"),
        P("mp", "dp"),
    )
    return jax.shard_map(
        per_device, mesh=mesh, in_specs=placed, out_specs=P("dp", "mp"), check_vma=False
    )
```

```python
import math

import functools

import jax
import jax.numpy as jnp
import numpy as np
from jax import lax
from jax.experimental import pallas as pl
from jax.experimental.pallas import tpu as pltpu
from jax.sharding import PartitionSpec as P

MESH = pl.DeviceIdType.MESH

F = 16
R = 16


EPSILON = 1e-05


def taylor(inputs):
    squares = (inputs[..., :, None] * inputs[..., None, :]).reshape(
        inputs.shape[:-1] + (inputs.shape[-1] * inputs.shape[-1],)
    )
    constant = jnp.ones(inputs.shape[:-1] + (1,), jnp.float32)
    return jnp.concatenate([constant, 0.5 * inputs, squares * (0.25 / math.sqrt(2.0))], axis=-1)


def packed_taylor(inputs):
    width = inputs.shape[-1]
    squares = [inputs[..., a : a + 1] * inputs[..., a:] for a in range(width)]
    constant = jnp.ones(inputs.shape[:-1] + (1,), jnp.float32)
    return jnp.concatenate(
        [constant, 0.5 * inputs] + [s * (0.25 / math.sqrt(2.0)) for s in squares], axis=-1
    )


def packed_features(width):
    index, weight = list(range(1 + width)), [1.0] * (1 + width)
    for a in range(width):
        for b in range(a, width):
            index.append(1 + width + a * width + b)
            weight.append(1.0 if a == b else 2.0)
    return np.asarray(index, np.int32), np.asarray(weight, np.float32)


def request_of(bounds, positions):
    return jnp.sum((positions[:, None] >= bounds[None, :]).astype(jnp.int32), axis=1)


def token_tables(lengths, adapter_ids, positions):
    bounds = jnp.cumsum(lengths)
    request = request_of(bounds, positions)
    openings = bounds - lengths
    starts = jnp.any(positions[:, None] == openings[None, :], axis=1)
    picked = request[:, None] == jnp.arange(lengths.shape[0], dtype=jnp.int32)[None, :]
    adapter = jnp.sum(jnp.where(picked, adapter_ids[None, :], 0), axis=1)
    return (request, starts, adapter)


def block_local(query, key_rows, values, request, starts):
    scores = jnp.einsum("ihd,jhd->hij", query, key_rows, preferred_element_type=jnp.float32) * 0.25
    weights = 1.0 + scores + 0.5 * scores * scores
    indexes = jnp.arange(request.shape[0], dtype=jnp.int32)
    allowed = (indexes[None, :] <= indexes[:, None]) & (request[None, :] == request[:, None])
    weights = jnp.where(allowed[None], weights, 0.0).astype(jnp.bfloat16)
    within = jnp.einsum("hij,jhe->ihe", weights, values, preferred_element_type=jnp.float32)
    index, weight = packed_features(query.shape[-1])
    query_map = taylor(query.astype(jnp.float32)).astype(jnp.bfloat16)
    query_map = query_map[..., index] * jnp.asarray(weight, jnp.bfloat16)
    key_map = packed_taylor(key_rows.astype(jnp.float32)).astype(jnp.bfloat16)
    tail_mask = (request == request[-1]).astype(jnp.bfloat16)
    masked_keys = key_map * tail_mask[:, None, None]
    summary = jnp.einsum("ihf,ihe->hfe", masked_keys, values, preferred_element_type=jnp.float32)
    return (within, query_map, summary)


def finish(within, query_map, carried, request, starts, gains):
    follows = ((request == request[0]) & jnp.logical_not(starts[0])).astype(jnp.float32)
    cross = jnp.einsum(
        "ihf,hfe->ihe", query_map, carried.astype(jnp.bfloat16), preferred_element_type=jnp.float32
    )
    combined = within + follows[:, None, None] * cross
    factor = lax.rsqrt(jnp.mean(combined * combined, axis=-1, keepdims=True) + EPSILON)
    return (combined * factor * gains[None]).astype(jnp.bfloat16)


def scan_masks(lengths, row_count, place, blocks, rounds):
    openings = jnp.cumsum(lengths) - lengths
    ids = jnp.arange(blocks, dtype=jnp.int32)
    firsts = ids * row_count
    inside = (openings[None, :] >= firsts[:, None]) & (openings[None, :] < firsts[:, None] + row_count)
    flags = jnp.any(inside, axis=1).astype(jnp.int32)
    spans = jnp.asarray([1 << (k // 2) for k in range(2 * rounds)], jnp.int32)
    tops = place - jnp.asarray([k % 2 for k in range(2 * rounds)], jnp.int32)
    lows = place - spans + 1
    covered = (ids[None, :] >= lows[:, None]) & (ids[None, :] <= tops[:, None])
    hits = jnp.sum(jnp.where(covered, flags[None, :], 0), axis=1)
    return (hits == 0).astype(jnp.float32)


def scan_kernel(n, rounds, s_ref, m_ref, xo_ref, e_ref, go_ref, parts, recv, total, send_sem, recv_sem,
                send_o, recv_o, send_x, recv_x, own):
    me = lax.axis_index("dp")
    col = lax.axis_index("mp")
    chips = n // 2
    side = me % 2
    chip = me // 2
    mate = me + 1 - 2 * side
    barrier = pltpu.get_barrier_semaphore()

    def each(lo, hi, body):
        def step(k, carry):
            body(k)
            return carry

        lax.fori_loop(lo, hi, step, 0)

    each(1, chips, lambda k: pl.semaphore_signal(
        barrier, 1, device_id=((me + 2 * k) % n, col), device_id_type=MESH))
    pl.semaphore_signal(barrier, 1, device_id=(mate, col), device_id_type=MESH)
    for k in range(rounds):
        d = 1 << k

        @pl.when(me + d < n)
        def _():
            pl.semaphore_signal(barrier, 1, device_id=(me + d, col), device_id_type=MESH)

        @pl.when(me >= d)
        def _():
            pl.semaphore_signal(barrier, 1, device_id=(me - d, col), device_id_type=MESH)

    peers = 0
    for k in range(rounds):
        d = 1 << k
        peers = peers + (me // d + n - 1) // n + ((n - 1 - me) // d + n - 1) // n
    pl.semaphore_wait(barrier, peers + chips)

    mine = pltpu.make_async_copy(xo_ref, go_ref.at[side, chip], own)
    mine.start()

    def to_far(k):
        return pltpu.make_async_remote_copy(
            src_ref=xo_ref,
            dst_ref=go_ref.at[side, chip],
            send_sem=send_o.at[k],
            recv_sem=recv_o.at[chip],
            device_id=((me + 2 * k) % n, col),
            device_id_type=MESH,
        )

    def from_far(k):
        other = (chip + chips - k) % chips
        return pltpu.make_async_remote_copy(
            src_ref=xo_ref,
            dst_ref=go_ref.at[side, other],
            send_sem=send_o.at[k],
            recv_sem=recv_o.at[other],
            device_id=(2 * other + side, col),
            device_id_type=MESH,
        )

    swap_out = pltpu.make_async_remote_copy(
        src_ref=go_ref.at[side],
        dst_ref=go_ref.at[side],
        send_sem=send_x,
        recv_sem=recv_x,
        device_id=(mate, col),
        device_id_type=MESH,
    )
    swap_in = pltpu.make_async_remote_copy(
        src_ref=go_ref.at[1 - side],
        dst_ref=go_ref.at[1 - side],
        send_sem=send_x,
        recv_sem=recv_x,
        device_id=(mate, col),
        device_id_type=MESH,
    )
    each(1, chips, lambda k: to_far(k).start())

    total[...] = jnp.zeros_like(total)
    copies = []
    for k in range(rounds):
        d = 1 << k
        src = s_ref if k == 0 else parts.at[k - 1]
        copy = pltpu.make_async_remote_copy(
            src_ref=src,
            dst_ref=recv.at[k],
            send_sem=send_sem.at[k],
            recv_sem=recv_sem.at[k],
            device_id=(me + d, col),
            device_id_type=MESH,
        )
        copies.append(copy)

        @pl.when(me + d < n)
        def _():
            copy.start()

        @pl.when(me >= d)
        def _():
            copy.wait_recv()
            got = recv[k].astype(jnp.float32)
            if k < rounds - 1:
                parts[k] = (src[...].astype(jnp.float32) + m_ref[2 * k] * got).astype(parts.dtype)
            total[...] += m_ref[2 * k + 1] * got

        if k < rounds - 1:

            @pl.when(me < d)
            def _():
                parts[k] = src[...]

    e_ref[...] = total[...].astype(e_ref.dtype)
    each(1, chips, lambda k: from_far(k).wait_recv())
    mine.wait()
    swap_out.start()
    swap_in.wait_recv()
    each(1, chips, lambda k: to_far(k).wait_send())
    swap_out.wait_send()

    for k in range(rounds):
        d = 1 << k

        @pl.when(me + d < n)
        def _():
            copies[k].wait_send()


def carried_scan(summary, masks, piece, n, rounds):
    shape = summary.shape
    flat = summary.reshape(-1, shape[-1]).astype(jnp.bfloat16)
    size = flat.shape[0] * flat.shape[1]
    out, gathered = pl.pallas_call(
        functools.partial(scan_kernel, n, rounds),
        out_shape=(
            jax.ShapeDtypeStruct(flat.shape, jnp.bfloat16),
            jax.ShapeDtypeStruct((2, n // 2) + piece.shape, piece.dtype),
        ),
        in_specs=[
            pl.BlockSpec(memory_space=pltpu.VMEM),
            pl.BlockSpec(memory_space=pltpu.SMEM),
            pl.BlockSpec(memory_space=pltpu.VMEM),
        ],
        out_specs=(pl.BlockSpec(memory_space=pltpu.VMEM), pl.BlockSpec(memory_space=pltpu.VMEM)),
        scratch_shapes=[
            pltpu.VMEM((max(rounds - 1, 1),) + flat.shape, jnp.bfloat16),
            pltpu.VMEM((rounds,) + flat.shape, jnp.bfloat16),
            pltpu.VMEM(flat.shape, jnp.float32),
            pltpu.SemaphoreType.DMA((rounds,)),
            pltpu.SemaphoreType.DMA((rounds,)),
            pltpu.SemaphoreType.DMA((n // 2,)),
            pltpu.SemaphoreType.DMA((n // 2,)),
            pltpu.SemaphoreType.DMA(()),
            pltpu.SemaphoreType.DMA(()),
            pltpu.SemaphoreType.DMA(()),
        ],
        compiler_params=pltpu.CompilerParams(collective_id=0, has_side_effects=True),
        cost_estimate=pl.CostEstimate(
            flops=3 * rounds * size,
            bytes_accessed=6 * rounds * size + 2 * n * piece.size,
            transcendentals=0,
        ),
    )(flat, masks, piece)
    gathered = jnp.transpose(gathered, (1, 0, 2, 3)).reshape(n * piece.shape[0], piece.shape[1])
    return out.reshape(shape), gathered


def gather_kernel(n, m, xd_ref, xm_ref, early_ref, gd_ref, gm_ref, send_d, recv_d, send_x, recv_x, send_m, recv_m, own):
    me = lax.axis_index("dp")
    col = lax.axis_index("mp")
    chips = n // 2
    side = me % 2
    chip = me // 2
    mate = me + 1 - 2 * side
    barrier = pltpu.get_barrier_semaphore()

    def each(lo, hi, body):
        def step(k, carry):
            body(k)
            return carry

        lax.fori_loop(lo, hi, step, 0)

    each(1, chips, lambda k: pl.semaphore_signal(
        barrier, 1, device_id=((me + 2 * k) % n, col), device_id_type=MESH))
    pl.semaphore_signal(barrier, 1, device_id=(mate, col), device_id_type=MESH)
    each(1, m, lambda k: pl.semaphore_signal(
        barrier, 1, device_id=(me, (col + k) % m), device_id_type=MESH))
    pl.semaphore_wait(barrier, chips + m - 1)

    mine = pltpu.make_async_copy(xd_ref, gd_ref.at[side, chip], own)
    mine.start()

    def to_far(k):
        return pltpu.make_async_remote_copy(
            src_ref=xd_ref,
            dst_ref=gd_ref.at[side, chip],
            send_sem=send_d.at[k],
            recv_sem=recv_d.at[chip],
            device_id=((me + 2 * k) % n, col),
            device_id_type=MESH,
        )

    def from_far(k):
        other = (chip + chips - k) % chips
        return pltpu.make_async_remote_copy(
            src_ref=xd_ref,
            dst_ref=gd_ref.at[side, other],
            send_sem=send_d.at[k],
            recv_sem=recv_d.at[other],
            device_id=(2 * other + side, col),
            device_id_type=MESH,
        )

    swap_out = pltpu.make_async_remote_copy(
        src_ref=gd_ref.at[side],
        dst_ref=gd_ref.at[side],
        send_sem=send_x,
        recv_sem=recv_x,
        device_id=(mate, col),
        device_id_type=MESH,
    )
    swap_in = pltpu.make_async_remote_copy(
        src_ref=gd_ref.at[1 - side],
        dst_ref=gd_ref.at[1 - side],
        send_sem=send_x,
        recv_sem=recv_x,
        device_id=(mate, col),
        device_id_type=MESH,
    )

    def to_mp(k):
        return pltpu.make_async_remote_copy(
            src_ref=xm_ref,
            dst_ref=gm_ref.at[col],
            send_sem=send_m.at[k],
            recv_sem=recv_m.at[col],
            device_id=(me, (col + k) % m),
            device_id_type=MESH,
        )

    def from_mp(k):
        other = (col + m - k) % m
        return pltpu.make_async_remote_copy(
            src_ref=xm_ref,
            dst_ref=gm_ref.at[other],
            send_sem=send_m.at[k],
            recv_sem=recv_m.at[other],
            device_id=(me, other),
            device_id_type=MESH,
        )

    each(1, chips, lambda k: to_far(k).start())
    each(1, m, lambda k: to_mp(k).start())
    gm_ref[col] = xm_ref[...]
    each(1, chips, lambda k: from_far(k).wait_recv())
    mine.wait()
    swap_out.start()
    each(1, m, lambda k: from_mp(k).wait_recv())
    swap_in.wait_recv()
    each(1, chips, lambda k: to_far(k).wait_send())
    swap_out.wait_send()
    each(1, m, lambda k: to_mp(k).wait_send())


def direct_gather(xd, xm, early, n, m):
    moved = n * xd.size * 2 + m * xm.size * 2
    gd, gm = pl.pallas_call(
        functools.partial(gather_kernel, n, m),
        out_shape=(
            jax.ShapeDtypeStruct((2, n // 2) + xd.shape, xd.dtype),
            jax.ShapeDtypeStruct((m,) + xm.shape, xm.dtype),
        ),
        in_specs=[pl.BlockSpec(memory_space=pltpu.VMEM)] * 2 + [pl.BlockSpec(memory_space=pltpu.SMEM)],
        out_specs=(pl.BlockSpec(memory_space=pltpu.VMEM), pl.BlockSpec(memory_space=pltpu.VMEM)),
        scratch_shapes=[
            pltpu.SemaphoreType.DMA((n // 2,)),
            pltpu.SemaphoreType.DMA((n // 2,)),
            pltpu.SemaphoreType.DMA(()),
            pltpu.SemaphoreType.DMA(()),
            pltpu.SemaphoreType.DMA((m,)),
            pltpu.SemaphoreType.DMA((m,)),
            pltpu.SemaphoreType.DMA(()),
        ],
        compiler_params=pltpu.CompilerParams(collective_id=1, has_side_effects=True),
        cost_estimate=pl.CostEstimate(flops=0, bytes_accessed=moved, transcendentals=0),
    )(xd, xm, early)
    return jnp.transpose(gd, (1, 0, 2, 3)), gm


def ring_kernel(m, n_ref, w_ref, o_ref, acc_a, acc_b, got_a, got_b, send_a, recv_a, send_b, recv_b):
    me = lax.axis_index("dp")
    col = lax.axis_index("mp")
    right = (col + 1) % m
    left = (col + m - 1) % m
    half = o_ref.shape[2]
    width = 2 * half
    barrier = pltpu.get_barrier_semaphore()
    pl.semaphore_signal(barrier, 1, device_id=(me, right), device_id_type=MESH)
    pl.semaphore_signal(barrier, 1, device_id=(me, left), device_id_type=MESH)
    pl.semaphore_wait(barrier, 2)

    def own(t, side):
        rows = w_ref[pl.ds(pl.multiple_of(t * width + side * half, half), half), :]
        return lax.dot_general(
            n_ref[...], rows, (((1,), (1,)), ((), ())), preferred_element_type=jnp.float32
        )

    copies = []
    for s in range(m - 1):
        ta = (col + 2 * m - 1 - s) % m
        tb = (col + 1 + s) % m
        part_a = own(ta, 0)
        part_b = own(tb, 1)
        if s > 0:
            copies[-1][0].wait_recv()
            part_a = part_a + got_a[s - 1].astype(jnp.float32)
        acc_a[s] = part_a.astype(acc_a.dtype)
        ca = pltpu.make_async_remote_copy(
            src_ref=acc_a.at[s],
            dst_ref=got_a.at[s],
            send_sem=send_a.at[s],
            recv_sem=recv_a.at[s],
            device_id=(me, right),
            device_id_type=MESH,
        )
        ca.start()
        if s > 0:
            copies[-1][1].wait_recv()
            part_b = part_b + got_b[s - 1].astype(jnp.float32)
        acc_b[s] = part_b.astype(acc_b.dtype)
        cb = pltpu.make_async_remote_copy(
            src_ref=acc_b.at[s],
            dst_ref=got_b.at[s],
            send_sem=send_b.at[s],
            recv_sem=recv_b.at[s],
            device_id=(me, left),
            device_id_type=MESH,
        )
        cb.start()
        copies.append((ca, cb))
    copies[-1][0].wait_recv()
    copies[-1][1].wait_recv()
    o_ref[0] = got_a[m - 2]
    o_ref[1] = got_b[m - 2]
    for ca, cb in copies:
        ca.wait_send()
        cb.wait_send()


def ring_scatter(normed, out_t, m):
    rows = normed.shape[0]
    total = out_t.shape[0]
    width = total // m
    half = width // 2
    slot = (m - 1, rows, half)
    got = pl.pallas_call(
        functools.partial(ring_kernel, m),
        out_shape=jax.ShapeDtypeStruct((2, rows, half), jnp.bfloat16),
        in_specs=[pl.BlockSpec(memory_space=pltpu.VMEM)] * 2,
        out_specs=pl.BlockSpec(memory_space=pltpu.VMEM),
        scratch_shapes=[
            pltpu.VMEM(slot, jnp.bfloat16),
            pltpu.VMEM(slot, jnp.bfloat16),
            pltpu.VMEM(slot, jnp.bfloat16),
            pltpu.VMEM(slot, jnp.bfloat16),
            pltpu.SemaphoreType.DMA((m - 1,)),
            pltpu.SemaphoreType.DMA((m - 1,)),
            pltpu.SemaphoreType.DMA((m - 1,)),
            pltpu.SemaphoreType.DMA((m - 1,)),
        ],
        compiler_params=pltpu.CompilerParams(collective_id=2, has_side_effects=True),
        cost_estimate=pl.CostEstimate(
            flops=2 * rows * normed.shape[1] * total,
            bytes_accessed=2 * (normed.size + out_t.size) + 4 * rows * total,
            transcendentals=0,
        ),
    )(normed, out_t)
    col = lax.axis_index("mp")
    mine = lax.dynamic_slice_in_dim(out_t, col * width, width, axis=0)
    own = lax.dot_general(normed, mine, (((1,), (1,)), ((), ())), preferred_element_type=jnp.float32)
    got = jnp.concatenate([got[0], got[1]], axis=1).astype(jnp.float32)
    return (got + own).astype(jnp.bfloat16)


def per_device(
    tokens,
    q_weight,
    k_weight,
    v_weight,
    adapter_down,
    adapter_up,
    lengths,
    adapter_ids,
    head_gain,
    out_weight,
):
    row_count = tokens.shape[0]
    qf = q_weight.shape[1]
    heads_here = qf // F
    vw = v_weight.shape[1]
    value_width = vw // heads_here
    blocks = lax.axis_size("dp")
    place = lax.axis_index("dp")
    positions = place * row_count + jnp.arange(row_count, dtype=jnp.int32)
    request, starts, adapter = token_tables(lengths, adapter_ids, positions)

    local = jnp.concatenate([q_weight, k_weight, v_weight], axis=1)
    part_low = jnp.dot(tokens, adapter_down, preferred_element_type=jnp.float32)
    owners = lax.axis_index("mp") * (adapter_down.shape[1] // R) + (
        jnp.arange(adapter_down.shape[1], dtype=jnp.int32) // R
    )
    part_low = jnp.where(adapter[:, None] == owners[None, :], part_low, 0.0).astype(jnp.bfloat16)
    cols = lax.axis_size("mp")
    rounds = max(1, (blocks - 1).bit_length())
    masks = scan_masks(lengths, row_count, place, blocks, rounds)
    gathered, low_parts = direct_gather(local, part_low, masks, blocks, cols)
    gathered = gathered.reshape(blocks * local.shape[0], local.shape[1])
    q_full = gathered[:, :qf]
    k_full = gathered[:, qf : 2 * qf]
    v_full = gathered[:, 2 * qf :]

    query_sum = jnp.dot(tokens, q_full, preferred_element_type=jnp.float32)
    key_sum = jnp.dot(tokens, k_full, preferred_element_type=jnp.float32)
    value_sum = jnp.dot(tokens, v_full, preferred_element_type=jnp.float32)
    query = query_sum.astype(jnp.bfloat16).reshape(row_count, heads_here, F)
    key_rows = key_sum.astype(jnp.bfloat16).reshape(row_count, heads_here, F)
    ups = adapter_up.reshape(cols, part_low.shape[1], adapter_up.shape[1])
    values = value_sum + jnp.einsum("mtc,mce->te", low_parts, ups, preferred_element_type=jnp.float32)
    values = values.astype(jnp.bfloat16).reshape(row_count, heads_here, value_width)
    within, query_map, summary = block_local(query, key_rows, values, request, starts)

    carried, out_t = carried_scan(summary, masks, out_weight.T, blocks, rounds)

    gains = head_gain.reshape(heads_here, value_width)
    normed = finish(within, query_map, carried, request, starts, gains).reshape(
        row_count, heads_here * value_width
    )
    return ring_scatter(normed, out_t, cols)


def solution(mesh):
    placed = (
        P("dp", None),
        P("dp", "mp"),
        P("dp", "mp"),
        P("dp", "mp"),
        P(None, "mp"),
        P(None, "mp"),
        P(),
        P(),
        P("mp"),
        P("mp", "dp"),
    )
    return jax.shard_map(
        per_device, mesh=mesh, in_specs=placed, out_specs=P("dp", "mp"), check_vma=False
    )
```
